32 devices in a mesh: dp: 8 (over y, x, core), mp: 4 (over z).
Axes of the slice: x: 2, y: 2, z: 4, core: 2. Of those that a mesh axis runs over, the one named last changes fastest.
Arguments:
- tokens: bfloat16 [2, 8704, 1024], P(None, ('dp', 'mp')), may hold values from -6 to 6
- seg_ids: int32 [2, 8704], P(None, 'dp'), may hold values from 0 to 1, as said below
- qkv_weight: bfloat16 [3, 1024, 1024], P(None, 'dp', 'mp'), may hold values from -0.25 to 0.25
- qv_bias: bfloat16 [2, 1024], P(None, ('mp', 'dp')), may hold values from -2 to 2
- out_weight: bfloat16 [1024, 1024], P(('mp', 'dp')), may hold values from -0.1875 to 0.1875
- up_weight: bfloat16 [1024, 4096], P('dp', 'mp'), may hold values from -0.1875 to 0.1875
- up_bias: bfloat16 [4096], P(('mp', 'dp')), may hold values from -3 to 3
- down_weight: bfloat16 [4096, 1024], P(('mp', 'dp')), may hold values from -0.09375 to 0.09375
- norm_gain: bfloat16 [4, 1024], P(None, 'dp'), may hold values from 0.099609375 to 1.8984375
- norm_bias: bfloat16 [4, 1024], P(None, 'dp'), may hold values from -2 to 2
- branch_bias: bfloat16 [2, 1024], P(None, 'dp'), may hold values from -3 to 3
- out_grad: bfloat16 [2, 8704, 1024], P(None, ('dp', 'mp')), may hold values from -6 to 6
Outputs:
- layer_out: bfloat16 [2, 8704, 1024], P(None, ('dp', 'mp'))
- input_grad: float32 [2, 8704, 1024], P(None, ('dp', 'mp'))
- qkv_grad: float32 [3, 1024, 1024], P(None, 'dp', 'mp')
- qv_bias_grad: float32 [2, 1024], P(None, ('mp', 'dp'))
- out_weight_grad: float32 [1024, 1024], P(('mp', 'dp'))
- up_weight_grad: float32 [1024, 4096], P('dp', 'mp')
- up_bias_grad: float32 [4096], P(('mp', 'dp'))
- down_weight_grad: float32 [4096, 1024], P(('mp', 'dp'))
- norm_gain_grad: float32 [4, 1024], P(None, 'dp')
- norm_bias_grad: float32 [4, 1024], P(None, 'dp')
- branch_bias_grad: float32 [2, 1024], P(None, 'dp')
The draws below stay inside these ranges and needn't reach their ends.
Inputs may be any that keep to these rules, and one draw needn't show every extreme that they name: `seg_ids`: each packed row of 1088 tokens holds 1 items numbered 0 upward in order, each of 1024 image codes plus 5 to 64 caption tokens; the rest of the row is padding numbered 1.
All inputs are finite; a program needn't handle non-finite values.
Results may differ from the reference program's by a relative error of at most 0.019.
Values may be sent and summed in bfloat16 or wider, within the bound.
A program may use at most 192 MiB of HBM per device.

```python
import math
import jax
import jax.numpy as jnp
from jax import lax

D = 1024
HEADS = 16
HEAD_DIM = 64
FF = 4096
IMAGE = 1024
CAPTION = 64
ITEMS = 1
MB = 2
PACK = 1088
ROWS = 8704
N_DP = 8


def draw_seg_ids(key, part):
    captions = jax.random.randint(jax.random.fold_in(key, 11), (MB, N_DP_ROWS(), ITEMS), 5, CAPTION + 1)
    lengths = captions + IMAGE
    ends = jnp.cumsum(lengths, axis=-1).astype(jnp.int32)
    positions = jnp.arange(PACK, dtype=jnp.int32)
    numbers = jnp.sum((positions[None, None, :, None] >= ends[:, :, None, :]).astype(jnp.int32), axis=-1)
    return numbers.reshape(MB, ROWS).astype(jnp.int32)


def N_DP_ROWS():
    return ROWS // PACK


def with_spikes(drawn, own_key, source, target, parts, factor):
    owner, partner = [(jnp.arange(drawn.shape[axis_at]) // (drawn.shape[axis_at] // parts)).reshape([-1 if axis == axis_at else 1 for axis in range(drawn.ndim)]) for axis_at in (source, target)]
    chosen = jax.random.permutation(own_key, parts)[partner]
    strong = (owner == chosen) | (owner == (partner + parts // 2) % parts)
    return jnp.where(strong, factor * drawn, drawn)


def levels(rng, dims, pieces, smallest, high):
    loudness = 1.0
    for axis_at, shards_of in pieces:
        steps = jax.random.uniform(jax.random.fold_in(jax.random.fold_in(rng, 6), axis_at), (shards_of,), jnp.float32, smallest / len(pieces), high / len(pieces))
        loudness = loudness * jnp.repeat(jnp.exp(steps), dims[axis_at] // shards_of).reshape((-1,) + (1,) * (len(dims) - 1 - axis_at))
    return loudness


def gaussian(key, dims, deviation, most, split=(), held_as=jnp.bfloat16):
    drawn = jax.random.normal(key, dims, jnp.float32) * deviation
    if len(split) > 0:
        drawn = levels(key, dims, split, -0.22, 0.18) * drawn
    return jnp.clip(drawn, min=-most, max=most).astype(held_as)


def bell_draw_with(rng, extent, deviation, limit, pieces, heavy, kind=jnp.bfloat16):
    drawn = deviation * jax.random.normal(rng, extent, jnp.float32)
    if pieces:
        drawn = drawn * levels(rng, extent, pieces, -0.22, 0.18)
    return jnp.clip(with_spikes(drawn, jax.random.fold_in(rng, 3), *heavy), -limit, limit).astype(kind)


def setup_inputs(seed: int = 0) -> dict:
    key_list = jax.random.split(jax.random.key(seed), 13)
    tokens = gaussian(key_list[0], (MB, ROWS, D), 1.0, 6.0, ((1, 32),))
    seg_ids = draw_seg_ids(jax.random.fold_in(key_list[12], 71), 0)
    qkv_weight = gaussian(key_list[2], (3, D, D), (D // 2) ** -0.5, 0.25, ((1, 8), (2, 4)))
    qv_bias = gaussian(key_list[3], (2, D), 0.3, 2.0, ((1, 32),))
    out_weight = gaussian(key_list[4], (D, D), D ** -0.5, 0.1875, ((0, 32),))
    up_weight = gaussian(key_list[5], (D, FF), D ** -0.5, 0.1875, ((0, 8), (1, 4)))
    up_bias = gaussian(key_list[6], (FF,), 0.5, 3.0, ((0, 32),))
    down_weight = gaussian(key_list[7], (FF, D), FF ** -0.5, 0.09375, ((0, 32),))
    norm_gain = jnp.clip(1.0 + 0.18 * jax.random.normal(key_list[8], (4, D), jnp.float32), 0.099609375, 1.8984375).astype(jnp.bfloat16)
    norm_bias = gaussian(key_list[9], (4, D), 0.3, 2.0, ((1, 8),))
    branch_bias = gaussian(key_list[10], (2, D), 0.5, 3.0, ((1, 8),))
    out_grad = bell_draw_with(key_list[11], (MB, ROWS, D), 1.0, 6.0, ((1, 32),), (1, 2, 32, 2.75))
    return {"tokens": tokens, "seg_ids": seg_ids, "qkv_weight": qkv_weight, "qv_bias": qv_bias, "out_weight": out_weight, "up_weight": up_weight, "up_bias": up_bias, "down_weight": down_weight, "norm_gain": norm_gain, "norm_bias": norm_bias, "branch_bias": branch_bias, "out_grad": out_grad}


ALPHA = 32.0
EPS = 1e-05
HIGH = lax.Precision.HIGHEST

@jax.custom_vjp
def low(v):
    return lax.optimization_barrier(v.astype(jnp.bfloat16)).astype(jnp.float32)

@jax.custom_vjp
def low_back(v):
    return v

def low_keep(v):
    return (low(v), None)

def low_pass(kept, grad):
    return (grad,)

def back_keep(v):
    return (v, None)

def back_low(kept, grad):
    return (low(grad),)
low.defvjp(low_keep, low_pass)
low_back.defvjp(back_keep, back_low)

def normalize(value, gain, shift):
    mean = lax.optimization_barrier(jnp.mean(value, axis=-1, keepdims=True))
    centred = value - mean
    variance = lax.optimization_barrier(jnp.mean(centred * centred, axis=-1, keepdims=True))
    return centred * lax.rsqrt(variance + EPS) * gain + shift

def packed_row(x_row, seg_row, params):
    qkv_w, qv_b, out_w, up_w, up_b, down_w, gains, shifts, branch_b = params
    scale = 1.0 / (ALPHA * math.sqrt(HEAD_DIM))
    h_one = low(normalize(x_row, gains[0], shifts[0]))
    query = jnp.dot(h_one, qkv_w[0], precision=HIGH) + qv_b[0]
    key_full = jnp.dot(h_one, qkv_w[1], precision=HIGH)
    value = jnp.dot(h_one, qkv_w[2], precision=HIGH) + qv_b[1]
    q_heads = low_back(low(query * scale)).reshape(PACK, HEADS, HEAD_DIM)
    k_heads = low_back(low(key_full)).reshape(PACK, HEADS, HEAD_DIM)
    v_heads = low_back(low(value)).reshape(PACK, HEADS, HEAD_DIM)
    block = PACK // 4
    key_pos = jnp.arange(PACK, dtype=jnp.int32)

    def attend(start):
        q_block = lax.dynamic_slice_in_dim(q_heads, start, block, 0)
        seg_block = lax.dynamic_slice_in_dim(seg_row, start, block, 0)
        query_pos = start + jnp.arange(block, dtype=jnp.int32)
        allowed = (seg_block[:, None] == seg_row[None, :]) & (key_pos[None, :] <= query_pos[:, None])
        scores = low_back(jnp.einsum('qhd,khd->hqk', q_block, k_heads, precision=HIGH))
        masked = jnp.where(allowed[None], scores, -1e+30)
        top = lax.optimization_barrier(jnp.max(masked, axis=-1, keepdims=True))
        expo = jnp.exp(ALPHA * (masked - top))
        probs = low(expo / lax.optimization_barrier(jnp.sum(expo, axis=-1, keepdims=True)))
        return jnp.einsum('hqk,khd->qhd', probs, v_heads, precision=HIGH)
    starts = jnp.arange(4, dtype=jnp.int32) * block
    attended = lax.map(jax.checkpoint(attend), starts).reshape(PACK, D)
    attended = low_back(low(attended))
    branch = low_back(jnp.dot(attended, out_w, precision=HIGH) + branch_b[0])
    middle = x_row + normalize(branch, gains[1], shifts[1])
    h_two = low(normalize(middle, gains[2], shifts[2]))
    pre = low_back(jnp.dot(h_two, up_w, precision=HIGH) + up_b)
    act = low(jax.nn.gelu(pre, approximate=False))
    ffn_out = low_back(jnp.dot(act, down_w, precision=HIGH) + branch_b[1])
    return middle + normalize(ffn_out, gains[3], shifts[3])

def reference(tokens, seg_ids, qkv_weight, qv_bias, out_weight, up_weight, up_bias, down_weight, norm_gain, norm_bias, branch_bias, out_grad):
    params = (qkv_weight.astype(jnp.float32), qv_bias.astype(jnp.float32), out_weight.astype(jnp.float32), up_weight.astype(jnp.float32), up_bias.astype(jnp.float32), down_weight.astype(jnp.float32), norm_gain.astype(jnp.float32), norm_bias.astype(jnp.float32), branch_bias.astype(jnp.float32))
    x_all = tokens.astype(jnp.float32).reshape(MB * N_DP, PACK, D)
    segments = seg_ids.reshape(MB * N_DP, PACK)

    def forward(x_rows, weights):

        def one_row(pair):
            return packed_row(pair[0], pair[1], weights)
        return lax.map(jax.checkpoint(one_row), (x_rows, segments))
    result, pull = jax.vjp(forward, x_all, params)
    grad_x, grads = pull(out_grad.astype(jnp.float32).reshape(MB * N_DP, PACK, D))
    return (result.reshape(MB, ROWS, D).astype(jnp.bfloat16), grad_x.reshape(MB, ROWS, D), grads[0], grads[1], grads[2], grads[3], grads[4], grads[5], grads[6], grads[7], grads[8])
```

```python
import functools
import math

import jax
import jax.numpy as jnp
from jax import lax
from jax.experimental import pallas as pl
from jax.experimental.pallas import tpu as pltpu
from jax.sharding import PartitionSpec as P

HEAD_DIM = 64
CAPTION = 64
ALPHA = 32.0
EPS = 1e-05
SCALE = 1.0 / (ALPHA * math.sqrt(HEAD_DIM))
NEG = -1e30
BF = jnp.bfloat16
F32 = jnp.float32


def stats(value):
    mean = jnp.mean(value, axis=-1, keepdims=True)
    centred = value - mean
    inverse = lax.rsqrt(jnp.mean(centred * centred, axis=-1, keepdims=True) + EPS)
    return centred * inverse, inverse


def norm_back(unit, inverse, gain, grad):
    scaled = grad * gain
    grad_in = inverse * (
        scaled
        - jnp.mean(scaled, axis=-1, keepdims=True)
        - unit * jnp.mean(scaled * unit, axis=-1, keepdims=True)
    )
    return grad_in, jnp.sum(grad * unit, axis=0), jnp.sum(grad, axis=0)


def gelu_both(value):
    cdf = 0.5 * (1.0 + lax.erf(value * (1.0 / math.sqrt(2.0))))
    pdf = jnp.exp(-0.5 * value * value) * (1.0 / math.sqrt(2.0 * math.pi))
    return (value * cdf).astype(BF), (cdf + value * pdf).astype(BF)


def dot_nt(a, b):
    return lax.dot_general(a, b, (((1,), (1,)), ((), ())), preferred_element_type=F32)


def dot_tn(a, b):
    return lax.dot_general(a, b, (((0,), (0,)), ((), ())), preferred_element_type=F32)


def dot_nn(a, b):
    return lax.dot_general(a, b, (((1,), (0,)), ((), ())), preferred_element_type=F32)


def row_blocks(length):
    body = length - CAPTION
    cuts = list(range(0, body, 256)) + [body, length]
    return list(zip(cuts[:-1], cuts[1:]))


def masks(start, stop, length, seg_c, seg_r):
    rows = stop - start
    if stop < length:
        causal = lax.broadcasted_iota(jnp.int32, (rows, rows), 0) >= lax.broadcasted_iota(
            jnp.int32, (rows, rows), 1
        )
        return causal, None
    own = lax.broadcasted_iota(jnp.int32, (rows, rows), 0) >= lax.broadcasted_iota(
        jnp.int32, (rows, rows), 1
    )
    same = seg_c[:, 0:1] == seg_r[0:1, start:stop]
    before = seg_c[:, 0:1] == seg_r[0:1, 0:start]
    return own & same, before


def attend_fwd_kernel(q_ref, k_ref, v_ref, segc_ref, segr_ref, o_ref, lse_ref):
    length = q_ref.shape[0]
    lane = lax.broadcasted_iota(jnp.int32, (1, 128), 1)
    for start, stop in row_blocks(length):
        own, before = masks(start, stop, length, segc_ref[...], segr_ref[...])
        outs = []
        lses = []
        for head in range(2):
            q = jnp.where((lane >= 64) == (head == 1), q_ref[start:stop, :], jnp.zeros((), BF))
            s2 = jnp.where(own, dot_nt(q, k_ref[start:stop, :]), NEG)
            top = jnp.max(s2, axis=-1, keepdims=True)
            if start:
                s1 = dot_nt(q, k_ref[0:start, :])
                if before is not None:
                    s1 = jnp.where(before, s1, NEG)
                top = jnp.maximum(top, jnp.max(s1, axis=-1, keepdims=True))
            e2 = jnp.exp(ALPHA * (s2 - top))
            total = jnp.sum(e2, axis=-1, keepdims=True)
            acc = dot_nn(e2.astype(BF), v_ref[start:stop, :])
            if start:
                e1 = jnp.exp(ALPHA * (s1 - top))
                total = total + jnp.sum(e1, axis=-1, keepdims=True)
                acc = acc + dot_nn(e1.astype(BF), v_ref[0:start, :])
            outs.append(acc / total)
            lses.append(ALPHA * top + jnp.log(total))
        o_ref[start:stop, :] = jnp.where(lane < 64, outs[0], outs[1]).astype(BF)
        lse_ref[start:stop, :] = jnp.where(lane < 64, lses[0], lses[1])


def attend_bwd_kernel(
    q_ref, k_ref, v_ref, do_ref, lse_ref, segc_ref, segr_ref, d_ref, dk_ref, dv_ref
):
    length = q_ref.shape[0]
    pair = pl.program_id(0)
    pairs = d_ref.shape[1] // 384
    lane = lax.broadcasted_iota(jnp.int32, (1, 128), 1)
    dk_ref[...] = jnp.zeros_like(dk_ref)
    dv_ref[...] = jnp.zeros_like(dv_ref)
    zero = jnp.zeros((), BF)
    for start, stop in row_blocks(length):
        own, before = masks(start, stop, length, segc_ref[...], segr_ref[...])
        dqs = []
        for head in range(2):
            mine = (lane >= 64) == (head == 1)
            q = jnp.where(mine, q_ref[start:stop, :], zero)
            do = jnp.where(mine, do_ref[start:stop, :], zero)
            lse = lse_ref[start:stop, head * 64 : head * 64 + 1]
            p2 = jnp.where(own, jnp.exp(ALPHA * dot_nt(q, k_ref[start:stop, :]) - lse), 0.0)
            g2 = dot_nt(do, v_ref[start:stop, :])
            delta = jnp.sum(p2 * g2, axis=-1, keepdims=True)
            if start:
                p1 = jnp.exp(ALPHA * dot_nt(q, k_ref[0:start, :]) - lse)
                if before is not None:
                    p1 = jnp.where(before, p1, 0.0)
                g1 = dot_nt(do, v_ref[0:start, :])
                delta = delta + jnp.sum(p1 * g1, axis=-1, keepdims=True)
            ds2 = (ALPHA * p2 * (g2 - delta)).astype(BF)
            dq = dot_nn(ds2, k_ref[start:stop, :])
            dk_ref[start:stop, :] += dot_tn(ds2, q)
            dv_ref[start:stop, :] += dot_tn(p2.astype(BF), do)
            if start:
                ds1 = (ALPHA * p1 * (g1 - delta)).astype(BF)
                dq = dq + dot_nn(ds1, k_ref[0:start, :])
                dk_ref[0:start, :] += dot_tn(ds1, q)
                dv_ref[0:start, :] += dot_tn(p1.astype(BF), do)
            dqs.append(dq)
        merged = jnp.where(lane < 64, dqs[0], dqs[1]) * SCALE
        d_ref[start:stop, pl.ds(pl.multiple_of(pair * 128, 128), 128)] = merged.astype(BF)
    d_ref[:, pl.ds(pl.multiple_of((pairs + pair) * 128, 128), 128)] = dk_ref[...].astype(BF)
    d_ref[:, pl.ds(pl.multiple_of((2 * pairs + pair) * 128, 128), 128)] = dv_ref[...].astype(BF)


def attend_forward(qkv, seg_c, seg_r):
    length, width = qkv.shape
    pairs = width // 384
    col = lambda base: pl.BlockSpec((length, 128), lambda j, base=base: (0, base + j))
    whole = lambda a: pl.BlockSpec(a.shape, lambda j: (0, 0))
    return pl.pallas_call(
        attend_fwd_kernel,
        grid=(pairs,),
        in_specs=[col(0), col(pairs), col(2 * pairs), whole(seg_c), whole(seg_r)],
        out_specs=[col(0), col(0)],
        out_shape=[
            jax.ShapeDtypeStruct((length, 128 * pairs), BF),
            jax.ShapeDtypeStruct((length, 128 * pairs), F32),
        ],
        compiler_params=pltpu.CompilerParams(vmem_limit_bytes=40 << 20),
        cost_estimate=pl.CostEstimate(
            flops=8 * pairs * length * length * 128,
            bytes_accessed=10 * length * 128 * pairs,
            transcendentals=pairs * length * length,
        ),
    )(qkv, qkv, qkv, seg_c, seg_r)


def attend_backward(qkv, grad_o, lse, seg_c, seg_r):
    length, width = qkv.shape
    pairs = width // 384
    col = lambda base: pl.BlockSpec((length, 128), lambda j, base=base: (0, base + j))
    whole = lambda a: pl.BlockSpec(a.shape, lambda j: (0, 0))
    return pl.pallas_call(
        attend_bwd_kernel,
        grid=(pairs,),
        in_specs=[
            col(0),
            col(pairs),
            col(2 * pairs),
            col(0),
            col(0),
            whole(seg_c),
            whole(seg_r),
        ],
        out_specs=pl.BlockSpec((length, width), lambda j: (0, 0)),
        out_shape=jax.ShapeDtypeStruct((length, width), BF),
        scratch_shapes=[pltpu.VMEM((length, 128), F32), pltpu.VMEM((length, 128), F32)],
        compiler_params=pltpu.CompilerParams(vmem_limit_bytes=48 << 20),
        cost_estimate=pl.CostEstimate(
            flops=20 * pairs * length * length * 128,
            bytes_accessed=18 * length * 128 * pairs,
            transcendentals=pairs * length * length,
        ),
    )(qkv, qkv, qkv, grad_o, lse, seg_c, seg_r)


def build(n_dp, n_mp):
    groups = n_dp // 2
    bits = [1 << b for b in range(groups.bit_length() - 1)]
    orders = (bits, bits[::-1])

    def flat(dp, mp):
        return dp * n_mp + mp

    token_out = []
    token_in = []
    for k in range(2):
        pairs_out = []
        for dp in range(n_dp):
            for z in range(n_mp):
                m = (k + z) % 2
                dest = flat(2 * (dp // 2) + z // 2, 2 * m + dp % 2)
                pairs_out.append((flat(dp, z), dest))
        token_out.append(pairs_out)
        token_in.append([(b, a) for a, b in pairs_out])
    weight_out = []
    weight_in = []
    for k in range(n_mp):
        pairs_out = []
        for dp in range(n_dp):
            for z in range(n_mp):
                s = 2 * (z % 2) + dp % 2
                pairs_out.append((flat(dp, z), flat(2 * (dp // 2) + z // 2, s ^ k)))
        weight_out.append(pairs_out)
        weight_in.append([(b, a) for a, b in pairs_out])
    both = ("dp", "mp")

    def swap(value):
        return lax.ppermute(value, "dp", [(i, i ^ 1) for i in range(n_dp)])

    def hop(value, bit):
        return lax.ppermute(value, "dp", [(i, i ^ (2 * bit)) for i in range(n_dp)])

    def on_device(
        tokens,
        seg_ids,
        qkv_weight,
        qv_bias,
        out_weight,
        up_weight,
        up_bias,
        down_weight,
        norm_gain,
        norm_bias,
        branch_bias,
        out_grad,
    ):
        dp = lax.axis_index("dp")
        z = lax.axis_index("mp")
        core = dp % 2
        group = dp // 2
        length = seg_ids.shape[1]
        half = length // 2
        quarter = length // n_mp
        width = tokens.shape[2]

        def pick2(flag, first, second):
            return jnp.where(flag == 0, first, second)

        def to_rows(value):
            got = []
            for k in range(2):
                mine = lax.dynamic_index_in_dim(value, (k + z) % 2, 0, keepdims=False)
                got.append(lax.ppermute(mine, both, token_out[k]))
            m = z // 2
            stack = jnp.stack(got)
            return jnp.concatenate(
                [
                    lax.dynamic_index_in_dim(stack, m, 0, keepdims=False),
                    lax.dynamic_index_in_dim(stack, 1 - m, 0, keepdims=False),
                ]
            )

        def from_rows(value):
            parts = value.reshape(2, quarter, width)
            m = z // 2
            got = []
            for k in range(2):
                mine = lax.dynamic_index_in_dim(parts, (m + k) % 2, 0, keepdims=False)
                got.append(lax.ppermute(mine, both, token_in[k]))
            first = pick2(z % 2, got[0], got[1])
            second = pick2(z % 2, got[1], got[0])
            return first, second

        def gather(block):
            rows, columns = block.shape
            got = [lax.ppermute(block, both, weight_out[k]) for k in range(n_mp)]
            local = jnp.zeros((n_mp, rows, columns), block.dtype)
            for k in range(n_mp):
                local = lax.dynamic_update_slice(local, got[k][None], (z ^ k, 0, 0))
            local = local.reshape(2, 1, 2 * rows, columns)
            result = []
            for i in range(2):
                pieces = [(0, local[i])]
                for bit in orders[i]:
                    pieces = pieces + [(rel ^ bit, hop(piece, bit)) for rel, piece in pieces]
                full = jnp.zeros((groups, 2 * rows, columns), block.dtype)
                for rel, piece in pieces:
                    full = lax.dynamic_update_slice(full, piece, (group ^ rel, 0, 0))
                result.append(full.reshape(n_dp * rows, columns))
            return result

        def scatter(grads):
            kept = []
            for i in range(2):
                total, columns = grads[i].shape
                rows = total // n_dp
                full = grads[i].astype(BF).reshape(groups, 2 * rows, columns)
                pieces = {
                    rel: lax.dynamic_index_in_dim(full, group ^ rel, 0, keepdims=False)
                    for rel in range(groups)
                }
                for bit in orders[i][::-1]:
                    keep = [rel for rel in pieces if not rel & bit]
                    pieces = {
                        rel: (
                            pieces[rel].astype(F32) + hop(pieces[rel ^ bit], bit).astype(F32)
                        ).astype(BF)
                        for rel in keep
                    }
                kept.append(pieces[0].reshape(2, rows, columns))
            local = jnp.concatenate(kept)
            summed = None
            for k in range(n_mp):
                mine = lax.dynamic_index_in_dim(local, z ^ k, 0, keepdims=False)
                got = lax.ppermute(mine, both, weight_in[k]).astype(F32)
                summed = got if summed is None else summed + got
            return summed

        def share(mine):
            other = swap(mine)
            return jnp.concatenate([pick2(core, mine, other), pick2(core, other, mine)])

        def reduce_half(partial):
            theirs = lax.dynamic_slice_in_dim(partial, (1 - core) * half, half, 0)
            ours = lax.dynamic_slice_in_dim(partial, core * half, half, 0)
            return ours.astype(F32) + swap(theirs.astype(BF)).astype(F32)

        x = to_rows(tokens).astype(F32)
        grad_y = to_rows(out_grad).astype(F32)

        per_qv = qv_bias.shape[1]
        slim = width // n_dp
        rows = [
            jnp.pad(value, ((0, 0), (0, slim_up - value.shape[1])))
            for slim_up in [max(slim, 2 * per_qv, up_bias.shape[0])]
            for value in (
                qv_bias.reshape(1, -1),
                up_bias.reshape(1, -1),
                norm_gain,
                norm_bias,
                branch_bias,
            )
        ]
        small = jnp.concatenate(rows, axis=0)
        every = lax.all_gather(small, both, axis=0)
        every = every.reshape(n_dp, n_mp, *small.shape).astype(F32)
        wide = every[:, 0, :, :slim].transpose(1, 0, 2).reshape(small.shape[0], width)
        gains = wide[2:6]
        shifts = wide[6:10]
        branch_b = wide[10:12]
        served = lax.dynamic_slice_in_dim(every, 2 * core, 2, 1)
        qv_b = served[:, :, 0, : 2 * per_qv].reshape(n_dp, 2, 2, per_qv)
        qv_b = qv_b.transpose(1, 2, 0, 3).reshape(2, 2, n_dp * per_qv)
        up_b = served[:, :, 1, : up_bias.shape[0]].transpose(1, 0, 2).reshape(2, -1)

        seg_other = swap(seg_ids)
        seg_own = pick2((core + z) % 2, seg_ids, seg_other)
        seg_row = lax.dynamic_index_in_dim(seg_own, z // 2, 0, keepdims=False)
        seg_r = jnp.broadcast_to(seg_row[None, :], (8, length))
        seg_c = jnp.broadcast_to(seg_row[length - CAPTION :, None], (CAPTION, 128))

        block_qkv = qkv_weight.transpose(1, 0, 2).reshape(qkv_weight.shape[1], -1)
        w_qkv = gather(block_qkv)
        n_out = out_weight.shape[0]
        w_out = gather(out_weight)
        w_up = gather(up_weight)
        w_down = gather(down_weight)

        unit0, inv0 = stats(x)
        h1 = share((unit0 * gains[0] + shifts[0]).astype(BF))
        cols = w_qkv[0].shape[1] // 3
        qkvs = []
        attended = []
        log_sums = []
        partial = None
        for i in range(2):
            bias = jnp.concatenate([qv_b[i, 0], jnp.zeros((cols,), F32), qv_b[i, 1]])
            factor = jnp.concatenate([jnp.full((cols,), SCALE, F32), jnp.ones((2 * cols,), F32)])
            qkv = ((dot_nn(h1, w_qkv[i]) + bias) * factor).astype(BF)
            o, lse = attend_forward(qkv, seg_c, seg_r)
            qkvs.append(qkv)
            attended.append(o)
            log_sums.append(lse)
            term = dot_nn(o, w_out[i])
            partial = term if partial is None else partial + term
        branch = reduce_half(partial) + branch_b[0]
        unit1, inv1 = stats(branch)
        middle = x + unit1 * gains[1] + shifts[1]
        unit2, inv2 = stats(middle)
        h2 = share((unit2 * gains[2] + shifts[2]).astype(BF))
        acts = []
        slopes = []
        partial = None
        for i in range(2):
            act, slope = gelu_both(dot_nn(h2, w_up[i]) + up_b[i])
            acts.append(act)
            slopes.append(slope)
            term = dot_nn(act, w_down[i])
            partial = term if partial is None else partial + term
        ffn_out = reduce_half(partial) + branch_b[1]
        unit3, inv3 = stats(ffn_out)
        out_rows = (middle + unit3 * gains[3] + shifts[3]).astype(BF)
        layer_out = jnp.stack(from_rows(out_rows))

        grad_f, dgain3, dshift3 = norm_back(unit3, inv3, gains[3], grad_y)
        grad_f = grad_f.astype(BF)
        dbranch1 = jnp.sum(grad_f.astype(F32), axis=0)
        grad_f_all = share(grad_f)
        dw_down = []
        dw_up = []
        dup = []
        partial = None
        for i in range(2):
            dw_down.append(dot_tn(acts[i], grad_f_all))
            grad_pre = (dot_nt(grad_f_all, w_down[i]) * slopes[i].astype(F32)).astype(BF)
            dup.append(jnp.sum(grad_pre.astype(F32), axis=0))
            dw_up.append(dot_tn(h2, grad_pre))
            term = dot_nt(grad_pre, w_up[i])
            partial = term if partial is None else partial + term
        down_grad = scatter(dw_down)
        up_grad = scatter(dw_up)
        grad_h2 = reduce_half(partial)
        back2, dgain2, dshift2 = norm_back(unit2, inv2, gains[2], grad_h2)
        grad_mid = grad_y + back2
        grad_a, dgain1, dshift1 = norm_back(unit1, inv1, gains[1], grad_mid)
        grad_a = grad_a.astype(BF)
        dbranch0 = jnp.sum(grad_a.astype(F32), axis=0)
        grad_a_all = share(grad_a)
        dw_out = []
        dw_qkv = []
        dqv = []
        partial = None
        for i in range(2):
            dw_out.append(dot_tn(attended[i], grad_a_all))
            grad_o = dot_nt(grad_a_all, w_out[i]).astype(BF)
            grad_qkv = attend_backward(qkvs[i], grad_o, log_sums[i], seg_c, seg_r)
            sums = jnp.sum(grad_qkv.astype(F32), axis=0)
            dqv.append(jnp.stack([sums[:cols], sums[2 * cols :]]))
            dw_qkv.append(dot_tn(h1, grad_qkv))
            term = dot_nt(grad_qkv, w_qkv[i])
            partial = term if partial is None else partial + term
        out_grad_w = scatter(dw_out)
        qkv_grad = scatter(dw_qkv)
        grad_h1 = reduce_half(partial)
        back0, dgain0, dshift0 = norm_back(unit0, inv0, gains[0], grad_h1)
        input_grad = jnp.stack(from_rows((grad_mid + back0).astype(BF))).astype(F32)
        qkv_grad = qkv_grad.reshape(qkv_weight.shape[1], 3, cols).transpose(1, 0, 2)

        n_ff = up_bias.shape[0] * n_dp * n_mp
        placed_up = lax.dynamic_update_slice(
            jnp.zeros((n_ff,), F32), jnp.concatenate(dup), (core * (n_ff // 2),)
        )
        placed_qv = lax.dynamic_update_slice(
            jnp.zeros((2, width), F32), jnp.concatenate(dqv, axis=1), (0, core * (width // 2))
        )
        vectors = jnp.concatenate(
            [
                jnp.stack(
                    [
                        dgain0,
                        dgain1,
                        dgain2,
                        dgain3,
                        dshift0,
                        dshift1,
                        dshift2,
                        dshift3,
                        dbranch0,
                        dbranch1,
                    ]
                ),
                placed_qv,
                placed_up.reshape(-1, width),
            ]
        )
        vectors = lax.psum(vectors, both)
        mine = lax.dynamic_slice_in_dim(vectors[:10], dp * slim, slim, 1)
        where_qv = (z * n_dp + dp) * per_qv
        qv_grad = lax.dynamic_slice_in_dim(vectors[10:12], where_qv, per_qv, 1)
        up_bias_grad = lax.dynamic_slice_in_dim(
            vectors[12:].reshape(-1), (z * n_dp + dp) * up_bias.shape[0], up_bias.shape[0], 0
        )
        return (
            layer_out,
            input_grad,
            qkv_grad,
            qv_grad,
            out_grad_w,
            up_grad,
            up_bias_grad,
            down_grad,
            mine[0:4],
            mine[4:8],
            mine[8:10],
        )

    return on_device


def solution(mesh):
    n_dp, n_mp = mesh.shape["dp"], mesh.shape["mp"]
    in_specs = (
        P(None, ("dp", "mp"), None),
        P(None, "dp"),
        P(None, "dp", "mp"),
        P(None, ("mp", "dp")),
        P(("mp", "dp"), None),
        P("dp", "mp"),
        P(("mp", "dp")),
        P(("mp", "dp"), None),
        P(None, "dp"),
        P(None, "dp"),
        P(None, "dp"),
        P(None, ("dp", "mp"), None),
    )
    out_specs = (
        P(None, ("dp", "mp"), None),
        P(None, ("dp", "mp"), None),
        P(None, "dp", "mp"),
        P(None, ("mp", "dp")),
        P(("mp", "dp"), None),
        P("dp", "mp"),
        P(("mp", "dp")),
        P(("mp", "dp"), None),
        P(None, "dp"),
        P(None, "dp"),
        P(None, "dp"),
    )
    return jax.shard_map(
        build(n_dp, n_mp), mesh=mesh, in_specs=in_specs, out_specs=out_specs, check_vma=False
    )
```

```python
import functools
import math

import jax
import jax.numpy as jnp
from jax import lax
from jax.experimental import pallas as pl
from jax.experimental.pallas import tpu as pltpu
from jax.sharding import PartitionSpec as P

HEAD_DIM = 64
CAPTION = 64
ALPHA = 32.0
EPS = 1e-05
SCALE = 1.0 / (ALPHA * math.sqrt(HEAD_DIM))
NEG = -1e30
BF = jnp.bfloat16
F32 = jnp.float32


def stats(value):
    mean = jnp.mean(value, axis=-1, keepdims=True)
    centred = value - mean
    inverse = lax.rsqrt(jnp.mean(centred * centred, axis=-1, keepdims=True) + EPS)
    return centred * inverse, inverse


def norm_back(unit, inverse, gain, grad):
    scaled = grad * gain
    grad_in = inverse * (
        scaled
        - jnp.mean(scaled, axis=-1, keepdims=True)
        - unit * jnp.mean(scaled * unit, axis=-1, keepdims=True)
    )
    return grad_in, jnp.sum(grad * unit, axis=0), jnp.sum(grad, axis=0)


def gelu_both(value):
    cdf = 0.5 * (1.0 + lax.erf(value * (1.0 / math.sqrt(2.0))))
    pdf = jnp.exp(-0.5 * value * value) * (1.0 / math.sqrt(2.0 * math.pi))
    return (value * cdf).astype(BF), (cdf + value * pdf).astype(BF)


def dot_nt(a, b):
    return lax.dot_general(a, b, (((1,), (1,)), ((), ())), preferred_element_type=F32)


def dot_tn(a, b):
    return lax.dot_general(a, b, (((0,), (0,)), ((), ())), preferred_element_type=F32)


def dot_nn(a, b):
    return lax.dot_general(a, b, (((1,), (0,)), ((), ())), preferred_element_type=F32)


def row_blocks(length):
    body = length - CAPTION
    cuts = list(range(0, body, 256)) + [body, length]
    return list(zip(cuts[:-1], cuts[1:]))


def masks(start, stop, length, seg_c, seg_r):
    rows = stop - start
    if stop < length:
        causal = lax.broadcasted_iota(jnp.int32, (rows, rows), 0) >= lax.broadcasted_iota(
            jnp.int32, (rows, rows), 1
        )
        return causal, None
    own = lax.broadcasted_iota(jnp.int32, (rows, rows), 0) >= lax.broadcasted_iota(
        jnp.int32, (rows, rows), 1
    )
    same = seg_c[:, 0:1] == seg_r[0:1, start:stop]
    before = seg_c[:, 0:1] == seg_r[0:1, 0:start]
    return own & same, before


def attend_fwd_kernel(q_ref, k_ref, v_ref, segc_ref, segr_ref, o_ref, lse_ref):
    length = q_ref.shape[0]
    lane = lax.broadcasted_iota(jnp.int32, (1, 128), 1)
    for start, stop in row_blocks(length):
        own, before = masks(start, stop, length, segc_ref[...], segr_ref[...])
        outs = []
        lses = []
        for head in range(2):
            q = jnp.where((lane >= 64) == (head == 1), q_ref[start:stop, :], jnp.zeros((), BF))
            s2 = jnp.where(own, dot_nt(q, k_ref[start:stop, :]), NEG)
            top = jnp.max(s2, axis=-1, keepdims=True)
            if start:
                s1 = dot_nt(q, k_ref[0:start, :])
                if before is not None:
                    s1 = jnp.where(before, s1, NEG)
                top = jnp.maximum(top, jnp.max(s1, axis=-1, keepdims=True))
            e2 = jnp.exp(ALPHA * (s2 - top))
            total = jnp.sum(e2, axis=-1, keepdims=True)
            acc = dot_nn(e2.astype(BF), v_ref[start:stop, :])
            if start:
                e1 = jnp.exp(ALPHA * (s1 - top))
                total = total + jnp.sum(e1, axis=-1, keepdims=True)
                acc = acc + dot_nn(e1.astype(BF), v_ref[0:start, :])
            outs.append(acc / total)
            lses.append(ALPHA * top + jnp.log(total))
        o_ref[start:stop, :] = jnp.where(lane < 64, outs[0], outs[1]).astype(BF)
        lse_ref[start:stop, :] = jnp.where(lane < 64, lses[0], lses[1])


def attend_bwd_kernel(
    q_ref, k_ref, v_ref, do_ref, lse_ref, segc_ref, segr_ref, d_ref, dk_ref, dv_ref
):
    length = q_ref.shape[0]
    pair = pl.program_id(0)
    pairs = d_ref.shape[1] // 384
    lane = lax.broadcasted_iota(jnp.int32, (1, 128), 1)
    dk_ref[...] = jnp.zeros_like(dk_ref)
    dv_ref[...] = jnp.zeros_like(dv_ref)
    zero = jnp.zeros((), BF)
    for start, stop in row_blocks(length):
        own, before = masks(start, stop, length, segc_ref[...], segr_ref[...])
        dqs = []
        for head in range(2):
            mine = (lane >= 64) == (head == 1)
            q = jnp.where(mine, q_ref[start:stop, :], zero)
            do = jnp.where(mine, do_ref[start:stop, :], zero)
            lse = lse_ref[start:stop, head * 64 : head * 64 + 1]
            p2 = jnp.where(own, jnp.exp(ALPHA * dot_nt(q, k_ref[start:stop, :]) - lse), 0.0)
            g2 = dot_nt(do, v_ref[start:stop, :])
            delta = jnp.sum(p2 * g2, axis=-1, keepdims=True)
            if start:
                p1 = jnp.exp(ALPHA * dot_nt(q, k_ref[0:start, :]) - lse)
                if before is not None:
                    p1 = jnp.where(before, p1, 0.0)
                g1 = dot_nt(do, v_ref[0:start, :])
                delta = delta + jnp.sum(p1 * g1, axis=-1, keepdims=True)
            ds2 = (ALPHA * p2 * (g2 - delta)).astype(BF)
            dq = dot_nn(ds2, k_ref[start:stop, :])
            dk_ref[start:stop, :] += dot_tn(ds2, q)
            dv_ref[start:stop, :] += dot_tn(p2.astype(BF), do)
            if start:
                ds1 = (ALPHA * p1 * (g1 - delta)).astype(BF)
                dq = dq + dot_nn(ds1, k_ref[0:start, :])
                dk_ref[0:start, :] += dot_tn(ds1, q)
                dv_ref[0:start, :] += dot_tn(p1.astype(BF), do)
            dqs.append(dq)
        merged = jnp.where(lane < 64, dqs[0], dqs[1]) * SCALE
        d_ref[start:stop, pl.ds(pl.multiple_of(pair * 128, 128), 128)] = merged.astype(BF)
    d_ref[:, pl.ds(pl.multiple_of((pairs + pair) * 128, 128), 128)] = dk_ref[...].astype(BF)
    d_ref[:, pl.ds(pl.multiple_of((2 * pairs + pair) * 128, 128), 128)] = dv_ref[...].astype(BF)


def attend_forward(qkv, seg_c, seg_r):
    length, width = qkv.shape
    pairs = width // 384
    col = lambda base: pl.BlockSpec((length, 128), lambda j, base=base: (0, base + j))
    whole = lambda a: pl.BlockSpec(a.shape, lambda j: (0, 0))
    return pl.pallas_call(
        attend_fwd_kernel,
        grid=(pairs,),
        in_specs=[col(0), col(pairs), col(2 * pairs), whole(seg_c), whole(seg_r)],
        out_specs=[col(0), col(0)],
        out_shape=[
            jax.ShapeDtypeStruct((length, 128 * pairs), BF),
            jax.ShapeDtypeStruct((length, 128 * pairs), F32),
        ],
        compiler_params=pltpu.CompilerParams(vmem_limit_bytes=40 << 20),
        cost_estimate=pl.CostEstimate(
            flops=8 * pairs * length * length * 128,
            bytes_accessed=10 * length * 128 * pairs,
            transcendentals=pairs * length * length,
        ),
    )(qkv, qkv, qkv, seg_c, seg_r)


def attend_backward(qkv, grad_o, lse, seg_c, seg_r):
    length, width = qkv.shape
    pairs = width // 384
    col = lambda base: pl.BlockSpec((length, 128), lambda j, base=base: (0, base + j))
    whole = lambda a: pl.BlockSpec(a.shape, lambda j: (0, 0))
    return pl.pallas_call(
        attend_bwd_kernel,
        grid=(pairs,),
        in_specs=[
            col(0),
            col(pairs),
            col(2 * pairs),
            col(0),
            col(0),
            whole(seg_c),
            whole(seg_r),
        ],
        out_specs=pl.BlockSpec((length, width), lambda j: (0, 0)),
        out_shape=jax.ShapeDtypeStruct((length, width), BF),
        scratch_shapes=[pltpu.VMEM((length, 128), F32), pltpu.VMEM((length, 128), F32)],
        compiler_params=pltpu.CompilerParams(vmem_limit_bytes=48 << 20),
        cost_estimate=pl.CostEstimate(
            flops=20 * pairs * length * length * 128,
            bytes_accessed=18 * length * 128 * pairs,
            transcendentals=pairs * length * length,
        ),
    )(qkv, qkv, qkv, grad_o, lse, seg_c, seg_r)


MESH = pl.DeviceIdType.MESH


def plan_hops(groups, which):
    bits = [1 << b for b in range(groups.bit_length() - 1)]
    if len(bits) == 2 and which:
        bits = bits[::-1]
    known = [0]
    steps = []
    for bit in bits:
        steps.append((bit, list(known)))
        known = known + [rel ^ bit for rel in known]
    return steps


class Links:
    def __init__(self, n_dp, n_mp, send_sems):
        self.n_dp, self.n_mp = n_dp, n_mp
        self.dp = lax.axis_index("dp")
        self.z = lax.axis_index("mp")
        self.core = lax.rem(self.dp, 2)
        self.group = self.dp // 2
        self.send_sems = send_sems
        self.used = 0
        self.open = []

    def barrier(self):
        sem = pltpu.get_barrier_semaphore()
        count = 0
        for cc in range(2):
            for zz in range(self.n_mp):

                @pl.when(jnp.logical_or(cc != self.core, zz != self.z))
                def _(cc=cc, zz=zz):
                    pl.semaphore_signal(
                        sem, inc=1, device_id=(2 * self.group + cc, zz), device_id_type=MESH
                    )

                count += 1
        bit = 1
        while bit < self.n_dp // 2:
            pl.semaphore_signal(
                sem, inc=1, device_id=(self.dp ^ (2 * bit), self.z), device_id_type=MESH
            )
            count += 1
            bit *= 2
        pl.semaphore_wait(sem, count - 1)

    def send(self, src, dst, recv_sem, dp, z):
        copy = pltpu.make_async_remote_copy(
            src_ref=src,
            dst_ref=dst,
            send_sem=self.send_sems.at[self.used],
            recv_sem=recv_sem,
            device_id=(dp, z),
            device_id_type=MESH,
        )
        copy.start()
        self.used += 1
        self.open.append((None, copy))

    def send_or_keep(self, src, dst, recv_sem, dp, z):
        own = jnp.logical_and(dp == self.dp, z == self.z)
        copy = pltpu.make_async_remote_copy(
            src_ref=src,
            dst_ref=dst,
            send_sem=self.send_sems.at[self.used],
            recv_sem=recv_sem,
            device_id=(dp, z),
            device_id_type=MESH,
        )
        here = pltpu.make_async_copy(src, dst, recv_sem)

        @pl.when(jnp.logical_not(own))
        def _():
            copy.start()

        @pl.when(own)
        def _():
            here.start()

        self.used += 1
        self.open.append((own, copy))

    def arrived(self, src, dst, recv_sem):
        pltpu.make_async_remote_copy(
            src_ref=src,
            dst_ref=dst,
            send_sem=self.send_sems.at[0],
            recv_sem=recv_sem,
            device_id=(self.dp ^ 1, self.z),
            device_id_type=MESH,
        ).wait_recv()

    def finish(self):
        for own, copy in self.open:
            if own is None:
                copy.wait_send()
            else:

                @pl.when(jnp.logical_not(own))
                def _(copy=copy):
                    copy.wait_send()

        self.open = []


def rows_at(index, rows):
    return pl.ds(pl.multiple_of(index * rows, rows), rows)


class Gather:
    def __init__(self, links, src, dst, col_sems, hop_sems):
        self.links, self.src, self.dst = links, src, dst
        self.rows = src.shape[0]
        self.col_sems, self.hop_sems = col_sems, hop_sems
        self.groups = links.n_dp // 2

    def column(self):
        k = self.links
        i = lax.rem(k.z, 2)
        for zz in range(k.n_mp):
            k.send_or_keep(
                self.src,
                self.dst.at[i, rows_at(k.dp, self.rows), :],
                self.col_sems.at[i, k.core],
                2 * k.group + k.z // 2,
                zz,
            )

    def piece(self, i, group):
        return self.dst.at[i, rows_at(group, 2 * self.rows), :]

    def column_wait(self, i):
        for c in range(2):
            self.links.arrived(
                self.src,
                self.dst.at[i, rows_at(2 * self.links.group + c, self.rows), :],
                self.col_sems.at[i, c],
            )

    def hop(self, i, rel, bit):
        k = self.links
        piece = self.piece(i, k.group ^ rel)
        k.send(piece, piece, self.hop_sems.at[i, rel ^ bit], k.dp ^ (2 * bit), k.z)

    def hop_wait(self, i, rel):
        piece = self.piece(i, self.links.group ^ rel)
        self.links.arrived(piece, piece, self.hop_sems.at[i, rel])

    def first(self):
        for i in range(2):
            self.column_wait(i)
            for bit, _ in plan_hops(self.groups, i):
                self.hop(i, 0, bit)

    def second(self):
        steps = [plan_hops(self.groups, i) for i in range(2)]
        self.waited = [set(), set()]
        for level in range(1, len(steps[0])):
            for i in range(2):
                bit, known = steps[i][level]
                for rel in known[1:]:
                    if rel not in self.waited[i]:
                        self.hop_wait(i, rel)
                        self.waited[i].add(rel)
                    self.hop(i, rel, bit)

    def last(self):
        for i in range(2):
            for rel in range(1, self.groups):
                if rel not in self.waited[i]:
                    self.hop_wait(i, rel)


def exchange_tokens(links, src, dst, sems):
    quarter = src.shape[1]
    for m in range(2):
        links.send_or_keep(
            src.at[m],
            dst.at[rows_at(lax.rem(links.z, 2), quarter), :],
            sems.at[lax.rem(links.z, 2)],
            2 * links.group + links.z // 2,
            2 * m + links.core,
        )


def exchange_tokens_wait(links, src, dst, sems):
    quarter = src.shape[1]
    for s in range(2):
        links.arrived(src.at[0], dst.at[pl.ds(s * quarter, quarter), :], sems.at[s])


def gather_kernel(n_dp, n_mp, *refs):
    tokens, grads = refs[0:2]
    blocks = refs[2:7]
    x_out, g_out = refs[7:9]
    fulls = refs[9:14]
    send_sems, col_sems, hop_sems, tok_sems = refs[14:18]
    links = Links(n_dp, n_mp, send_sems)
    links.barrier()
    ways = [
        Gather(links, blocks[a], fulls[a], col_sems.at[a], hop_sems.at[a]) for a in range(5)
    ]
    ways[0].column()
    ways[1].column()
    exchange_tokens(links, tokens, x_out, tok_sems.at[0])
    for way in ways[2:]:
        way.column()
    exchange_tokens(links, grads, g_out, tok_sems.at[1])
    ways[0].first()
    for a in range(1, 5):
        ways[a].first()
        ways[a - 1].second()
    ways[4].second()
    exchange_tokens_wait(links, tokens, x_out, tok_sems.at[0])
    exchange_tokens_wait(links, grads, g_out, tok_sems.at[1])
    for way in ways:
        way.last()
    links.finish()


def gather_all(n_dp, n_mp, tokens, grads, blocks):
    groups = n_dp // 2
    hops = groups - 1
    any_spec = pl.BlockSpec(memory_space=pl.ANY)
    half = (2 * tokens.shape[1], tokens.shape[2])
    shapes = [jax.ShapeDtypeStruct(half, tokens.dtype)] * 2 + [
        jax.ShapeDtypeStruct((2, n_dp * b.shape[0], b.shape[1]), b.dtype) for b in blocks
    ]
    return pl.pallas_call(
        functools.partial(gather_kernel, n_dp, n_mp),
        in_specs=[any_spec] * 7,
        out_specs=[any_spec] * 7,
        out_shape=shapes,
        scratch_shapes=[
            pltpu.SemaphoreType.DMA((4 + 5 * (n_mp + 2 * hops),)),
            pltpu.SemaphoreType.DMA((5, 2, 2)),
            pltpu.SemaphoreType.DMA((5, 2, groups)),
            pltpu.SemaphoreType.DMA((2, 2)),
        ],
        compiler_params=pltpu.CompilerParams(collective_id=0, has_side_effects=True),
    )(tokens, grads, *blocks)


def build(n_dp, n_mp):
    groups = n_dp // 2
    bits = [1 << b for b in range(groups.bit_length() - 1)]
    orders = (bits, bits[::-1])

    def flat(dp, mp):
        return dp * n_mp + mp

    token_out = []
    token_in = []
    for k in range(2):
        pairs_out = []
        for dp in range(n_dp):
            for z in range(n_mp):
                m = (k + z) % 2
                dest = flat(2 * (dp // 2) + z // 2, 2 * m + dp % 2)
                pairs_out.append((flat(dp, z), dest))
        token_out.append(pairs_out)
        token_in.append([(b, a) for a, b in pairs_out])
    weight_out = []
    weight_in = []
    for k in range(n_mp):
        pairs_out = []
        for dp in range(n_dp):
            for z in range(n_mp):
                s = 2 * (z % 2) + dp % 2
                pairs_out.append((flat(dp, z), flat(2 * (dp // 2) + z // 2, s ^ k)))
        weight_out.append(pairs_out)
        weight_in.append([(b, a) for a, b in pairs_out])
    both = ("dp", "mp")

    def swap(value):
        return lax.ppermute(value, "dp", [(i, i ^ 1) for i in range(n_dp)])

    def hop(value, bit):
        return lax.ppermute(value, "dp", [(i, i ^ (2 * bit)) for i in range(n_dp)])

    def on_device(
        tokens,
        seg_ids,
        qkv_weight,
        qv_bias,
        out_weight,
        up_weight,
        up_bias,
        down_weight,
        norm_gain,
        norm_bias,
        branch_bias,
        out_grad,
    ):
        dp = lax.axis_index("dp")
        z = lax.axis_index("mp")
        core = dp % 2
        group = dp // 2
        length = seg_ids.shape[1]
        half = length // 2
        quarter = length // n_mp
        width = tokens.shape[2]

        def pick2(flag, first, second):
            return jnp.where(flag == 0, first, second)

        def to_rows(value):
            got = []
            for k in range(2):
                mine = lax.dynamic_index_in_dim(value, (k + z) % 2, 0, keepdims=False)
                got.append(lax.ppermute(mine, both, token_out[k]))
            m = z // 2
            stack = jnp.stack(got)
            return jnp.concatenate(
                [
                    lax.dynamic_index_in_dim(stack, m, 0, keepdims=False),
                    lax.dynamic_index_in_dim(stack, 1 - m, 0, keepdims=False),
                ]
            )

        def from_rows(value):
            parts = value.reshape(2, quarter, width)
            m = z // 2
            got = []
            for k in range(2):
                mine = lax.dynamic_index_in_dim(parts, (m + k) % 2, 0, keepdims=False)
                got.append(lax.ppermute(mine, both, token_in[k]))
            first = pick2(z % 2, got[0], got[1])
            second = pick2(z % 2, got[1], got[0])
            return first, second

        def gather(block):
            rows, columns = block.shape
            got = [lax.ppermute(block, both, weight_out[k]) for k in range(n_mp)]
            local = jnp.zeros((n_mp, rows, columns), block.dtype)
            for k in range(n_mp):
                local = lax.dynamic_update_slice(local, got[k][None], (z ^ k, 0, 0))
            local = local.reshape(2, 1, 2 * rows, columns)
            result = []
            for i in range(2):
                pieces = [(0, local[i])]
                for bit in orders[i]:
                    pieces = pieces + [(rel ^ bit, hop(piece, bit)) for rel, piece in pieces]
                full = jnp.zeros((groups, 2 * rows, columns), block.dtype)
                for rel, piece in pieces:
                    full = lax.dynamic_update_slice(full, piece, (group ^ rel, 0, 0))
                result.append(full.reshape(n_dp * rows, columns))
            return result

        def scatter(grads):
            kept = []
            for i in range(2):
                total, columns = grads[i].shape
                rows = total // n_dp
                full = grads[i].astype(BF).reshape(groups, 2 * rows, columns)
                pieces = {
                    rel: lax.dynamic_index_in_dim(full, group ^ rel, 0, keepdims=False)
                    for rel in range(groups)
                }
                for bit in orders[i][::-1]:
                    keep = [rel for rel in pieces if not rel & bit]
                    pieces = {
                        rel: (
                            pieces[rel].astype(F32) + hop(pieces[rel ^ bit], bit).astype(F32)
                        ).astype(BF)
                        for rel in keep
                    }
                kept.append(pieces[0].reshape(2, rows, columns))
            local = jnp.concatenate(kept)
            summed = None
            for k in range(n_mp):
                mine = lax.dynamic_index_in_dim(local, z ^ k, 0, keepdims=False)
                got = lax.ppermute(mine, both, weight_in[k]).astype(F32)
                summed = got if summed is None else summed + got
            return summed

        def share(mine):
            other = swap(mine)
            return jnp.concatenate([pick2(core, mine, other), pick2(core, other, mine)])

        def reduce_half(partial):
            theirs = lax.dynamic_slice_in_dim(partial, (1 - core) * half, half, 0)
            ours = lax.dynamic_slice_in_dim(partial, core * half, half, 0)
            return ours.astype(F32) + swap(theirs.astype(BF)).astype(F32)

        per_qv = qv_bias.shape[1]
        slim = width // n_dp
        rows = [
            jnp.pad(value, ((0, 0), (0, slim_up - value.shape[1])))
            for slim_up in [max(slim, 2 * per_qv, up_bias.shape[0])]
            for value in (
                qv_bias.reshape(1, -1),
                up_bias.reshape(1, -1),
                norm_gain,
                norm_bias,
                branch_bias,
            )
        ]
        small = jnp.concatenate(rows, axis=0)
        small = jnp.pad(small, ((0, 16 - small.shape[0]), (0, 0)))
        small = jnp.pad(small, ((0, 0), (0, max(0, 128 - small.shape[1]))))
        block_qkv = qkv_weight.transpose(1, 0, 2).reshape(qkv_weight.shape[1], -1)
        x, grad_y, every, w_qkv, w_out, w_up, w_down = gather_all(
            n_dp,
            n_mp,
            tokens,
            out_grad,
            [small, block_qkv, out_weight, up_weight, down_weight],
        )
        x = x.astype(F32)
        grad_y = grad_y.astype(F32)
        every = every.reshape(2, n_dp, *small.shape).astype(F32)
        wide = every[0, :, :, :slim].transpose(1, 0, 2).reshape(small.shape[0], width)
        gains = wide[2:6]
        shifts = wide[6:10]
        branch_b = wide[10:12]
        qv_b = every[:, :, 0, : 2 * per_qv].reshape(2, n_dp, 2, per_qv)
        qv_b = qv_b.transpose(0, 2, 1, 3).reshape(2, 2, n_dp * per_qv)
        up_b = every[:, :, 1, : up_bias.shape[0]].reshape(2, -1)

        seg_other = swap(seg_ids)
        seg_own = pick2((core + z) % 2, seg_ids, seg_other)
        seg_row = lax.dynamic_index_in_dim(seg_own, z // 2, 0, keepdims=False)
        seg_r = jnp.broadcast_to(seg_row[None, :], (8, length))
        seg_c = jnp.broadcast_to(seg_row[length - CAPTION :, None], (CAPTION, 128))

        unit0, inv0 = stats(x)
        h1 = share((unit0 * gains[0] + shifts[0]).astype(BF))
        cols = w_qkv[0].shape[1] // 3
        qkvs = []
        attended = []
        log_sums = []
        partial = None
        for i in range(2):
            bias = jnp.concatenate([qv_b[i, 0], jnp.zeros((cols,), F32), qv_b[i, 1]])
            factor = jnp.concatenate([jnp.full((cols,), SCALE, F32), jnp.ones((2 * cols,), F32)])
            qkv = ((dot_nn(h1, w_qkv[i]) + bias) * factor).astype(BF)
            o, lse = attend_forward(qkv, seg_c, seg_r)
            qkvs.append(qkv)
            attended.append(o)
            log_sums.append(lse)
            term = dot_nn(o, w_out[i])
            partial = term if partial is None else partial + term
        branch = reduce_half(partial) + branch_b[0]
        unit1, inv1 = stats(branch)
        middle = x + unit1 * gains[1] + shifts[1]
        unit2, inv2 = stats(middle)
        h2 = share((unit2 * gains[2] + shifts[2]).astype(BF))
        acts = []
        slopes = []
        partial = None
        for i in range(2):
            act, slope = gelu_both(dot_nn(h2, w_up[i]) + up_b[i])
            acts.append(act)
            slopes.append(slope)
            term = dot_nn(act, w_down[i])
            partial = term if partial is None else partial + term
        ffn_out = reduce_half(partial) + branch_b[1]
        unit3, inv3 = stats(ffn_out)
        out_rows = (middle + unit3 * gains[3] + shifts[3]).astype(BF)
        layer_out = jnp.stack(from_rows(out_rows))

        grad_f, dgain3, dshift3 = norm_back(unit3, inv3, gains[3], grad_y)
        grad_f = grad_f.astype(BF)
        dbranch1 = jnp.sum(grad_f.astype(F32), axis=0)
        grad_f_all = share(grad_f)
        dw_down = []
        dw_up = []
        dup = []
        partial = None
        for i in range(2):
            dw_down.append(dot_tn(acts[i], grad_f_all))
            grad_pre = (dot_nt(grad_f_all, w_down[i]) * slopes[i].astype(F32)).astype(BF)
            dup.append(jnp.sum(grad_pre.astype(F32), axis=0))
            dw_up.append(dot_tn(h2, grad_pre))
            term = dot_nt(grad_pre, w_up[i])
            partial = term if partial is None else partial + term
        down_grad = scatter(dw_down)
        up_grad = scatter(dw_up)
        grad_h2 = reduce_half(partial)
        back2, dgain2, dshift2 = norm_back(unit2, inv2, gains[2], grad_h2)
        grad_mid = grad_y + back2
        grad_a, dgain1, dshift1 = norm_back(unit1, inv1, gains[1], grad_mid)
        grad_a = grad_a.astype(BF)
        dbranch0 = jnp.sum(grad_a.astype(F32), axis=0)
        grad_a_all = share(grad_a)
        dw_out = []
        dw_qkv = []
        dqv = []
        partial = None
        for i in range(2):
            dw_out.append(dot_tn(attended[i], grad_a_all))
            grad_o = dot_nt(grad_a_all, w_out[i]).astype(BF)
            grad_qkv = attend_backward(qkvs[i], grad_o, log_sums[i], seg_c, seg_r)
            sums = jnp.sum(grad_qkv.astype(F32), axis=0)
            dqv.append(jnp.stack([sums[:cols], sums[2 * cols :]]))
            dw_qkv.append(dot_tn(h1, grad_qkv))
            term = dot_nt(grad_qkv, w_qkv[i])
            partial = term if partial is None else partial + term
        out_grad_w = scatter(dw_out)
        qkv_grad = scatter(dw_qkv)
        grad_h1 = reduce_half(partial)
        back0, dgain0, dshift0 = norm_back(unit0, inv0, gains[0], grad_h1)
        input_grad = jnp.stack(from_rows((grad_mid + back0).astype(BF))).astype(F32)
        qkv_grad = qkv_grad.reshape(qkv_weight.shape[1], 3, cols).transpose(1, 0, 2)

        n_ff = up_bias.shape[0] * n_dp * n_mp
        placed_up = lax.dynamic_update_slice(
            jnp.zeros((n_ff,), F32), jnp.concatenate(dup), (core * (n_ff // 2),)
        )
        placed_qv = lax.dynamic_update_slice(
            jnp.zeros((2, width), F32), jnp.concatenate(dqv, axis=1), (0, core * (width // 2))
        )
        vectors = jnp.concatenate(
            [
                jnp.stack(
                    [
                        dgain0,
                        dgain1,
                        dgain2,
                        dgain3,
                        dshift0,
                        dshift1,
                        dshift2,
                        dshift3,
                        dbranch0,
                        dbranch1,
                    ]
                ),
                placed_qv,
                placed_up.reshape(-1, width),
            ]
        )
        vectors = lax.psum(vectors, both)
        mine = lax.dynamic_slice_in_dim(vectors[:10], dp * slim, slim, 1)
        where_qv = (z * n_dp + dp) * per_qv
        qv_grad = lax.dynamic_slice_in_dim(vectors[10:12], where_qv, per_qv, 1)
        up_bias_grad = lax.dynamic_slice_in_dim(
            vectors[12:].reshape(-1), (z * n_dp + dp) * up_bias.shape[0], up_bias.shape[0], 0
        )
        return (
            layer_out,
            input_grad,
            qkv_grad,
            qv_grad,
            out_grad_w,
            up_grad,
            up_bias_grad,
            down_grad,
            mine[0:4],
            mine[4:8],
            mine[8:10],
        )

    return on_device


def solution(mesh):
    n_dp, n_mp = mesh.shape["dp"], mesh.shape["mp"]
    in_specs = (
        P(None, ("dp", "mp"), None),
        P(None, "dp"),
        P(None, "dp", "mp"),
        P(None, ("mp", "dp")),
        P(("mp", "dp"), None),
        P("dp", "mp"),
        P(("mp", "dp")),
        P(("mp", "dp"), None),
        P(None, "dp"),
        P(None, "dp"),
        P(None, "dp"),
        P(None, ("dp", "mp"), None),
    )
    out_specs = (
        P(None, ("dp", "mp"), None),
        P(None, ("dp", "mp"), None),
        P(None, "dp", "mp"),
        P(None, ("mp", "dp")),
        P(("mp", "dp"), None),
        P("dp", "mp"),
        P(("mp", "dp")),
        P(("mp", "dp"), None),
        P(None, "dp"),
        P(None, "dp"),
        P(None, "dp"),
    )
    return jax.shard_map(
        build(n_dp, n_mp), mesh=mesh, in_specs=in_specs, out_specs=out_specs, check_vma=False
    )
```

```python
import functools
import math

import jax
import jax.numpy as jnp
from jax import lax
from jax.experimental import pallas as pl
from jax.experimental.pallas import tpu as pltpu
from jax.sharding import PartitionSpec as P

HEAD_DIM = 64
CAPTION = 64
ALPHA = 32.0
EPS = 1e-05
SCALE = 1.0 / (ALPHA * math.sqrt(HEAD_DIM))
NEG = -1e30
BF = jnp.bfloat16
F32 = jnp.float32


def stats(value):
    mean = jnp.mean(value, axis=-1, keepdims=True)
    centred = value - mean
    inverse = lax.rsqrt(jnp.mean(centred * centred, axis=-1, keepdims=True) + EPS)
    return centred * inverse, inverse


def norm_back(unit, inverse, gain, grad):
    scaled = grad * gain
    grad_in = inverse * (
        scaled
        - jnp.mean(scaled, axis=-1, keepdims=True)
        - unit * jnp.mean(scaled * unit, axis=-1, keepdims=True)
    )
    return grad_in, jnp.sum(grad * unit, axis=0), jnp.sum(grad, axis=0)


def gelu_both(value):
    cdf = 0.5 * (1.0 + lax.erf(value * (1.0 / math.sqrt(2.0))))
    pdf = jnp.exp(-0.5 * value * value) * (1.0 / math.sqrt(2.0 * math.pi))
    return (value * cdf).astype(BF), (cdf + value * pdf).astype(BF)


def dot_nt(a, b):
    return lax.dot_general(a, b, (((1,), (1,)), ((), ())), preferred_element_type=F32)


def dot_tn(a, b):
    return lax.dot_general(a, b, (((0,), (0,)), ((), ())), preferred_element_type=F32)


def dot_nn(a, b):
    return lax.dot_general(a, b, (((1,), (0,)), ((), ())), preferred_element_type=F32)


def row_blocks(length):
    body = length - CAPTION
    cuts = list(range(0, body, 256)) + [body, length]
    return list(zip(cuts[:-1], cuts[1:]))


def masks(start, stop, length, count):
    rows = stop - start
    query = lax.broadcasted_iota(jnp.int32, (rows, 1), 0)
    own = query >= lax.broadcasted_iota(jnp.int32, (1, rows), 1)
    if stop < length:
        return own, None
    real = query + start < count
    same = real == (lax.broadcasted_iota(jnp.int32, (1, rows), 1) + start < count)
    before = real == (lax.broadcasted_iota(jnp.int32, (1, start), 1) < count)
    return jnp.logical_and(own, same), before


def attend_bwd_kernel(
    q_ref, k_ref, v_ref, do_ref, lse_ref, count_ref, d_ref, dk_ref, dv_ref
):
    length = q_ref.shape[0]
    pair = pl.program_id(0)
    pairs = d_ref.shape[1] // 384
    lane = lax.broadcasted_iota(jnp.int32, (1, 128), 1)
    dk_ref[...] = jnp.zeros_like(dk_ref)
    dv_ref[...] = jnp.zeros_like(dv_ref)
    zero = jnp.zeros((), BF)
    for start, stop in row_blocks(length):
        own, before = masks(start, stop, length, count_ref[0:1, 0:1])
        dqs = []
        for head in range(2):
            mine = (lane >= 64) == (head == 1)
            q = jnp.where(mine, q_ref[start:stop, :], zero)
            do = jnp.where(mine, do_ref[start:stop, :], zero)
            lse = lse_ref[start:stop, head * 64 : head * 64 + 1]
            p2 = jnp.where(own, jnp.exp(ALPHA * dot_nt(q, k_ref[start:stop, :]) - lse), 0.0)
            g2 = dot_nt(do, v_ref[start:stop, :])
            delta = jnp.sum(p2 * g2, axis=-1, keepdims=True)
            if start:
                p1 = jnp.exp(ALPHA * dot_nt(q, k_ref[0:start, :]) - lse)
                if before is not None:
                    p1 = jnp.where(before, p1, 0.0)
                g1 = dot_nt(do, v_ref[0:start, :])
                delta = delta + jnp.sum(p1 * g1, axis=-1, keepdims=True)
            ds2 = (ALPHA * p2 * (g2 - delta)).astype(BF)
            dq = dot_nn(ds2, k_ref[start:stop, :])
            dk_ref[start:stop, :] += dot_tn(ds2, q)
            dv_ref[start:stop, :] += dot_tn(p2.astype(BF), do)
            if start:
                ds1 = (ALPHA * p1 * (g1 - delta)).astype(BF)
                dq = dq + dot_nn(ds1, k_ref[0:start, :])
                dk_ref[0:start, :] += dot_tn(ds1, q)
                dv_ref[0:start, :] += dot_tn(p1.astype(BF), do)
            dqs.append(dq)
        merged = jnp.where(lane < 64, dqs[0], dqs[1]) * SCALE
        d_ref[start:stop, pl.ds(pl.multiple_of(pair * 128, 128), 128)] = merged.astype(BF)
    d_ref[:, pl.ds(pl.multiple_of((pairs + pair) * 128, 128), 128)] = dk_ref[...].astype(BF)
    d_ref[:, pl.ds(pl.multiple_of((2 * pairs + pair) * 128, 128), 128)] = dv_ref[...].astype(BF)


def attend_backward(qkv, grad_o, lse, count):
    length, width = qkv.shape
    pairs = width // 384
    col = lambda base: pl.BlockSpec((length, 128), lambda j, base=base: (0, base + j))
    whole = lambda a: pl.BlockSpec(a.shape, lambda j: (0, 0))
    return pl.pallas_call(
        attend_bwd_kernel,
        grid=(pairs,),
        in_specs=[
            col(0),
            col(pairs),
            col(2 * pairs),
            col(0),
            col(0),
            whole(count),
        ],
        out_specs=pl.BlockSpec((length, width), lambda j: (0, 0)),
        out_shape=jax.ShapeDtypeStruct((length, width), BF),
        scratch_shapes=[pltpu.VMEM((length, 128), F32), pltpu.VMEM((length, 128), F32)],
        compiler_params=pltpu.CompilerParams(vmem_limit_bytes=48 << 20),
        cost_estimate=pl.CostEstimate(
            flops=20 * pairs * length * length * 128,
            bytes_accessed=18 * length * 128 * pairs,
            transcendentals=pairs * length * length,
        ),
    )(qkv, qkv, qkv, grad_o, lse, count)


MESH = pl.DeviceIdType.MESH


def plan_hops(groups, which):
    bits = [1 << b for b in range(groups.bit_length() - 1)]
    if len(bits) == 2 and which:
        bits = bits[::-1]
    known = [0]
    steps = []
    for bit in bits:
        steps.append((bit, list(known)))
        known = known + [rel ^ bit for rel in known]
    return steps


class Links:
    def __init__(self, n_dp, n_mp, send_sems):
        self.n_dp, self.n_mp = n_dp, n_mp
        self.dp = lax.axis_index("dp")
        self.z = lax.axis_index("mp")
        self.core = lax.rem(self.dp, 2)
        self.group = self.dp // 2
        self.send_sems = send_sems
        self.used = 0
        self.open = []

    def barrier(self):
        sem = pltpu.get_barrier_semaphore()
        count = 0
        for cc in range(2):
            for zz in range(self.n_mp):

                @pl.when(jnp.logical_or(cc != self.core, zz != self.z))
                def _(cc=cc, zz=zz):
                    pl.semaphore_signal(
                        sem, inc=1, device_id=(2 * self.group + cc, zz), device_id_type=MESH
                    )

                count += 1
        bit = 1
        while bit < self.n_dp // 2:
            pl.semaphore_signal(
                sem, inc=1, device_id=(self.dp ^ (2 * bit), self.z), device_id_type=MESH
            )
            count += 1
            bit *= 2
        pl.semaphore_wait(sem, count - 1)

    def send(self, src, dst, recv_sem, dp, z):
        copy = pltpu.make_async_remote_copy(
            src_ref=src,
            dst_ref=dst,
            send_sem=self.send_sems.at[self.used],
            recv_sem=recv_sem,
            device_id=(dp, z),
            device_id_type=MESH,
        )
        copy.start()
        self.used += 1
        self.open.append((None, copy))

    def send_or_keep(self, src, dst, recv_sem, dp, z):
        own = jnp.logical_and(dp == self.dp, z == self.z)
        copy = pltpu.make_async_remote_copy(
            src_ref=src,
            dst_ref=dst,
            send_sem=self.send_sems.at[self.used],
            recv_sem=recv_sem,
            device_id=(dp, z),
            device_id_type=MESH,
        )
        here = pltpu.make_async_copy(src, dst, recv_sem)

        @pl.when(jnp.logical_not(own))
        def _():
            copy.start()

        @pl.when(own)
        def _():
            here.start()

        self.used += 1
        self.open.append((own, copy))

    def send_if(self, condition, src, dst, recv_sem, dp, z):
        copy = pltpu.make_async_remote_copy(
            src_ref=src,
            dst_ref=dst,
            send_sem=self.send_sems.at[self.used],
            recv_sem=recv_sem,
            device_id=(dp, z),
            device_id_type=MESH,
        )

        @pl.when(condition)
        def _():
            copy.start()

        self.used += 1
        self.open.append((jnp.logical_not(condition), copy))

    def arrived(self, src, dst, recv_sem):
        pltpu.make_async_remote_copy(
            src_ref=src,
            dst_ref=dst,
            send_sem=self.send_sems.at[0],
            recv_sem=recv_sem,
            device_id=(self.dp ^ 1, self.z),
            device_id_type=MESH,
        ).wait_recv()

    def finish(self):
        for own, copy in self.open:
            if own is None:
                copy.wait_send()
            else:

                @pl.when(jnp.logical_not(own))
                def _(copy=copy):
                    copy.wait_send()

        self.open = []


def rows_at(index, rows):
    return pl.ds(pl.multiple_of(index * rows, rows), rows)


def exchange_tokens(links, src, dst, sems):
    quarter = src.shape[1]
    for m in range(2):
        links.send_or_keep(
            src.at[m],
            dst.at[rows_at(lax.rem(links.z, 2), quarter), :],
            sems.at[lax.rem(links.z, 2)],
            2 * links.group + links.z // 2,
            2 * m + links.core,
        )


def exchange_tokens_wait(links, src, dst, sems):
    quarter = src.shape[1]
    for s in range(2):
        links.arrived(src.at[0], dst.at[pl.ds(s * quarter, quarter), :], sems.at[s])


class Column:
    def __init__(self, links, src, dst, col_sems, hop_sems):
        self.links, self.src, self.dst = links, src, dst
        self.rows = src.shape[0]
        self.col_sems, self.hop_sems = col_sems, hop_sems
        self.groups = links.n_dp // 2
        self.waited = [set(), set()]

    def start(self):
        k = self.links
        i = lax.rem(k.z, 2)
        home = k.z // 2
        step = 1 - 2 * home
        dst = self.dst.at[i, rows_at(k.dp, self.rows), :]
        sem = self.col_sems.at[i, k.core]
        owner = 2 * k.group + home
        k.send(self.src, dst, sem, owner, k.z + step)
        k.send_if(jnp.logical_or(k.z == 1, k.z == 2), self.src, dst, sem, owner, k.z - step)
        k.send_or_keep(self.src, dst, sem, owner, k.z)

    def piece(self, i, group):
        return self.dst.at[i, rows_at(group, 2 * self.rows), :]

    def hop(self, i, rel, bit):
        k = self.links
        piece = self.piece(i, k.group ^ rel)
        k.send(piece, piece, self.hop_sems.at[i, rel ^ bit], k.dp ^ (2 * bit), k.z)

    def hop_wait(self, i, rel):
        if rel not in self.waited[i]:
            piece = self.piece(i, self.links.group ^ rel)
            self.links.arrived(piece, piece, self.hop_sems.at[i, rel])
            self.waited[i].add(rel)

    def first(self):
        k = self.links
        for i in range(2):
            for c in range(2):
                block = self.dst.at[i, rows_at(2 * k.group + c, self.rows), :]
                k.arrived(self.src, block, self.col_sems.at[i, c])
            up = jnp.logical_and(k.core == 0, jnp.logical_and(k.z > i, k.z < k.n_mp - 1))
            down = jnp.logical_and(k.core == 1, jnp.logical_and(k.z < 2 + i, k.z > 0))
            onward = jnp.logical_or(up, down)
            for c in range(2):
                block = self.dst.at[i, rows_at(2 * k.group + c, self.rows), :]
                k.send_if(
                    onward, block, block, self.col_sems.at[i, c], k.dp, k.z + 1 - 2 * k.core
                )
            for bit, _ in plan_hops(self.groups, i):
                self.hop(i, 0, bit)

    def second(self):
        steps = [plan_hops(self.groups, i) for i in range(2)]
        for level in range(1, len(steps[0])):
            for i in range(2):
                bit, known = steps[i][level]
                for rel in known[1:]:
                    self.hop_wait(i, rel)
                    self.hop(i, rel, bit)

    def last(self):
        for i in range(2):
            for rel in range(1, self.groups):
                self.hop_wait(i, rel)


def sends_of_column(n_mp, hops):
    return 3 + 4 + 2 * hops


def forward_kernel(n_dp, n_mp, *refs):
    (tokens, grads, seg_ref) = refs[0:3]
    blocks = refs[3:8]
    (x_out, g_out, h1_out, qkv_out, o_out, lse_out, a_out, mid_out, h2_out) = refs[8:17]
    (act_out, slope_out, f_out, y_out) = refs[17:21]
    w_outs = refs[21:25]
    count_out, vec_ref = refs[25:27]
    weights = refs[27:32]
    (xb, seg_other, h1, qkv, o, lse, a_send, a_recv, a_own, mid) = refs[32:42]
    (h2, act, slope, f_send, f_recv, f_own, y, bias_ref, upb_ref) = refs[42:51]
    (send_sems, col_sems, hop_sems, tok_sems, swap_sems, keep_sems) = refs[51:57]
    smalls, w_qkv, w_out, w_up, w_down = weights
    links = Links(n_dp, n_mp, send_sems)
    half = xb.shape[0]
    length = 2 * half
    tile = half // 2
    other = links.dp + 1 - 2 * links.core
    mine0 = links.core * half
    other0 = (1 - links.core) * half
    kept = []

    def keep(src, dst):
        copy = pltpu.make_async_copy(src, dst, keep_sems.at[len(kept)])
        copy.start()
        kept.append(copy)

    def at(start, rows):
        return pl.ds(pl.multiple_of(start, 16), rows)

    links.barrier()
    ways = [Column(links, blocks[a], weights[a], col_sems.at[a], hop_sems.at[a]) for a in range(5)]
    v_way, q_way, o_way, u_way, d_way = ways
    v_way.start()
    q_way.start()
    o_way.start()
    links.send(seg_ref, seg_other, swap_sems.at[0], other, links.z)
    v_way.first()
    u_way.start()
    q_way.first()
    exchange_tokens(links, tokens, xb, tok_sems.at[0])
    v_way.second()
    o_way.first()
    q_way.second()
    d_way.start()
    u_way.first()
    o_way.second()
    links.arrived(seg_ref, seg_other, swap_sems.at[0])
    pick = lax.rem(links.core + links.z, 2) == 0
    seg_row = jnp.where(
        pick, seg_ref[pl.ds(links.z // 2, 1), :], seg_other[pl.ds(links.z // 2, 1), :]
    )
    count = jnp.sum((seg_row == 0).astype(jnp.int32), axis=1, keepdims=True)
    count_out[...] = jnp.broadcast_to(count, count_out.shape)
    v_way.last()
    spread_smalls(n_dp, smalls, vec_ref, bias_ref, upb_ref)
    exchange_tokens_wait(links, tokens, xb, tok_sems.at[0])
    keep(xb, x_out)

    def first_norm(t, _):
        rows = at(t * tile, tile)
        unit, _ = stats(xb[rows, :].astype(F32))
        h1[at(mine0 + t * tile, tile), :] = (unit * vec_ref[0:1, :] + vec_ref[4:5, :]).astype(BF)
        return 0

    lax.fori_loop(0, 2, first_norm, 0)
    links.send(h1.at[at(mine0, half), :], h1.at[at(mine0, half), :], swap_sems.at[1], other, links.z)
    q_way.last()
    cols = qkv.shape[2] // 3
    scale_row = jnp.where(
        lax.broadcasted_iota(jnp.int32, (1, 3 * cols), 1) < cols, SCALE, 1.0
    ).astype(F32)

    def project(start):
        def body(t, _):
            rows = at(start + t * tile, tile)
            for i in range(2):
                value = dot_nn(h1[rows, :], w_qkv[i]) + bias_ref[i : i + 1, :]
                qkv[i, rows, :] = (value * scale_row).astype(BF)
            return 0

        lax.fori_loop(0, 2, body, 0)

    project(mine0)
    links.arrived(
        h1.at[at(mine0, half), :], h1.at[at(other0, half), :], swap_sems.at[1]
    )
    project(other0)
    keep(h1, h1_out)
    keep(qkv, qkv_out)
    u_way.second()
    d_way.first()
    exchange_tokens(links, grads, g_out, tok_sems.at[1])
    pairs = cols // 128

    def attend(i):
        def body(j, _):
            attend_pair_fwd(
                qkv.at[i, :, pl.ds(pl.multiple_of(j * 128, 128), 128)],
                qkv.at[i, :, pl.ds(pl.multiple_of((pairs + j) * 128, 128), 128)],
                qkv.at[i, :, pl.ds(pl.multiple_of((2 * pairs + j) * 128, 128), 128)],
                count,
                o.at[i, :, pl.ds(pl.multiple_of(j * 128, 128), 128)],
                lse.at[i, :, pl.ds(pl.multiple_of(j * 128, 128), 128)],
            )
            return 0

        lax.fori_loop(0, pairs, body, 0)

    attend(0)
    attend(1)
    d_way.second()
    keep(o, o_out)
    keep(lse, lse_out)
    o_way.last()

    def out_tile(start):
        return dot_nn(o[0, at(start, tile), :], w_out[0]) + dot_nn(
            o[1, at(start, tile), :], w_out[1]
        )

    def out_theirs(t, _):
        a_send[at(t * tile, tile), :] = out_tile(other0 + t * tile).astype(BF)
        return 0

    def out_ours(t, _):
        a_own[at(t * tile, tile), :] = out_tile(mine0 + t * tile)
        return 0

    lax.fori_loop(0, 2, out_theirs, 0)
    links.send(a_send, a_recv, swap_sems.at[2], other, links.z)
    lax.fori_loop(0, 2, out_ours, 0)
    links.arrived(a_send, a_recv, swap_sems.at[2])

    def middle_norms(t, _):
        rows = at(t * tile, tile)
        branch = a_own[rows, :] + a_recv[rows, :].astype(F32) + vec_ref[8:9, :]
        a_own[rows, :] = branch
        unit, _ = stats(branch)
        middle = xb[rows, :].astype(F32) + unit * vec_ref[1:2, :] + vec_ref[5:6, :]
        mid[rows, :] = middle
        unit, _ = stats(middle)
        h2[at(mine0 + t * tile, tile), :] = (unit * vec_ref[2:3, :] + vec_ref[6:7, :]).astype(BF)
        return 0

    lax.fori_loop(0, 2, middle_norms, 0)
    links.send(h2.at[at(mine0, half), :], h2.at[at(mine0, half), :], swap_sems.at[3], other, links.z)
    keep(a_own, a_out)
    keep(mid, mid_out)
    u_way.last()

    def up(start):
        def body(t, _):
            rows = at(start + t * tile, tile)
            for i in range(2):
                value, slant = gelu_both(dot_nn(h2[rows, :], w_up[i]) + upb_ref[i : i + 1, :])
                act[i, rows, :] = value
                slope[i, rows, :] = slant
            return 0

        lax.fori_loop(0, 2, body, 0)

    up(mine0)
    links.arrived(h2.at[at(mine0, half), :], h2.at[at(other0, half), :], swap_sems.at[3])
    up(other0)
    keep(h2, h2_out)
    keep(act, act_out)
    keep(slope, slope_out)
    d_way.last()

    def down_tile(start):
        return dot_nn(act[0, at(start, tile), :], w_down[0]) + dot_nn(
            act[1, at(start, tile), :], w_down[1]
        )

    def down_theirs(t, _):
        f_send[at(t * tile, tile), :] = down_tile(other0 + t * tile).astype(BF)
        return 0

    def down_ours(t, _):
        f_own[at(t * tile, tile), :] = down_tile(mine0 + t * tile)
        return 0

    lax.fori_loop(0, 2, down_theirs, 0)
    links.send(f_send, f_recv, swap_sems.at[4], other, links.z)
    lax.fori_loop(0, 2, down_ours, 0)
    for weight, w_hbm in zip(weights[1:], w_outs):
        keep(weight, w_hbm)
    links.arrived(f_send, f_recv, swap_sems.at[4])

    def last_norm(t, _):
        rows = at(t * tile, tile)
        value = f_own[rows, :] + f_recv[rows, :].astype(F32) + vec_ref[9:10, :]
        f_own[rows, :] = value
        unit, _ = stats(value)
        y[rows, :] = (mid[rows, :] + unit * vec_ref[3:4, :] + vec_ref[7:8, :]).astype(BF)
        return 0

    lax.fori_loop(0, 2, last_norm, 0)
    keep(f_own, f_out)
    keep(y, y_out)
    exchange_tokens_wait(links, grads, g_out, tok_sems.at[1])
    for copy in kept:
        copy.wait()
    links.finish()


def spread_smalls(n_dp, smalls, vec_ref, bias_ref, upb_ref):
    width = vec_ref.shape[1]
    slim = width // n_dp
    per_qv = bias_ref.shape[1] // 3 // n_dp
    per_up = upb_ref.shape[1] // n_dp
    row = [
        [smalls[i, 16 * dp : 16 * dp + 16, :].astype(F32) for dp in range(n_dp)] for i in range(2)
    ]
    wide = jnp.concatenate([row[0][dp][2:12, 0:slim] for dp in range(n_dp)], axis=1)
    vec_ref[0:10, :] = wide
    vec_ref[10:16, :] = jnp.zeros((6, width), F32)
    for i in range(2):
        queries = [row[i][dp][0:1, 0:per_qv] for dp in range(n_dp)]
        values = [row[i][dp][0:1, per_qv : 2 * per_qv] for dp in range(n_dp)]
        zeros = [jnp.zeros((1, n_dp * per_qv), F32)]
        bias_ref[i : i + 1, :] = jnp.concatenate(queries + zeros + values, axis=1)
        upb_ref[i : i + 1, :] = jnp.concatenate(
            [row[i][dp][1:2, 0:per_up] for dp in range(n_dp)], axis=1
        )


def attend_pair_fwd(q_ref, k_ref, v_ref, count, o_ref, lse_ref):
    length = q_ref.shape[0]
    lane = lax.broadcasted_iota(jnp.int32, (1, 128), 1)
    for start, stop in row_blocks(length):
        own, before = masks(start, stop, length, count)
        outs = []
        lses = []
        for head in range(2):
            q = jnp.where((lane >= 64) == (head == 1), q_ref[start:stop, :], jnp.zeros((), BF))
            s2 = jnp.where(own, dot_nt(q, k_ref[start:stop, :]), NEG)
            top = jnp.max(s2, axis=-1, keepdims=True)
            if start:
                s1 = dot_nt(q, k_ref[0:start, :])
                if before is not None:
                    s1 = jnp.where(before, s1, NEG)
                top = jnp.maximum(top, jnp.max(s1, axis=-1, keepdims=True))
            e2 = jnp.exp(ALPHA * (s2 - top))
            total = jnp.sum(e2, axis=-1, keepdims=True)
            acc = dot_nn(e2.astype(BF), v_ref[start:stop, :])
            if start:
                e1 = jnp.exp(ALPHA * (s1 - top))
                total = total + jnp.sum(e1, axis=-1, keepdims=True)
                acc = acc + dot_nn(e1.astype(BF), v_ref[0:start, :])
            outs.append(acc / total)
            lses.append(ALPHA * top + jnp.log(total))
        o_ref[start:stop, :] = jnp.where(lane < 64, outs[0], outs[1]).astype(BF)
        lse_ref[start:stop, :] = jnp.where(lane < 64, lses[0], lses[1])


def forward_all(n_dp, n_mp, tokens, grads, seg_ids, blocks):
    groups = n_dp // 2
    hops = groups - 1
    any_spec = pl.BlockSpec(memory_space=pl.ANY)
    vmem = pl.BlockSpec(memory_space=pltpu.VMEM)
    width = tokens.shape[2]
    half = 2 * tokens.shape[1]
    length = 2 * half
    cols3 = blocks[1].shape[1]
    cols = cols3 // 3
    ff = n_dp * blocks[4].shape[0]
    shape = jax.ShapeDtypeStruct
    full = [(2, n_dp * b.shape[0], b.shape[1]) for b in blocks]
    out_shape = [
        shape((half, width), BF),
        shape((half, width), BF),
        shape((length, width), BF),
        shape((2, length, cols3), BF),
        shape((2, length, cols), BF),
        shape((2, length, cols), F32),
        shape((half, width), F32),
        shape((half, width), F32),
        shape((length, width), BF),
        shape((2, length, ff), BF),
        shape((2, length, ff), BF),
        shape((half, width), F32),
        shape((half, width), BF),
    ] + [shape(f, BF) for f in full[1:]] + [shape((8, 128), jnp.int32), shape((16, width), F32)]
    return pl.pallas_call(
        functools.partial(forward_kernel, n_dp, n_mp),
        in_specs=[any_spec] * 2 + [vmem] + [any_spec] * 5,
        out_specs=[any_spec] * 17 + [vmem] * 2,
        out_shape=out_shape,
        scratch_shapes=[pltpu.VMEM(f, BF) for f in full]
        + [
            pltpu.VMEM((half, width), BF),
            pltpu.VMEM(seg_ids.shape, jnp.int32),
            pltpu.VMEM((length, width), BF),
            pltpu.VMEM((2, length, cols3), BF),
            pltpu.VMEM((2, length, cols), BF),
            pltpu.VMEM((2, length, cols), F32),
            pltpu.VMEM((half, width), BF),
            pltpu.VMEM((half, width), BF),
            pltpu.VMEM((half, width), F32),
            pltpu.VMEM((half, width), F32),
            pltpu.VMEM((length, width), BF),
            pltpu.VMEM((2, length, ff), BF),
            pltpu.VMEM((2, length, ff), BF),
            pltpu.VMEM((half, width), BF),
            pltpu.VMEM((half, width), BF),
            pltpu.VMEM((half, width), F32),
            pltpu.VMEM((half, width), BF),
            pltpu.VMEM((2, cols3), F32),
            pltpu.VMEM((2, ff), F32),
            pltpu.SemaphoreType.DMA((9 + 5 * sends_of_column(n_mp, hops),)),
            pltpu.SemaphoreType.DMA((5, 2, 2)),
            pltpu.SemaphoreType.DMA((5, 2, groups)),
            pltpu.SemaphoreType.DMA((2, 2)),
            pltpu.SemaphoreType.DMA((5,)),
            pltpu.SemaphoreType.DMA((17,)),
        ],
        compiler_params=pltpu.CompilerParams(
            collective_id=0, has_side_effects=True, vmem_limit_bytes=60 << 20
        ),
    )(tokens, grads, seg_ids, *blocks)


def build(n_dp, n_mp):
    groups = n_dp // 2
    bits = [1 << b for b in range(groups.bit_length() - 1)]
    orders = (bits, bits[::-1])

    def flat(dp, mp):
        return dp * n_mp + mp

    token_out = []
    token_in = []
    for k in range(2):
        pairs_out = []
        for dp in range(n_dp):
            for z in range(n_mp):
                m = (k + z) % 2
                dest = flat(2 * (dp // 2) + z // 2, 2 * m + dp % 2)
                pairs_out.append((flat(dp, z), dest))
        token_out.append(pairs_out)
        token_in.append([(b, a) for a, b in pairs_out])
    weight_out = []
    weight_in = []
    for k in range(n_mp):
        pairs_out = []
        for dp in range(n_dp):
            for z in range(n_mp):
                s = 2 * (z % 2) + dp % 2
                pairs_out.append((flat(dp, z), flat(2 * (dp // 2) + z // 2, s ^ k)))
        weight_out.append(pairs_out)
        weight_in.append([(b, a) for a, b in pairs_out])
    both = ("dp", "mp")

    def swap(value):
        return lax.ppermute(value, "dp", [(i, i ^ 1) for i in range(n_dp)])

    def hop(value, bit):
        return lax.ppermute(value, "dp", [(i, i ^ (2 * bit)) for i in range(n_dp)])

    def on_device(
        tokens,
        seg_ids,
        qkv_weight,
        qv_bias,
        out_weight,
        up_weight,
        up_bias,
        down_weight,
        norm_gain,
        norm_bias,
        branch_bias,
        out_grad,
    ):
        dp = lax.axis_index("dp")
        z = lax.axis_index("mp")
        core = dp % 2
        group = dp // 2
        length = seg_ids.shape[1]
        half = length // 2
        quarter = length // n_mp
        width = tokens.shape[2]

        def pick2(flag, first, second):
            return jnp.where(flag == 0, first, second)

        def to_rows(value):
            got = []
            for k in range(2):
                mine = lax.dynamic_index_in_dim(value, (k + z) % 2, 0, keepdims=False)
                got.append(lax.ppermute(mine, both, token_out[k]))
            m = z // 2
            stack = jnp.stack(got)
            return jnp.concatenate(
                [
                    lax.dynamic_index_in_dim(stack, m, 0, keepdims=False),
                    lax.dynamic_index_in_dim(stack, 1 - m, 0, keepdims=False),
                ]
            )

        def from_rows(value):
            parts = value.reshape(2, quarter, width)
            m = z // 2
            got = []
            for k in range(2):
                mine = lax.dynamic_index_in_dim(parts, (m + k) % 2, 0, keepdims=False)
                got.append(lax.ppermute(mine, both, token_in[k]))
            first = pick2(z % 2, got[0], got[1])
            second = pick2(z % 2, got[1], got[0])
            return first, second

        def gather(block):
            rows, columns = block.shape
            got = [lax.ppermute(block, both, weight_out[k]) for k in range(n_mp)]
            local = jnp.zeros((n_mp, rows, columns), block.dtype)
            for k in range(n_mp):
                local = lax.dynamic_update_slice(local, got[k][None], (z ^ k, 0, 0))
            local = local.reshape(2, 1, 2 * rows, columns)
            result = []
            for i in range(2):
                pieces = [(0, local[i])]
                for bit in orders[i]:
                    pieces = pieces + [(rel ^ bit, hop(piece, bit)) for rel, piece in pieces]
                full = jnp.zeros((groups, 2 * rows, columns), block.dtype)
                for rel, piece in pieces:
                    full = lax.dynamic_update_slice(full, piece, (group ^ rel, 0, 0))
                result.append(full.reshape(n_dp * rows, columns))
            return result

        def scatter(grads):
            kept = []
            for i in range(2):
                total, columns = grads[i].shape
                rows = total // n_dp
                full = grads[i].astype(BF).reshape(groups, 2 * rows, columns)
                pieces = {
                    rel: lax.dynamic_index_in_dim(full, group ^ rel, 0, keepdims=False)
                    for rel in range(groups)
                }
                for bit in orders[i][::-1]:
                    keep = [rel for rel in pieces if not rel & bit]
                    pieces = {
                        rel: (
                            pieces[rel].astype(F32) + hop(pieces[rel ^ bit], bit).astype(F32)
                        ).astype(BF)
                        for rel in keep
                    }
                kept.append(pieces[0].reshape(2, rows, columns))
            local = jnp.concatenate(kept)
            summed = None
            for k in range(n_mp):
                mine = lax.dynamic_index_in_dim(local, z ^ k, 0, keepdims=False)
                got = lax.ppermute(mine, both, weight_in[k]).astype(F32)
                summed = got if summed is None else summed + got
            return summed

        def share(mine):
            other = swap(mine)
            return jnp.concatenate([pick2(core, mine, other), pick2(core, other, mine)])

        def reduce_half(partial):
            theirs = lax.dynamic_slice_in_dim(partial, (1 - core) * half, half, 0)
            ours = lax.dynamic_slice_in_dim(partial, core * half, half, 0)
            return ours.astype(F32) + swap(theirs.astype(BF)).astype(F32)

        per_qv = qv_bias.shape[1]
        slim = width // n_dp
        rows = [
            jnp.pad(value, ((0, 0), (0, slim_up - value.shape[1])))
            for slim_up in [max(slim, 2 * per_qv, up_bias.shape[0])]
            for value in (
                qv_bias.reshape(1, -1),
                up_bias.reshape(1, -1),
                norm_gain,
                norm_bias,
                branch_bias,
            )
        ]
        small = jnp.concatenate(rows, axis=0)
        small = jnp.pad(small, ((0, 16 - small.shape[0]), (0, 0)))
        small = jnp.pad(small, ((0, 0), (0, max(0, 128 - small.shape[1]))))
        cols = qkv_weight.shape[2]
        block_qkv = qkv_weight.transpose(1, 0, 2).reshape(qkv_weight.shape[1], -1)
        (
            x,
            grad_y,
            h1,
            qkvs,
            attended,
            log_sums,
            branch,
            middle,
            h2,
            acts,
            slopes,
            ffn_out,
            out_rows,
            w_qkv,
            w_out,
            w_up,
            w_down,
            count,
            vec,
        ) = forward_all(
            n_dp,
            n_mp,
            tokens,
            out_grad,
            seg_ids,
            [small, block_qkv, out_weight, up_weight, down_weight],
        )
        x = x.astype(F32)
        grad_y = grad_y.astype(F32)
        gains = vec[0:4]
        unit0, inv0 = stats(x)
        unit1, inv1 = stats(branch)
        unit2, inv2 = stats(middle)
        unit3, inv3 = stats(ffn_out)
        layer_out = jnp.stack(from_rows(out_rows))

        grad_f, dgain3, dshift3 = norm_back(unit3, inv3, gains[3], grad_y)
        grad_f = grad_f.astype(BF)
        dbranch1 = jnp.sum(grad_f.astype(F32), axis=0)
        grad_f_all = share(grad_f)
        dw_down = []
        dw_up = []
        dup = []
        partial = None
        for i in range(2):
            dw_down.append(dot_tn(acts[i], grad_f_all))
            grad_pre = (dot_nt(grad_f_all, w_down[i]) * slopes[i].astype(F32)).astype(BF)
            dup.append(jnp.sum(grad_pre.astype(F32), axis=0))
            dw_up.append(dot_tn(h2, grad_pre))
            term = dot_nt(grad_pre, w_up[i])
            partial = term if partial is None else partial + term
        down_grad = scatter(dw_down)
        up_grad = scatter(dw_up)
        grad_h2 = reduce_half(partial)
        back2, dgain2, dshift2 = norm_back(unit2, inv2, gains[2], grad_h2)
        grad_mid = grad_y + back2
        grad_a, dgain1, dshift1 = norm_back(unit1, inv1, gains[1], grad_mid)
        grad_a = grad_a.astype(BF)
        dbranch0 = jnp.sum(grad_a.astype(F32), axis=0)
        grad_a_all = share(grad_a)
        dw_out = []
        dw_qkv = []
        dqv = []
        partial = None
        for i in range(2):
            dw_out.append(dot_tn(attended[i], grad_a_all))
            grad_o = dot_nt(grad_a_all, w_out[i]).astype(BF)
            grad_qkv = attend_backward(qkvs[i], grad_o, log_sums[i], count)
            sums = jnp.sum(grad_qkv.astype(F32), axis=0)
            dqv.append(jnp.stack([sums[:cols], sums[2 * cols :]]))
            dw_qkv.append(dot_tn(h1, grad_qkv))
            term = dot_nt(grad_qkv, w_qkv[i])
            partial = term if partial is None else partial + term
        out_grad_w = scatter(dw_out)
        qkv_grad = scatter(dw_qkv)
        grad_h1 = reduce_half(partial)
        back0, dgain0, dshift0 = norm_back(unit0, inv0, gains[0], grad_h1)
        input_grad = jnp.stack(from_rows((grad_mid + back0).astype(BF))).astype(F32)
        qkv_grad = qkv_grad.reshape(qkv_weight.shape[1], 3, cols).transpose(1, 0, 2)

        n_ff = up_bias.shape[0] * n_dp * n_mp
        placed_up = lax.dynamic_update_slice(
            jnp.zeros((n_ff,), F32), jnp.concatenate(dup), (core * (n_ff // 2),)
        )
        placed_qv = lax.dynamic_update_slice(
            jnp.zeros((2, width), F32), jnp.concatenate(dqv, axis=1), (0, core * (width // 2))
        )
        vectors = jnp.concatenate(
            [
                jnp.stack(
                    [
                        dgain0,
                        dgain1,
                        dgain2,
                        dgain3,
                        dshift0,
                        dshift1,
                        dshift2,
                        dshift3,
                        dbranch0,
                        dbranch1,
                    ]
                ),
                placed_qv,
                placed_up.reshape(-1, width),
            ]
        )
        vectors = lax.psum(vectors, both)
        mine = lax.dynamic_slice_in_dim(vectors[:10], dp * slim, slim, 1)
        where_qv = (z * n_dp + dp) * per_qv
        qv_grad = lax.dynamic_slice_in_dim(vectors[10:12], where_qv, per_qv, 1)
        up_bias_grad = lax.dynamic_slice_in_dim(
            vectors[12:].reshape(-1), (z * n_dp + dp) * up_bias.shape[0], up_bias.shape[0], 0
        )
        return (
            layer_out,
            input_grad,
            qkv_grad,
            qv_grad,
            out_grad_w,
            up_grad,
            up_bias_grad,
            down_grad,
            mine[0:4],
            mine[4:8],
            mine[8:10],
        )

    return on_device


def solution(mesh):
    n_dp, n_mp = mesh.shape["dp"], mesh.shape["mp"]
    in_specs = (
        P(None, ("dp", "mp"), None),
        P(None, "dp"),
        P(None, "dp", "mp"),
        P(None, ("mp", "dp")),
        P(("mp", "dp"), None),
        P("dp", "mp"),
        P(("mp", "dp")),
        P(("mp", "dp"), None),
        P(None, "dp"),
        P(None, "dp"),
        P(None, "dp"),
        P(None, ("dp", "mp"), None),
    )
    out_specs = (
        P(None, ("dp", "mp"), None),
        P(None, ("dp", "mp"), None),
        P(None, "dp", "mp"),
        P(None, ("mp", "dp")),
        P(("mp", "dp"), None),
        P("dp", "mp"),
        P(("mp", "dp")),
        P(("mp", "dp"), None),
        P(None, "dp"),
        P(None, "dp"),
        P(None, "dp"),
    )
    return jax.shard_map(
        build(n_dp, n_mp), mesh=mesh, in_specs=in_specs, out_specs=out_specs, check_vma=False
    )
```

```python
import functools
import math

import jax
import jax.numpy as jnp
from jax import lax
from jax.experimental import pallas as pl
from jax.experimental.pallas import tpu as pltpu
from jax.sharding import PartitionSpec as P

HEAD_DIM = 64
CAPTION = 64
ALPHA = 32.0
EPS = 1e-05
SCALE = 1.0 / (ALPHA * math.sqrt(HEAD_DIM))
NEG = -1e30
BF = jnp.bfloat16
F32 = jnp.float32


def stats(value):
    mean = jnp.mean(value, axis=-1, keepdims=True)
    centred = value - mean
    inverse = lax.rsqrt(jnp.mean(centred * centred, axis=-1, keepdims=True) + EPS)
    return centred * inverse, inverse


def norm_back(unit, inverse, gain, grad):
    scaled = grad * gain
    grad_in = inverse * (
        scaled
        - jnp.mean(scaled, axis=-1, keepdims=True)
        - unit * jnp.mean(scaled * unit, axis=-1, keepdims=True)
    )
    return grad_in, jnp.sum(grad * unit, axis=0), jnp.sum(grad, axis=0)


def gelu_both(value):
    cdf = 0.5 * (1.0 + lax.erf(value * (1.0 / math.sqrt(2.0))))
    pdf = jnp.exp(-0.5 * value * value) * (1.0 / math.sqrt(2.0 * math.pi))
    return (value * cdf).astype(BF), (cdf + value * pdf).astype(BF)


def dot_nt(a, b):
    return lax.dot_general(a, b, (((1,), (1,)), ((), ())), preferred_element_type=F32)


def dot_tn(a, b):
    return lax.dot_general(a, b, (((0,), (0,)), ((), ())), preferred_element_type=F32)


def dot_nn(a, b):
    return lax.dot_general(a, b, (((1,), (0,)), ((), ())), preferred_element_type=F32)


def row_blocks(length):
    body = length - CAPTION
    cuts = list(range(0, body, 256)) + [body, length]
    return list(zip(cuts[:-1], cuts[1:]))


def masks(start, stop, length, count):
    rows = stop - start
    query = lax.broadcasted_iota(jnp.int32, (rows, 1), 0)
    own = query >= lax.broadcasted_iota(jnp.int32, (1, rows), 1)
    if stop < length:
        return own, None
    real = query + start < count
    same = real == (lax.broadcasted_iota(jnp.int32, (1, rows), 1) + start < count)
    before = real == (lax.broadcasted_iota(jnp.int32, (1, start), 1) < count)
    return jnp.logical_and(own, same), before


MESH = pl.DeviceIdType.MESH


def plan_hops(groups, which):
    bits = [1 << b for b in range(groups.bit_length() - 1)]
    if len(bits) == 2 and which:
        bits = bits[::-1]
    known = [0]
    steps = []
    for bit in bits:
        steps.append((bit, list(known)))
        known = known + [rel ^ bit for rel in known]
    return steps


class Links:
    def __init__(self, n_dp, n_mp, send_sems):
        self.n_dp, self.n_mp = n_dp, n_mp
        self.dp = lax.axis_index("dp")
        self.z = lax.axis_index("mp")
        self.core = lax.rem(self.dp, 2)
        self.group = self.dp // 2
        self.send_sems = send_sems
        self.used = 0
        self.open = []

    def barrier(self):
        sem = pltpu.get_barrier_semaphore()
        count = 0
        for cc in range(2):
            for zz in range(self.n_mp):

                @pl.when(jnp.logical_or(cc != self.core, zz != self.z))
                def _(cc=cc, zz=zz):
                    pl.semaphore_signal(
                        sem, inc=1, device_id=(2 * self.group + cc, zz), device_id_type=MESH
                    )

                count += 1
        bit = 1
        while bit < self.n_dp // 2:
            pl.semaphore_signal(
                sem, inc=1, device_id=(self.dp ^ (2 * bit), self.z), device_id_type=MESH
            )
            count += 1
            bit *= 2
        pl.semaphore_wait(sem, count - 1)

    def send(self, src, dst, recv_sem, dp, z):
        copy = pltpu.make_async_remote_copy(
            src_ref=src,
            dst_ref=dst,
            send_sem=self.send_sems.at[self.used],
            recv_sem=recv_sem,
            device_id=(dp, z),
            device_id_type=MESH,
        )
        copy.start()
        self.used += 1
        self.open.append((None, copy))
        return copy

    def wait_sent(self, copy):
        copy.wait_send()
        self.open = [entry for entry in self.open if entry[1] is not copy]

    def send_or_keep(self, src, dst, recv_sem, dp, z):
        own = jnp.logical_and(dp == self.dp, z == self.z)
        copy = pltpu.make_async_remote_copy(
            src_ref=src,
            dst_ref=dst,
            send_sem=self.send_sems.at[self.used],
            recv_sem=recv_sem,
            device_id=(dp, z),
            device_id_type=MESH,
        )
        here = pltpu.make_async_copy(src, dst, recv_sem)

        @pl.when(jnp.logical_not(own))
        def _():
            copy.start()

        @pl.when(own)
        def _():
            here.start()

        self.used += 1
        self.open.append((own, copy))

    def send_if(self, condition, src, dst, recv_sem, dp, z):
        copy = pltpu.make_async_remote_copy(
            src_ref=src,
            dst_ref=dst,
            send_sem=self.send_sems.at[self.used],
            recv_sem=recv_sem,
            device_id=(dp, z),
            device_id_type=MESH,
        )

        @pl.when(condition)
        def _():
            copy.start()

        self.used += 1
        self.open.append((jnp.logical_not(condition), copy))

    def arrived(self, src, dst, recv_sem):
        pltpu.make_async_remote_copy(
            src_ref=src,
            dst_ref=dst,
            send_sem=self.send_sems.at[0],
            recv_sem=recv_sem,
            device_id=(self.dp ^ 1, self.z),
            device_id_type=MESH,
        ).wait_recv()

    def finish(self):
        for own, copy in self.open:
            if own is None:
                copy.wait_send()
            else:

                @pl.when(jnp.logical_not(own))
                def _(copy=copy):
                    copy.wait_send()

        self.open = []


def rows_at(index, rows):
    return pl.ds(pl.multiple_of(index * rows, rows), rows)


def exchange_tokens(links, src, dst, sems):
    quarter = src.shape[1]
    for m in range(2):
        links.send_or_keep(
            src.at[m],
            dst.at[rows_at(lax.rem(links.z, 2), quarter), :],
            sems.at[lax.rem(links.z, 2)],
            2 * links.group + links.z // 2,
            2 * m + links.core,
        )


def exchange_tokens_wait(links, src, dst, sems):
    quarter = src.shape[1]
    for s in range(2):
        links.arrived(src.at[0], dst.at[pl.ds(s * quarter, quarter), :], sems.at[s])


class Column:
    def __init__(self, links, src, dst, col_sems, hop_sems):
        self.links, self.src, self.dst = links, src, dst
        self.rows = src.shape[0]
        self.col_sems, self.hop_sems = col_sems, hop_sems
        self.groups = links.n_dp // 2
        self.waited = [set(), set()]

    def start(self):
        k = self.links
        i = lax.rem(k.z, 2)
        home = k.z // 2
        step = 1 - 2 * home
        dst = self.dst.at[i, rows_at(k.dp, self.rows), :]
        sem = self.col_sems.at[i, k.core]
        owner = 2 * k.group + home
        k.send(self.src, dst, sem, owner, k.z + step)
        k.send_if(jnp.logical_or(k.z == 1, k.z == 2), self.src, dst, sem, owner, k.z - step)
        k.send_or_keep(self.src, dst, sem, owner, k.z)

    def piece(self, i, group):
        return self.dst.at[i, rows_at(group, 2 * self.rows), :]

    def hop(self, i, rel, bit):
        k = self.links
        piece = self.piece(i, k.group ^ rel)
        k.send(piece, piece, self.hop_sems.at[i, rel ^ bit], k.dp ^ (2 * bit), k.z)

    def hop_wait(self, i, rel):
        if rel not in self.waited[i]:
            piece = self.piece(i, self.links.group ^ rel)
            self.links.arrived(piece, piece, self.hop_sems.at[i, rel])
            self.waited[i].add(rel)

    def first(self):
        k = self.links
        for i in range(2):
            for c in range(2):
                block = self.dst.at[i, rows_at(2 * k.group + c, self.rows), :]
                k.arrived(self.src, block, self.col_sems.at[i, c])
            up = jnp.logical_and(k.core == 0, jnp.logical_and(k.z > i, k.z < k.n_mp - 1))
            down = jnp.logical_and(k.core == 1, jnp.logical_and(k.z < 2 + i, k.z > 0))
            onward = jnp.logical_or(up, down)
            for c in range(2):
                block = self.dst.at[i, rows_at(2 * k.group + c, self.rows), :]
                k.send_if(
                    onward, block, block, self.col_sems.at[i, c], k.dp, k.z + 1 - 2 * k.core
                )
            for bit, _ in plan_hops(self.groups, i):
                self.hop(i, 0, bit)

    def second(self):
        steps = [plan_hops(self.groups, i) for i in range(2)]
        for level in range(1, len(steps[0])):
            for i in range(2):
                bit, known = steps[i][level]
                for rel in known[1:]:
                    self.hop_wait(i, rel)
                    self.hop(i, rel, bit)

    def last(self):
        for i in range(2):
            for rel in range(1, self.groups):
                self.hop_wait(i, rel)


def sends_of_column(n_mp, hops):
    return 3 + 4 + 2 * hops


def forward_kernel(n_dp, n_mp, *refs):
    (tokens, grads, seg_ref) = refs[0:3]
    blocks = refs[3:8]
    (x_out, g_out, h1_out, qkv_out, o_out, lse_out, a_out, mid_out, h2_out) = refs[8:17]
    (act_out, slope_out, f_out, y_out) = refs[17:21]
    w_outs = refs[21:25]
    count_out, vec_ref = refs[25:27]
    weights = refs[27:32]
    (xb, seg_other, h1, qkv, o, lse, a_send, a_recv, a_own, mid) = refs[32:42]
    (h2, act, slope, f_send, f_recv, f_own, y, bias_ref, upb_ref) = refs[42:51]
    (send_sems, col_sems, hop_sems, tok_sems, swap_sems, keep_sems) = refs[51:57]
    smalls, w_qkv, w_out, w_up, w_down = weights
    links = Links(n_dp, n_mp, send_sems)
    half = xb.shape[0]
    length = 2 * half
    tile = half // 2
    other = links.dp + 1 - 2 * links.core
    mine0 = links.core * half
    other0 = (1 - links.core) * half
    kept = []

    def keep(src, dst):
        copy = pltpu.make_async_copy(src, dst, keep_sems.at[len(kept)])
        copy.start()
        kept.append(copy)

    def at(start, rows):
        return pl.ds(pl.multiple_of(start, 16), rows)

    links.barrier()
    ways = [Column(links, blocks[a], weights[a], col_sems.at[a], hop_sems.at[a]) for a in range(5)]
    v_way, q_way, o_way, u_way, d_way = ways
    v_way.start()
    q_way.start()
    o_way.start()
    links.send(seg_ref, seg_other, swap_sems.at[0], other, links.z)
    v_way.first()
    u_way.start()
    q_way.first()
    exchange_tokens(links, tokens, xb, tok_sems.at[0])
    v_way.second()
    o_way.first()
    q_way.second()
    d_way.start()
    u_way.first()
    o_way.second()
    links.arrived(seg_ref, seg_other, swap_sems.at[0])
    pick = lax.rem(links.core + links.z, 2) == 0
    seg_row = jnp.where(
        pick, seg_ref[pl.ds(links.z // 2, 1), :], seg_other[pl.ds(links.z // 2, 1), :]
    )
    count = jnp.sum((seg_row == 0).astype(jnp.int32), axis=1, keepdims=True)
    count_out[...] = jnp.broadcast_to(count, count_out.shape)
    v_way.last()
    spread_smalls(n_dp, smalls, vec_ref, bias_ref, upb_ref)
    exchange_tokens_wait(links, tokens, xb, tok_sems.at[0])
    keep(xb, x_out)

    def first_norm(t, _):
        rows = at(t * tile, tile)
        unit, _ = stats(xb[rows, :].astype(F32))
        h1[at(mine0 + t * tile, tile), :] = (unit * vec_ref[0:1, :] + vec_ref[4:5, :]).astype(BF)
        return 0

    lax.fori_loop(0, 2, first_norm, 0)
    links.send(h1.at[at(mine0, half), :], h1.at[at(mine0, half), :], swap_sems.at[1], other, links.z)
    q_way.last()
    cols = qkv.shape[2] // 3
    scale_row = jnp.where(
        lax.broadcasted_iota(jnp.int32, (1, 3 * cols), 1) < cols, SCALE, 1.0
    ).astype(F32)

    def project(start):
        def body(t, _):
            rows = at(start + t * tile, tile)
            for i in range(2):
                value = dot_nn(h1[rows, :], w_qkv[i]) + bias_ref[i : i + 1, :]
                qkv[i, rows, :] = (value * scale_row).astype(BF)
            return 0

        lax.fori_loop(0, 2, body, 0)

    project(mine0)
    links.arrived(
        h1.at[at(mine0, half), :], h1.at[at(other0, half), :], swap_sems.at[1]
    )
    project(other0)
    keep(h1, h1_out)
    keep(qkv, qkv_out)
    u_way.second()
    d_way.first()
    exchange_tokens(links, grads, g_out, tok_sems.at[1])
    pairs = cols // 128

    def attend(i):
        def body(j, _):
            attend_pair_fwd(
                qkv.at[i, :, pl.ds(pl.multiple_of(j * 128, 128), 128)],
                qkv.at[i, :, pl.ds(pl.multiple_of((pairs + j) * 128, 128), 128)],
                qkv.at[i, :, pl.ds(pl.multiple_of((2 * pairs + j) * 128, 128), 128)],
                count,
                o.at[i, :, pl.ds(pl.multiple_of(j * 128, 128), 128)],
                lse,
                2 * (i * pairs + j),
            )
            return 0

        lax.fori_loop(0, pairs, body, 0)

    lse[...] = jnp.zeros_like(lse)
    attend(0)
    attend(1)
    d_way.second()
    keep(o, o_out)
    keep(lse, lse_out)
    o_way.last()

    def out_tile(start):
        return dot_nn(o[0, at(start, tile), :], w_out[0]) + dot_nn(
            o[1, at(start, tile), :], w_out[1]
        )

    def out_theirs(t, _):
        a_send[at(t * tile, tile), :] = out_tile(other0 + t * tile).astype(BF)
        return 0

    def out_ours(t, _):
        a_own[at(t * tile, tile), :] = out_tile(mine0 + t * tile)
        return 0

    lax.fori_loop(0, 2, out_theirs, 0)
    links.send(a_send, a_recv, swap_sems.at[2], other, links.z)
    lax.fori_loop(0, 2, out_ours, 0)
    links.arrived(a_send, a_recv, swap_sems.at[2])

    def middle_norms(t, _):
        rows = at(t * tile, tile)
        branch = a_own[rows, :] + a_recv[rows, :].astype(F32) + vec_ref[8:9, :]
        a_own[rows, :] = branch
        unit, _ = stats(branch)
        middle = xb[rows, :].astype(F32) + unit * vec_ref[1:2, :] + vec_ref[5:6, :]
        mid[rows, :] = middle
        unit, _ = stats(middle)
        h2[at(mine0 + t * tile, tile), :] = (unit * vec_ref[2:3, :] + vec_ref[6:7, :]).astype(BF)
        return 0

    lax.fori_loop(0, 2, middle_norms, 0)
    links.send(h2.at[at(mine0, half), :], h2.at[at(mine0, half), :], swap_sems.at[3], other, links.z)
    keep(a_own, a_out)
    keep(mid, mid_out)
    u_way.last()

    def up(start):
        def body(t, _):
            rows = at(start + t * tile, tile)
            for i in range(2):
                value, slant = gelu_both(dot_nn(h2[rows, :], w_up[i]) + upb_ref[i : i + 1, :])
                act[i, rows, :] = value
                slope[i, rows, :] = slant
            return 0

        lax.fori_loop(0, 2, body, 0)

    up(mine0)
    links.arrived(h2.at[at(mine0, half), :], h2.at[at(other0, half), :], swap_sems.at[3])
    up(other0)
    keep(h2, h2_out)
    keep(act, act_out)
    keep(slope, slope_out)
    d_way.last()

    def down_tile(start):
        return dot_nn(act[0, at(start, tile), :], w_down[0]) + dot_nn(
            act[1, at(start, tile), :], w_down[1]
        )

    def down_theirs(t, _):
        f_send[at(t * tile, tile), :] = down_tile(other0 + t * tile).astype(BF)
        return 0

    def down_ours(t, _):
        f_own[at(t * tile, tile), :] = down_tile(mine0 + t * tile)
        return 0

    lax.fori_loop(0, 2, down_theirs, 0)
    links.send(f_send, f_recv, swap_sems.at[4], other, links.z)
    lax.fori_loop(0, 2, down_ours, 0)
    for weight, w_hbm in zip(weights[1:], w_outs):
        keep(weight, w_hbm)
    links.arrived(f_send, f_recv, swap_sems.at[4])

    def last_norm(t, _):
        rows = at(t * tile, tile)
        value = f_own[rows, :] + f_recv[rows, :].astype(F32) + vec_ref[9:10, :]
        f_own[rows, :] = value
        unit, _ = stats(value)
        y[rows, :] = (mid[rows, :] + unit * vec_ref[3:4, :] + vec_ref[7:8, :]).astype(BF)
        return 0

    lax.fori_loop(0, 2, last_norm, 0)
    keep(f_own, f_out)
    keep(y, y_out)
    exchange_tokens_wait(links, grads, g_out, tok_sems.at[1])
    for copy in kept:
        copy.wait()
    links.finish()


def spread_smalls(n_dp, smalls, vec_ref, bias_ref, upb_ref):
    width = vec_ref.shape[1]
    slim = width // n_dp
    per_qv = bias_ref.shape[1] // 3 // n_dp
    per_up = upb_ref.shape[1] // n_dp
    row = [
        [smalls[i, 16 * dp : 16 * dp + 16, :].astype(F32) for dp in range(n_dp)] for i in range(2)
    ]
    wide = jnp.concatenate([row[0][dp][2:12, 0:slim] for dp in range(n_dp)], axis=1)
    vec_ref[0:10, :] = wide
    vec_ref[10:16, :] = jnp.zeros((6, width), F32)
    for i in range(2):
        queries = [row[i][dp][0:1, 0:per_qv] for dp in range(n_dp)]
        values = [row[i][dp][0:1, per_qv : 2 * per_qv] for dp in range(n_dp)]
        zeros = [jnp.zeros((1, n_dp * per_qv), F32)]
        bias_ref[i : i + 1, :] = jnp.concatenate(queries + zeros + values, axis=1)
        upb_ref[i : i + 1, :] = jnp.concatenate(
            [row[i][dp][1:2, 0:per_up] for dp in range(n_dp)], axis=1
        )


def attend_pair_fwd(q_ref, k_ref, v_ref, count, o_ref, lse_ref, head0):
    length = q_ref.shape[0]
    lane = lax.broadcasted_iota(jnp.int32, (1, 128), 1)
    for start, stop in row_blocks(length):
        own, before = masks(start, stop, length, count)
        outs = []
        lses = []
        for head in range(2):
            q = jnp.where((lane >= 64) == (head == 1), q_ref[start:stop, :], jnp.zeros((), BF))
            s2 = jnp.where(own, dot_nt(q, k_ref[start:stop, :]), NEG)
            top = jnp.max(s2, axis=-1, keepdims=True)
            if start:
                s1 = dot_nt(q, k_ref[0:start, :])
                if before is not None:
                    s1 = jnp.where(before, s1, NEG)
                top = jnp.maximum(top, jnp.max(s1, axis=-1, keepdims=True))
            e2 = jnp.exp(ALPHA * (s2 - top))
            total = jnp.sum(e2, axis=-1, keepdims=True)
            acc = dot_nn(e2.astype(BF), v_ref[start:stop, :])
            if start:
                e1 = jnp.exp(ALPHA * (s1 - top))
                total = total + jnp.sum(e1, axis=-1, keepdims=True)
                acc = acc + dot_nn(e1.astype(BF), v_ref[0:start, :])
            outs.append(acc / total)
            lses.append(ALPHA * top + jnp.log(total))
        o_ref[start:stop, :] = jnp.where(lane < 64, outs[0], outs[1]).astype(BF)
        kept = jnp.where(lane == head0, lses[0], lse_ref[start:stop, :])
        lse_ref[start:stop, :] = jnp.where(lane == head0 + 1, lses[1], kept)


def forward_all(n_dp, n_mp, tokens, grads, seg_ids, blocks):
    groups = n_dp // 2
    hops = groups - 1
    any_spec = pl.BlockSpec(memory_space=pl.ANY)
    vmem = pl.BlockSpec(memory_space=pltpu.VMEM)
    width = tokens.shape[2]
    half = 2 * tokens.shape[1]
    length = 2 * half
    cols3 = blocks[1].shape[1]
    cols = cols3 // 3
    ff = n_dp * blocks[4].shape[0]
    shape = jax.ShapeDtypeStruct
    full = [(2, n_dp * b.shape[0], b.shape[1]) for b in blocks]
    out_shape = [
        shape((half, width), BF),
        shape((half, width), BF),
        shape((length, width), BF),
        shape((2, length, cols3), BF),
        shape((2, length, cols), BF),
        shape((length, 128), F32),
        shape((half, width), F32),
        shape((half, width), F32),
        shape((length, width), BF),
        shape((2, length, ff), BF),
        shape((2, length, ff), BF),
        shape((half, width), F32),
        shape((half, width), BF),
    ] + [shape(f, BF) for f in full[1:]] + [shape((8, 128), jnp.int32), shape((16, width), F32)]
    return pl.pallas_call(
        functools.partial(forward_kernel, n_dp, n_mp),
        in_specs=[any_spec] * 2 + [vmem] + [any_spec] * 5,
        out_specs=[any_spec] * 17 + [vmem] * 2,
        out_shape=out_shape,
        scratch_shapes=[pltpu.VMEM(f, BF) for f in full]
        + [
            pltpu.VMEM((half, width), BF),
            pltpu.VMEM(seg_ids.shape, jnp.int32),
            pltpu.VMEM((length, width), BF),
            pltpu.VMEM((2, length, cols3), BF),
            pltpu.VMEM((2, length, cols), BF),
            pltpu.VMEM((length, 128), F32),
            pltpu.VMEM((half, width), BF),
            pltpu.VMEM((half, width), BF),
            pltpu.VMEM((half, width), F32),
            pltpu.VMEM((half, width), F32),
            pltpu.VMEM((length, width), BF),
            pltpu.VMEM((2, length, ff), BF),
            pltpu.VMEM((2, length, ff), BF),
            pltpu.VMEM((half, width), BF),
            pltpu.VMEM((half, width), BF),
            pltpu.VMEM((half, width), F32),
            pltpu.VMEM((half, width), BF),
            pltpu.VMEM((2, cols3), F32),
            pltpu.VMEM((2, ff), F32),
            pltpu.SemaphoreType.DMA((9 + 5 * sends_of_column(n_mp, hops),)),
            pltpu.SemaphoreType.DMA((5, 2, 2)),
            pltpu.SemaphoreType.DMA((5, 2, groups)),
            pltpu.SemaphoreType.DMA((2, 2)),
            pltpu.SemaphoreType.DMA((5,)),
            pltpu.SemaphoreType.DMA((17,)),
        ],
        compiler_params=pltpu.CompilerParams(
            collective_id=0, has_side_effects=True, vmem_limit_bytes=60 << 20
        ),
    )(tokens, grads, seg_ids, *blocks)


def attend_pair_bwd(q_ref, k_ref, v_ref, do_ref, lse_ref, head0, count, dk_ref, dv_ref):
    length = q_ref.shape[0]
    lane = lax.broadcasted_iota(jnp.int32, (1, 128), 1)
    dk_ref[...] = jnp.zeros_like(dk_ref)
    dv_ref[...] = jnp.zeros_like(dv_ref)
    zero = jnp.zeros((), BF)
    for start, stop in row_blocks(length):
        own, before = masks(start, stop, length, count)
        dqs = []
        for head in range(2):
            mine = (lane >= 64) == (head == 1)
            q = jnp.where(mine, q_ref[start:stop, :], zero)
            do = jnp.where(mine, do_ref[start:stop, :], zero)
            lse = jnp.sum(
                jnp.where(lane == head0 + head, lse_ref[start:stop, :], 0.0), axis=-1, keepdims=True
            )
            p2 = jnp.where(own, jnp.exp(ALPHA * dot_nt(q, k_ref[start:stop, :]) - lse), 0.0)
            g2 = dot_nt(do, v_ref[start:stop, :])
            delta = jnp.sum(p2 * g2, axis=-1, keepdims=True)
            if start:
                p1 = jnp.exp(ALPHA * dot_nt(q, k_ref[0:start, :]) - lse)
                if before is not None:
                    p1 = jnp.where(before, p1, 0.0)
                g1 = dot_nt(do, v_ref[0:start, :])
                delta = delta + jnp.sum(p1 * g1, axis=-1, keepdims=True)
            ds2 = (ALPHA * p2 * (g2 - delta)).astype(BF)
            dq = dot_nn(ds2, k_ref[start:stop, :])
            dk_ref[start:stop, :] += dot_tn(ds2, q)
            dv_ref[start:stop, :] += dot_tn(p2.astype(BF), do)
            if start:
                ds1 = (ALPHA * p1 * (g1 - delta)).astype(BF)
                dq = dq + dot_nn(ds1, k_ref[0:start, :])
                dk_ref[0:start, :] += dot_tn(ds1, q)
                dv_ref[0:start, :] += dot_tn(p1.astype(BF), do)
            dqs.append(dq)
        q_ref[start:stop, :] = (jnp.where(lane < 64, dqs[0], dqs[1]) * SCALE).astype(BF)
    k_ref[...] = dk_ref[...].astype(BF)
    v_ref[...] = dv_ref[...].astype(BF)


FAR = (1, 3, 4)


class Reduce:
    def __init__(self, links, part, slots, column, slot_sems, column_sems, load):
        self.load, self.near, self.copies = load, [], []
        self.links, self.part, self.slots, self.column = links, part, slots, column
        self.slot_sems, self.column_sems = slot_sems, column_sems
        self.groups = links.n_dp // 2
        self.rows = part.shape[1] // links.n_dp
        self.steps = [plan_hops(self.groups, i)[::-1] for i in range(2)]

    def piece(self, i, rel):
        return self.part.at[i, rows_at(self.links.group ^ rel, 2 * self.rows), :]

    def slot(self, i, rel):
        return self.slots.at[i, pl.ds((rel - 1) * 2 * self.rows, 2 * self.rows), :]

    def give(self, i, rel, bit):
        k = self.links
        k.send(self.piece(i, rel), self.slot(i, rel), self.slot_sems.at[i, rel], k.dp ^ (2 * bit), k.z)

    def start(self, i):
        bit, known = self.steps[i][0]
        for rel in known[::-1]:
            self.give(i, rel ^ bit, bit)

    def add(self, i, rel, slot):
        tile = min(32, 2 * self.rows)
        base = (self.links.group ^ rel) * 2 * self.rows

        def body(t, _):
            rows = pl.ds(pl.multiple_of(base + t * tile, tile), tile)
            came = self.slots[i, pl.ds(pl.multiple_of((slot - 1) * 2 * self.rows + t * tile, tile), tile), :]
            total = self.part[i, rows, :].astype(F32) + came.astype(F32)
            self.part[i, rows, :] = total.astype(self.part.dtype)
            return 0

        lax.fori_loop(0, 2 * self.rows // tile, body, 0)

    def level(self, i, number):
        k = self.links
        bit, known = self.steps[i][number]
        after = self.steps[i][number + 1][0] if number + 1 < len(self.steps[i]) else 0
        for rel in sorted(known, key=lambda r: not r & after):
            k.arrived(self.piece(i, rel), self.slot(i, rel ^ bit), self.slot_sems.at[i, rel ^ bit])
            self.add(i, rel, rel ^ bit)
            if rel & after:
                self.give(i, rel, after)
        if not after:
            for c in range(2):
                k.send_or_keep(
                    self.part.at[i, rows_at(2 * k.group + c, self.rows), :],
                    self.column.at[k.z],
                    self.column_sems.at[k.z],
                    2 * k.group + c,
                    2 * k.core + i,
                )

    def levels(self, number):
        for i in range(2):
            self.level(i, number)

    def collect(self):
        if self.near:
            return
        for zz in range(self.links.n_mp):
            term = self.column.at[zz]
            self.links.arrived(term, term, self.column_sems.at[zz])
            if self.load:
                near = self.slots.at[0, pl.ds(zz * self.rows, self.rows), :]
                self.copies.append(self.load(term, near))
                term = near
            self.near.append(term)

    def total(self, out):
        self.collect()
        for copy in self.copies:
            copy.wait()
        tile = min(32, self.rows)

        def body(t, _):
            rows = pl.ds(pl.multiple_of(t * tile, tile), tile)
            value = self.near[0][rows, :].astype(F32)
            for ref in self.near[1:]:
                value = value + ref[rows, :].astype(F32)
            out[rows, :] = value
            return 0

        lax.fori_loop(0, self.rows // tile, body, 0)


def return_tokens(links, parts, dst, sems):
    quarter = dst.shape[1]
    m = links.z // 2
    for s in range(2):
        links.send_or_keep(
            parts.at[pl.ds(s * quarter, quarter), :],
            dst.at[m],
            sems.at[m],
            2 * links.group + lax.rem(links.z, 2),
            2 * links.core + s,
        )


def return_tokens_wait(links, dst, sems):
    for m in range(2):
        links.arrived(dst.at[m], dst.at[m], sems.at[m])


def backward_kernel(n_dp, n_mp, *refs):
    (y_hbm, g_hbm, x_hbm, a_hbm, mid_hbm, f_hbm, h1_hbm, qkv_hbm, o_hbm, lse_hbm) = refs[0:10]
    (h2_hbm, act_hbm, slope_hbm, wq_hbm, wo_hbm, wu_hbm, wd_hbm, vec_ref, count_ref) = refs[10:19]
    (layer_out, grad_out, q_out, o_out, u_out, d_out, v_out, back) = refs[19:27]
    fars = refs[27:30]
    refs = refs[:27] + refs[30:]
    parts = refs[27:32]
    slots = refs[32:37]
    columns = list(refs[37:42])
    for a, far in zip(FAR, fars):
        columns[a] = far
    (pair, take, own, own2, g_buf) = refs[42:47]
    refs = refs[:47] + (None,) + refs[47:]
    (act, du, h, wd, wu, lse, dk, dv, vsum, vtake, vqkv, vup) = refs[48:60]
    (send_sems, slot_sems, column_sems, tok_sems, swap_sems, load_sems) = refs[60:66]
    links = Links(n_dp, n_mp, send_sems)
    half = g_buf.shape[0]
    length = 2 * half
    tile = half // 2
    width = g_buf.shape[1]
    other = links.dp + 1 - 2 * links.core
    mine0 = links.core * half
    other0 = (1 - links.core) * half
    cols3 = qkv_hbm.shape[2]
    cols = cols3 // 3
    loads = [0]
    parts = list(parts)
    give = h.at[pl.ds(0, half), :]
    parts[1] = du.at[:, pl.ds(0, width), pl.ds(cols, cols3)]
    if parts[2].dtype == BF:
        parts[2] = wu.at[:, pl.ds(half, cols), :]
    else:
        parts[2] = own2.at[:, pl.ds(0, cols), :]

    def load(src, dst):
        copy = pltpu.make_async_copy(src, dst, load_sems.at[loads[0]])
        loads[0] += 1
        copy.start()
        return copy

    def at(start, rows):
        return pl.ds(pl.multiple_of(start, 16), rows)

    def gain(k):
        return vec_ref[k : k + 1, :]

    f_load = load(f_hbm, own)
    g_load = load(g_hbm, g_buf)
    act_load = load(act_hbm, act)
    wd_load = load(wd_hbm, wd)
    slope_load = load(slope_hbm, du)
    h_load = load(h2_hbm, h)
    wu_load = load(wu_hbm, wu)
    lse_load = load(lse_hbm, lse)
    vsum[...] = jnp.zeros_like(vsum)
    vqkv[...] = jnp.zeros_like(vqkv)
    vup[...] = jnp.zeros_like(vup)
    links.barrier()
    ways = [
        Reduce(
            links,
            parts[a],
            slots[a],
            columns[a],
            slot_sems.at[a],
            column_sems.at[a],
            load if a in FAR else None,
        )
        for a in range(5)
    ]
    v_way, q_way, o_way, u_way, d_way = ways
    return_tokens(links, y_hbm, layer_out, tok_sems.at[0])

    def norm_grad(value, k, grad):
        unit, inverse = stats(value)
        back, dgain, dshift = norm_back(unit, inverse, gain(k), grad)
        vsum[k : k + 1, :] += dgain[None]
        vsum[4 + k : 5 + k, :] += dshift[None]
        return back

    f_load.wait()
    g_load.wait()

    def last_norm(t, _):
        rows = at(t * tile, tile)
        back = norm_grad(own[rows, :], 3, g_buf[rows, :].astype(F32)).astype(BF)
        vsum[9:10, :] += jnp.sum(back.astype(F32), axis=0, keepdims=True)
        pair[at(mine0 + t * tile, tile), :] = back
        return 0

    lax.fori_loop(0, 2, last_norm, 0)
    ours = pair.at[at(mine0, half), :]
    theirs = pair.at[at(other0, half), :]
    df_send = links.send(ours, ours, swap_sems.at[0], other, links.z)
    act_load.wait()
    links.arrived(ours, theirs, swap_sems.at[0])

    def weight_grad(left, right, part, i):
        step = min(256, left.shape[1])

        def body(t, _):
            lanes = pl.ds(pl.multiple_of(t * step, 128), step)
            rows = pl.ds(pl.multiple_of(t * step, 16), step)
            part[i, rows, :] = dot_tn(left[:, lanes], right[...]).astype(part.dtype)
            return 0

        lax.fori_loop(0, left.shape[1] // step, body, 0)

    for i in range(2):
        weight_grad(act.at[i], pair, parts[4], i)
        d_way.start(i)
    qkv_load = load(qkv_hbm, act.at[:, :, 0:cols3])
    wd_load.wait()
    slope_load.wait()
    h_load.wait()
    for i in range(2):

        def slant(t, _, i=i):
            rows = at(t * tile, tile)
            value = (dot_nt(pair[rows, :], wd[i]) * du[i, rows, :].astype(F32)).astype(BF)
            du[i, rows, :] = value
            vup[i : i + 1, :] += jnp.sum(value.astype(F32), axis=0, keepdims=True)
            return 0

        lax.fori_loop(0, 4, slant, 0)
        weight_grad(h, du.at[i], parts[3], i)
        u_way.start(i)
    wq_load = load(wq_hbm, wd.at[:, :, 0:cols3])
    a_load = load(a_hbm.at[pl.ds(0, tile), :], own2.at[0])
    mid_load = load(mid_hbm.at[pl.ds(0, tile), :], own2.at[1])
    wu_load.wait()

    def up_tile(start):
        return dot_nt(du[0, at(start, tile), :], wu[0]) + dot_nt(du[1, at(start, tile), :], wu[1])

    def up_theirs(t, _):
        give[at(t * tile, tile), :] = up_tile(other0 + t * tile).astype(BF)
        return 0

    def up_ours(t, _):
        own[at(t * tile, tile), :] = up_tile(mine0 + t * tile)
        return 0

    lax.fori_loop(0, 2, up_theirs, 0)
    up_send = links.send(give, take, swap_sems.at[1], other, links.z)
    lax.fori_loop(0, 2, up_ours, 0)
    o_load = load(o_hbm, du.at[:, :, 0:cols])
    x_load = load(x_hbm, wu.at[0, pl.ds(0, half), :])
    wo_load = [load(wo_hbm.at[i], wu.at[1, pl.ds(i * cols, cols), :]) for i in range(2)]
    links.wait_sent(df_send)
    links.arrived(give, take, swap_sems.at[1])
    for t in range(2):
        a_load.wait()
        mid_load.wait()
        rows = pl.ds(t * tile, tile)
        grad = own[rows, :] + take[rows, :].astype(F32)
        grad = g_buf[rows, :].astype(F32) + norm_grad(own2[1], 2, grad)
        own[rows, :] = grad
        grad = norm_grad(own2[0], 1, grad).astype(BF)
        vsum[8:9, :] += jnp.sum(grad.astype(F32), axis=0, keepdims=True)
        pair[at(mine0 + t * tile, tile), :] = grad
        if t == 0:
            a_load = load(a_hbm.at[pl.ds(tile, tile), :], own2.at[0])
            mid_load = load(mid_hbm.at[pl.ds(tile, tile), :], own2.at[1])
    links.send(ours, ours, swap_sems.at[2], other, links.z)
    links.wait_sent(up_send)
    h_load = load(h1_hbm, h)
    o_load.wait()
    qkv_load.wait()
    wo_load[0].wait()
    wo_load[1].wait()
    links.arrived(ours, theirs, swap_sems.at[2])

    def open_heads(t, _):
        rows = at(t * tile, tile)
        for i in range(2):
            value = dot_nt(pair[rows, :], wu[1, i * cols : (i + 1) * cols, :])
            act[i, rows, cols3 : cols3 + cols] = value.astype(BF)
        return 0

    lax.fori_loop(0, 4, open_heads, 0)
    for i in range(2):
        weight_grad(du.at[i, :, 0:cols], pair, parts[2], i)
        o_way.start(i)
    d_way.levels(0)
    lse_load.wait()
    h_load.wait()
    wq_load.wait()
    count = count_ref[0:1, 0:1]
    pairs = cols // 128

    for i in range(2):

        def attend(j, _, i=i):
            lanes = lambda base: pl.ds(pl.multiple_of((base + j) * 128, 128), 128)
            attend_pair_bwd(
                act.at[i, :, lanes(0)],
                act.at[i, :, lanes(pairs)],
                act.at[i, :, lanes(2 * pairs)],
                act.at[i, :, lanes(3 * pairs)],
                lse,
                2 * (i * pairs + j),
                count,
                dk,
                dv,
            )
            return 0

        lax.fori_loop(0, pairs, attend, 0)
        weight_grad(h, act.at[i, :, 0:cols3], parts[1], i)
        q_way.start(i)
        if i == 0:
            u_way.levels(0)

    def head_tile(start):
        rows = at(start, tile)
        total = None
        for i in range(2):
            value = act[i, rows, 0:cols3]
            vqkv[i : i + 1, :] += jnp.sum(value.astype(F32), axis=0, keepdims=True)
            term = dot_nt(value, wd[i, :, 0:cols3])
            total = term if total is None else total + term
        return total

    def head_theirs(t, _):
        give[at(t * tile, tile), :] = head_tile(other0 + t * tile).astype(BF)
        return 0

    lax.fori_loop(0, 2, head_theirs, 0)
    head_send = links.send(give, take, swap_sems.at[3], other, links.z)
    d_way.levels(1)
    o_way.levels(0)
    x_load.wait()
    links.arrived(give, take, swap_sems.at[3])

    def first_norm(t, _):
        rows = at(t * tile, tile)
        grad = head_tile(mine0 + t * tile) + take[rows, :].astype(F32)
        grad = own[rows, :] + norm_grad(wu[0, rows, :].astype(F32), 0, grad)
        g_buf[rows, :] = grad.astype(BF)
        return 0

    lax.fori_loop(0, 2, first_norm, 0)
    return_tokens(links, g_buf, back, tok_sems.at[1])
    links.send(vsum, vtake, swap_sems.at[4], other, links.z)
    q_way.level(0, 0)
    u_way.levels(1)
    q_way.level(1, 0)
    links.arrived(vsum, vtake, swap_sems.at[4])
    gather_smalls(n_dp, vsum[...] + vtake[...], vqkv, vup, parts[0])
    v_way.start(0)
    v_way.start(1)
    o_way.levels(1)
    v_way.levels(0)
    d_way.total(d_out)
    u_way.collect()
    q_way.levels(1)
    v_way.levels(1)
    o_way.total(o_out)
    u_way.total(u_out)
    links.wait_sent(head_send)
    return_tokens_wait(links, back, tok_sems.at[1])
    back_copies = [load(back.at[m], give.at[pl.ds(m * tile, tile), :]) for m in range(2)]
    back_copies[0].wait()
    back_copies[1].wait()

    def widen(t, _):
        rows = at(t * 32, 32)
        own[rows, :] = give[rows, :].astype(F32)
        return 0

    lax.fori_loop(0, half // 32, widen, 0)
    grad_copies = [load(own.at[pl.ds(m * tile, tile), :], grad_out.at[m]) for m in range(2)]
    v_way.total(v_out)
    q_way.total(q_out)
    return_tokens_wait(links, layer_out, tok_sems.at[0])
    grad_copies[0].wait()
    grad_copies[1].wait()
    links.finish()


def gather_smalls(n_dp, total, vqkv, vup, part):
    width = total.shape[1]
    slim = width // n_dp
    per_qv = vqkv.shape[1] // 3 // n_dp
    per_up = vup.shape[1] // n_dp
    lanes = part.shape[2]
    values = 2 * per_qv * n_dp

    def fill(value):
        short = lanes - value.shape[1]
        if not short:
            return value
        return jnp.concatenate([value, jnp.zeros((value.shape[0], short), F32)], axis=1)

    for i in range(2):
        qkv = vqkv[i : i + 1, :]
        up = vup[i : i + 1, :]
        for dp in range(n_dp):
            first = jnp.concatenate(
                [
                    qkv[:, dp * per_qv : (dp + 1) * per_qv],
                    qkv[:, values + dp * per_qv : values + (dp + 1) * per_qv],
                ],
                axis=1,
            )
            base = 16 * dp
            part[i, base : base + 1, :] = fill(first)
            part[i, base + 1 : base + 2, :] = fill(up[:, dp * per_up : (dp + 1) * per_up])
            part[i, base + 2 : base + 12, :] = fill(total[0:10, dp * slim : (dp + 1) * slim])
            part[i, base + 12 : base + 16, :] = jnp.zeros((4, lanes), F32)


def backward_all(n_dp, n_mp, saved, weights, vec, count):
    groups = n_dp // 2
    any_spec = pl.BlockSpec(memory_space=pl.ANY)
    vmem = pl.BlockSpec(memory_space=pltpu.VMEM)
    shape = jax.ShapeDtypeStruct
    half, width = saved[0].shape
    length = 2 * half
    cols3 = saved[7].shape[2]
    cols = cols3 // 3
    ff = saved[11].shape[2]
    full = [(2, n_dp * 16, 128)] + [w.shape for w in weights]
    each = [f[1] // n_dp for f in full]
    kinds = [F32] + [BF if r % 8 == 0 else F32 for r in each[1:]]
    out_shape = [shape((2, half // 2, width), BF), shape((2, half // 2, width), F32)] + [
        shape((each[a], full[a][2]), F32) for a in (1, 2, 3, 4, 0)
    ]
    out_shape += [shape((2, half // 2, width), BF)]
    out_shape += [shape((n_mp, each[a], full[a][2]), kinds[a]) for a in FAR]
    sends = 4 + 5 + 5 * (2 * (groups - 1) + 4)
    return pl.pallas_call(
        functools.partial(backward_kernel, n_dp, n_mp),
        in_specs=[any_spec] * 17 + [vmem] * 2,
        out_specs=[any_spec] * 2 + [vmem] * 5 + [any_spec] * 4,
        out_shape=out_shape,
        scratch_shapes=[
            pltpu.VMEM((1, 16, 128) if a in (1, 2) else f, k)
            for a, (f, k) in enumerate(zip(full, kinds))
        ]
        + [
            pltpu.VMEM((2, (groups - 1) * 2 * r, f[2]), k) for f, r, k in zip(full, each, kinds)
        ]
        + [
            pltpu.VMEM((n_mp, 16 if a in FAR else r, f[2]), k)
            for a, (f, r, k) in enumerate(zip(full, each, kinds))
        ]
        + [
            pltpu.VMEM((length, width), BF),
            pltpu.VMEM((half, width), BF),
            pltpu.VMEM((half, width), F32),
            pltpu.VMEM((2, half // 2, width), F32),
            pltpu.VMEM((half, width), BF),
            pltpu.VMEM((2, length, ff), BF),
            pltpu.VMEM((2, length, ff), BF),
            pltpu.VMEM((length, width), BF),
            pltpu.VMEM((2, ff, width), BF),
            pltpu.VMEM((2, width, ff), BF),
            pltpu.VMEM((length, 128), F32),
            pltpu.VMEM((length, 128), F32),
            pltpu.VMEM((length, 128), F32),
            pltpu.VMEM((16, width), F32),
            pltpu.VMEM((16, width), F32),
            pltpu.VMEM((2, cols3), F32),
            pltpu.VMEM((2, ff), F32),
            pltpu.SemaphoreType.DMA((sends,)),
            pltpu.SemaphoreType.DMA((5, 2, groups)),
            pltpu.SemaphoreType.DMA((5, n_mp)),
            pltpu.SemaphoreType.DMA((2, 2)),
            pltpu.SemaphoreType.DMA((5,)),
            pltpu.SemaphoreType.DMA((23 + len(FAR) * n_mp,)),
        ],
        compiler_params=pltpu.CompilerParams(
            collective_id=1, has_side_effects=True, vmem_limit_bytes=61 << 20
        ),
    )(*saved, *weights, vec, count)[:7]


def build(n_dp, n_mp):
    def on_device(
        tokens,
        seg_ids,
        qkv_weight,
        qv_bias,
        out_weight,
        up_weight,
        up_bias,
        down_weight,
        norm_gain,
        norm_bias,
        branch_bias,
        out_grad,
    ):
        width = tokens.shape[2]

        per_qv = qv_bias.shape[1]
        slim = width // n_dp
        rows = [
            jnp.pad(value, ((0, 0), (0, slim_up - value.shape[1])))
            for slim_up in [max(slim, 2 * per_qv, up_bias.shape[0])]
            for value in (
                qv_bias.reshape(1, -1),
                up_bias.reshape(1, -1),
                norm_gain,
                norm_bias,
                branch_bias,
            )
        ]
        small = jnp.concatenate(rows, axis=0)
        small = jnp.pad(small, ((0, 16 - small.shape[0]), (0, 0)))
        small = jnp.pad(small, ((0, 0), (0, max(0, 128 - small.shape[1]))))
        cols = qkv_weight.shape[2]
        block_qkv = qkv_weight.transpose(1, 0, 2).reshape(qkv_weight.shape[1], -1)
        (
            x,
            grad_y,
            h1,
            qkvs,
            attended,
            log_sums,
            branch,
            middle,
            h2,
            acts,
            slopes,
            ffn_out,
            out_rows,
            w_qkv,
            w_out,
            w_up,
            w_down,
            count,
            vec,
        ) = forward_all(
            n_dp,
            n_mp,
            tokens,
            out_grad,
            seg_ids,
            [small, block_qkv, out_weight, up_weight, down_weight],
        )
        saved = [
            out_rows,
            grad_y,
            x,
            branch,
            middle,
            ffn_out,
            h1,
            qkvs,
            attended,
            log_sums,
            h2,
            acts,
            slopes,
        ]
        layer_out, input_grad, qkv_grad, out_weight_grad, up_grad, down_grad, mine = backward_all(
            n_dp, n_mp, saved, [w_qkv, w_out, w_up, w_down], vec, count
        )
        return (
            layer_out,
            input_grad,
            qkv_grad.reshape(qkv_weight.shape[1], 3, cols).transpose(1, 0, 2),
            mine[0, : 2 * per_qv].reshape(2, per_qv),
            out_weight_grad,
            up_grad,
            mine[1, : up_bias.shape[0]],
            down_grad,
            mine[2:6, :slim],
            mine[6:10, :slim],
            mine[10:12, :slim],
        )

    return on_device


def solution(mesh):
    n_dp, n_mp = mesh.shape["dp"], mesh.shape["mp"]
    in_specs = (
        P(None, ("dp", "mp"), None),
        P(None, "dp"),
        P(None, "dp", "mp"),
        P(None, ("mp", "dp")),
        P(("mp", "dp"), None),
        P("dp", "mp"),
        P(("mp", "dp")),
        P(("mp", "dp"), None),
        P(None, "dp"),
        P(None, "dp"),
        P(None, "dp"),
        P(None, ("dp", "mp"), None),
    )
    out_specs = (
        P(None, ("dp", "mp"), None),
        P(None, ("dp", "mp"), None),
        P(None, "dp", "mp"),
        P(None, ("mp", "dp")),
        P(("mp", "dp"), None),
        P("dp", "mp"),
        P(("mp", "dp")),
        P(("mp", "dp"), None),
        P(None, "dp"),
        P(None, "dp"),
        P(None, "dp"),
    )
    return jax.shard_map(
        build(n_dp, n_mp), mesh=mesh, in_specs=in_specs, out_specs=out_specs, check_vma=False
    )
```

```python
import functools
import math

import jax
import jax.numpy as jnp
from jax import lax
from jax.experimental import pallas as pl
from jax.experimental.pallas import tpu as pltpu
from jax.sharding import PartitionSpec as P

HEAD_DIM = 64
CAPTION = 64
ALPHA = 32.0
EPS = 1e-05
SCALE = 1.0 / (ALPHA * math.sqrt(HEAD_DIM))
NEG = -1e30
BF = jnp.bfloat16
F32 = jnp.float32


def stats(value):
    mean = jnp.mean(value, axis=-1, keepdims=True)
    centred = value - mean
    inverse = lax.rsqrt(jnp.mean(centred * centred, axis=-1, keepdims=True) + EPS)
    return centred * inverse, inverse


def norm_back(unit, inverse, gain, grad):
    scaled = grad * gain
    grad_in = inverse * (
        scaled
        - jnp.mean(scaled, axis=-1, keepdims=True)
        - unit * jnp.mean(scaled * unit, axis=-1, keepdims=True)
    )
    return grad_in, jnp.sum(grad * unit, axis=0), jnp.sum(grad, axis=0)


def gelu_both(value):
    cdf = 0.5 * (1.0 + lax.erf(value * (1.0 / math.sqrt(2.0))))
    pdf = jnp.exp(-0.5 * value * value) * (1.0 / math.sqrt(2.0 * math.pi))
    return (value * cdf).astype(BF), (cdf + value * pdf).astype(BF)


def dot_nt(a, b):
    return lax.dot_general(a, b, (((1,), (1,)), ((), ())), preferred_element_type=F32)


def dot_tn(a, b):
    return lax.dot_general(a, b, (((0,), (0,)), ((), ())), preferred_element_type=F32)


def dot_nn(a, b):
    return lax.dot_general(a, b, (((1,), (0,)), ((), ())), preferred_element_type=F32)


def row_blocks(length):
    body = length - CAPTION
    cuts = list(range(0, body, 256)) + [body, length]
    return list(zip(cuts[:-1], cuts[1:]))


def masks(start, stop, length, count):
    rows = stop - start
    query = lax.broadcasted_iota(jnp.int32, (rows, 1), 0)
    own = query >= lax.broadcasted_iota(jnp.int32, (1, rows), 1)
    if stop < length:
        return own, None
    real = query + start < count
    same = real == (lax.broadcasted_iota(jnp.int32, (1, rows), 1) + start < count)
    before = real == (lax.broadcasted_iota(jnp.int32, (1, start), 1) < count)
    return jnp.logical_and(own, same), before


MESH = pl.DeviceIdType.MESH


def plan_hops(groups, which):
    bits = [1 << b for b in range(groups.bit_length() - 1)]
    if len(bits) == 2 and which:
        bits = bits[::-1]
    known = [0]
    steps = []
    for bit in bits:
        steps.append((bit, list(known)))
        known = known + [rel ^ bit for rel in known]
    return steps


def now(value):
    return value() if callable(value) else value


class Links:
    def __init__(self, n_dp, n_mp, send_sems):
        self.n_dp, self.n_mp = n_dp, n_mp
        self.dp = lax.axis_index("dp")
        self.z = lax.axis_index("mp")
        self.core = lax.rem(self.dp, 2)
        self.group = self.dp // 2
        self.send_sems = send_sems
        self.used = 0
        self.open = []

    def barrier(self):
        sem = pltpu.get_barrier_semaphore()
        count = 0
        for cc in range(2):
            for zz in range(self.n_mp):

                @pl.when(jnp.logical_or(cc != self.core, zz != self.z))
                def _(cc=cc, zz=zz):
                    pl.semaphore_signal(
                        sem, inc=1, device_id=(2 * self.group + cc, zz), device_id_type=MESH
                    )

                count += 1
        bit = 1
        while bit < self.n_dp // 2:
            pl.semaphore_signal(
                sem, inc=1, device_id=(self.dp ^ (2 * bit), self.z), device_id_type=MESH
            )
            count += 1
            bit *= 2
        pl.semaphore_wait(sem, count - 1)

    def leaves(self, dp, z, when, may_stay):
        away = None if when is None else now(when)
        if may_stay:
            other = jnp.logical_or(now(dp) != self.dp, now(z) != self.z)
            away = other if away is None else jnp.logical_and(away, other)
        return away

    def copy(self, src, dst, recv_sem, dp, z, slot):
        return pltpu.make_async_remote_copy(
            src_ref=now(src),
            dst_ref=now(dst),
            send_sem=self.send_sems.at[slot],
            recv_sem=recv_sem,
            device_id=(now(dp), now(z)),
            device_id_type=MESH,
        )

    def send(self, src, dst, recv_sem, dp, z, when=None, may_stay=False):
        slot = self.used
        self.used += 1
        away = self.leaves(dp, z, when, may_stay)
        if may_stay:
            stays = jnp.logical_and(now(dp) == self.dp, now(z) == self.z)
            if when is not None:
                stays = jnp.logical_and(now(when), stays)

            @pl.when(stays)
            def _():
                pltpu.make_async_copy(now(src), now(dst), recv_sem).start()

        if away is None:
            self.copy(src, dst, recv_sem, dp, z, slot).start()
        else:

            @pl.when(away)
            def _():
                self.copy(src, dst, recv_sem, dp, z, slot).start()

        def wait():
            self.copy(src, src, self.send_sems.at[slot], self.dp ^ 1, self.z, slot).wait_send()

        entry = (may_stay, when, dp, z, wait)
        self.open.append(entry)
        return entry

    def send_or_keep(self, src, dst, recv_sem, dp, z):
        return self.send(src, dst, recv_sem, dp, z, may_stay=True)

    def send_if(self, condition, src, dst, recv_sem, dp, z):
        return self.send(src, dst, recv_sem, dp, z, when=condition)

    def wait_sent(self, entry):
        entry[4]()
        self.open = [other for other in self.open if other is not entry]

    def arrived(self, src, dst, recv_sem):
        self.copy(src, dst, recv_sem, self.dp ^ 1, self.z, 0).wait_recv()

    def finish(self):
        for may_stay, when, dp, z, wait in self.open:
            away = self.leaves(dp, z, when, may_stay)
            if away is None:
                wait()
            else:
                pl.when(away)(wait)
        self.open = []


def rows_at(index, rows):
    return pl.ds(pl.multiple_of(index * rows, rows), rows)


def exchange_tokens(links, src, dst, sems):
    quarter = src.shape[1]
    for m in range(2):
        links.send_or_keep(
            src.at[m],
            dst.at[rows_at(lax.rem(links.z, 2), quarter), :],
            sems.at[lax.rem(links.z, 2)],
            2 * links.group + links.z // 2,
            2 * m + links.core,
        )


def exchange_tokens_wait(links, src, dst, sems):
    quarter = src.shape[1]
    for s in range(2):
        links.arrived(src.at[0], dst.at[pl.ds(s * quarter, quarter), :], sems.at[s])


class Column:
    def __init__(self, links, src, dst, col_sems, hop_sems):
        self.links, self.src, self.dst = links, src, dst
        self.rows = src.shape[0]
        self.col_sems, self.hop_sems = col_sems, hop_sems
        self.groups = links.n_dp // 2
        self.waited = [set(), set()]

    def start(self):
        k = self.links
        i = lax.rem(k.z, 2)
        home = k.z // 2
        step = 1 - 2 * home
        dst = self.dst.at[i, rows_at(k.dp, self.rows), :]
        sem = self.col_sems.at[i, k.core]
        owner = 2 * k.group + home
        k.send(self.src, dst, sem, owner, k.z + step)
        k.send_if(jnp.logical_or(k.z == 1, k.z == 2), self.src, dst, sem, owner, k.z - step)
        k.send_or_keep(self.src, dst, sem, owner, k.z)

    def piece(self, i, group):
        return self.dst.at[i, rows_at(group, 2 * self.rows), :]

    def hop(self, i, rel, bit):
        k = self.links
        piece = self.piece(i, k.group ^ rel)
        k.send(piece, piece, self.hop_sems.at[i, rel ^ bit], k.dp ^ (2 * bit), k.z)

    def hop_wait(self, i, rel):
        if rel not in self.waited[i]:
            piece = self.piece(i, self.links.group ^ rel)
            self.links.arrived(piece, piece, self.hop_sems.at[i, rel])
            self.waited[i].add(rel)

    def first(self):
        k = self.links
        for i in range(2):
            for c in range(2):
                block = self.dst.at[i, rows_at(2 * k.group + c, self.rows), :]
                k.arrived(self.src, block, self.col_sems.at[i, c])
            up = jnp.logical_and(k.core == 0, jnp.logical_and(k.z > i, k.z < k.n_mp - 1))
            down = jnp.logical_and(k.core == 1, jnp.logical_and(k.z < 2 + i, k.z > 0))
            onward = jnp.logical_or(up, down)
            for c in range(2):
                block = self.dst.at[i, rows_at(2 * k.group + c, self.rows), :]
                k.send_if(
                    onward, block, block, self.col_sems.at[i, c], k.dp, k.z + 1 - 2 * k.core
                )
            for bit, _ in plan_hops(self.groups, i):
                self.hop(i, 0, bit)

    def second(self):
        steps = [plan_hops(self.groups, i) for i in range(2)]
        for level in range(1, len(steps[0])):
            for i in range(2):
                bit, known = steps[i][level]
                for rel in known[1:]:
                    self.hop_wait(i, rel)
                    self.hop(i, rel, bit)

    def last(self):
        for i in range(2):
            for rel in range(1, self.groups):
                self.hop_wait(i, rel)


def sends_of_column(n_mp, hops):
    return 3 + 4 + 2 * hops


def forward_kernel(n_dp, n_mp, *refs):
    smallest = refs[3:8]
    qkv_ref = refs[8]
    v_block, q_block = refs[-2:]
    blocks = (v_block, q_block) + tuple(refs[9:12])
    refs = refs[0:3] + blocks + refs[12:]
    (tokens, grads, seg_ref) = refs[0:3]
    (x_out, g_out, h1_out, qkv_out, o_out, lse_out, a_out, mid_out, h2_out) = refs[8:17]
    (act_out, slope_out, f_out, y_out) = refs[17:21]
    w_outs = refs[21:25]
    count_out, vec_ref = refs[25:27]
    weights = refs[27:32]
    (xb, seg_other, h1, qkv, o, lse, a_send, a_recv, a_own, mid) = refs[32:42]
    (h2, act, slope, f_send, f_recv, f_own, y, bias_ref, upb_ref) = refs[42:51]
    (send_sems, col_sems, hop_sems, tok_sems, swap_sems, keep_sems) = refs[51:57]
    smalls, w_qkv, w_out, w_up, w_down = weights
    links = Links(n_dp, n_mp, send_sems)
    half = xb.shape[0]
    length = 2 * half
    tile = half // 2
    other = links.dp + 1 - 2 * links.core
    mine0 = links.core * half
    other0 = (1 - links.core) * half
    kept = []

    def keep(src, dst):
        copy = pltpu.make_async_copy(src, dst, keep_sems.at[len(kept)])
        copy.start()
        kept.append(copy)

    def at(start, rows):
        return pl.ds(pl.multiple_of(start, 16), rows)

    pack_smalls(smallest, v_block)
    for j in range(3):
        width = qkv_ref.shape[2]
        q_block[:, j * width : (j + 1) * width] = qkv_ref[j]
    links.barrier()
    ways = [Column(links, blocks[a], weights[a], col_sems.at[a], hop_sems.at[a]) for a in range(5)]
    v_way, q_way, o_way, u_way, d_way = ways
    v_way.start()
    o_way.start()
    q_way.start()
    links.send(seg_ref, seg_other, swap_sems.at[0], other, links.z)
    v_way.first()
    o_way.first()
    u_way.start()
    q_way.first()
    exchange_tokens(links, tokens, xb, tok_sems.at[0])
    v_way.second()
    o_way.second()
    q_way.second()
    d_way.start()
    u_way.first()
    links.arrived(seg_ref, seg_other, swap_sems.at[0])
    pick = lax.rem(links.core + links.z, 2) == 0
    seg_row = jnp.where(
        pick, seg_ref[pl.ds(links.z // 2, 1), :], seg_other[pl.ds(links.z // 2, 1), :]
    )
    count = jnp.sum((seg_row == 0).astype(jnp.int32), axis=1, keepdims=True)
    count_out[...] = jnp.broadcast_to(count, count_out.shape)
    v_way.last()
    spread_smalls(n_dp, smalls, vec_ref, bias_ref, upb_ref)
    exchange_tokens_wait(links, tokens, xb, tok_sems.at[0])
    keep(xb, x_out)

    def first_norm(t, _):
        rows = at(t * tile, tile)
        unit, _ = stats(xb[rows, :].astype(F32))
        h1[at(mine0 + t * tile, tile), :] = (unit * vec_ref[0:1, :] + vec_ref[4:5, :]).astype(BF)
        return 0

    lax.fori_loop(0, 2, first_norm, 0)
    links.send(h1.at[at(mine0, half), :], h1.at[at(mine0, half), :], swap_sems.at[1], other, links.z)
    q_way.last()
    cols = qkv.shape[2] // 3
    scale_row = jnp.where(
        lax.broadcasted_iota(jnp.int32, (1, 3 * cols), 1) < cols, SCALE, 1.0
    ).astype(F32)

    def project(start):
        def body(t, _):
            rows = at(start + t * tile, tile)
            for i in range(2):
                value = dot_nn(h1[rows, :], w_qkv[i]) + bias_ref[i : i + 1, :]
                qkv[i, rows, :] = (value * scale_row).astype(BF)
            return 0

        lax.fori_loop(0, 2, body, 0)

    project(mine0)
    links.arrived(
        h1.at[at(mine0, half), :], h1.at[at(other0, half), :], swap_sems.at[1]
    )
    project(other0)
    keep(h1, h1_out)
    keep(qkv, qkv_out)
    u_way.second()
    d_way.first()
    exchange_tokens(links, grads, g_out, tok_sems.at[1])
    pairs = cols // 128

    def attend(i):
        def body(j, _):
            attend_pair_fwd(
                qkv.at[i, :, pl.ds(pl.multiple_of(j * 128, 128), 128)],
                qkv.at[i, :, pl.ds(pl.multiple_of((pairs + j) * 128, 128), 128)],
                qkv.at[i, :, pl.ds(pl.multiple_of((2 * pairs + j) * 128, 128), 128)],
                count,
                o.at[i, :, pl.ds(pl.multiple_of(j * 128, 128), 128)],
                lse,
                2 * (i * pairs + j),
            )
            return 0

        lax.fori_loop(0, pairs, body, 0)

    lse[...] = jnp.zeros_like(lse)
    attend(0)
    attend(1)
    d_way.second()
    keep(o, o_out)
    keep(lse, lse_out)
    o_way.last()

    def out_tile(start):
        return dot_nn(o[0, at(start, tile), :], w_out[0]) + dot_nn(
            o[1, at(start, tile), :], w_out[1]
        )

    def out_theirs(t, _):
        a_send[at(t * tile, tile), :] = out_tile(other0 + t * tile).astype(BF)
        return 0

    def out_ours(t, _):
        a_own[at(t * tile, tile), :] = out_tile(mine0 + t * tile)
        return 0

    lax.fori_loop(0, 2, out_theirs, 0)
    links.send(a_send, a_recv, swap_sems.at[2], other, links.z)
    lax.fori_loop(0, 2, out_ours, 0)
    links.arrived(a_send, a_recv, swap_sems.at[2])

    def middle_norms(t, _):
        rows = at(t * tile, tile)
        branch = a_own[rows, :] + a_recv[rows, :].astype(F32) + vec_ref[8:9, :]
        a_own[rows, :] = branch
        unit, _ = stats(branch)
        middle = xb[rows, :].astype(F32) + unit * vec_ref[1:2, :] + vec_ref[5:6, :]
        mid[rows, :] = middle
        unit, _ = stats(middle)
        h2[at(mine0 + t * tile, tile), :] = (unit * vec_ref[2:3, :] + vec_ref[6:7, :]).astype(BF)
        return 0

    lax.fori_loop(0, 2, middle_norms, 0)
    links.send(h2.at[at(mine0, half), :], h2.at[at(mine0, half), :], swap_sems.at[3], other, links.z)
    keep(a_own, a_out)
    keep(mid, mid_out)
    u_way.last()

    def up(start):
        def body(t, _):
            rows = at(start + t * tile, tile)
            for i in range(2):
                value, slant = gelu_both(dot_nn(h2[rows, :], w_up[i]) + upb_ref[i : i + 1, :])
                act[i, rows, :] = value
                slope[i, rows, :] = slant
            return 0

        lax.fori_loop(0, 2, body, 0)

    up(mine0)
    links.arrived(h2.at[at(mine0, half), :], h2.at[at(other0, half), :], swap_sems.at[3])
    up(other0)
    keep(h2, h2_out)
    keep(act, act_out)
    keep(slope, slope_out)
    d_way.last()

    def down_tile(start):
        return dot_nn(act[0, at(start, tile), :], w_down[0]) + dot_nn(
            act[1, at(start, tile), :], w_down[1]
        )

    def down_theirs(t, _):
        f_send[at(t * tile, tile), :] = down_tile(other0 + t * tile).astype(BF)
        return 0

    def down_ours(t, _):
        f_own[at(t * tile, tile), :] = down_tile(mine0 + t * tile)
        return 0

    lax.fori_loop(0, 2, down_theirs, 0)
    links.send(f_send, f_recv, swap_sems.at[4], other, links.z)
    lax.fori_loop(0, 2, down_ours, 0)
    for weight, w_hbm in zip(weights[1:], w_outs):
        keep(weight, w_hbm)
    links.arrived(f_send, f_recv, swap_sems.at[4])

    def last_norm(t, _):
        rows = at(t * tile, tile)
        value = f_own[rows, :] + f_recv[rows, :].astype(F32) + vec_ref[9:10, :]
        f_own[rows, :] = value
        unit, _ = stats(value)
        y[rows, :] = (mid[rows, :] + unit * vec_ref[3:4, :] + vec_ref[7:8, :]).astype(BF)
        return 0

    lax.fori_loop(0, 2, last_norm, 0)
    keep(f_own, f_out)
    keep(y, y_out)
    exchange_tokens_wait(links, grads, g_out, tok_sems.at[1])
    for copy in kept:
        copy.wait()
    links.finish()


def pack_smalls(refs, block):
    qv, up, gain, shift, bias = refs
    lanes = block.shape[1]

    def fill(value):
        short = lanes - value.shape[1]
        if not short:
            return value
        return jnp.concatenate([value, jnp.zeros((value.shape[0], short), F32)], axis=1)

    first = qv[...].astype(F32)
    first = jnp.concatenate([first[0:1, :], first[1:2, :]], axis=1)
    rest = [ref[...].astype(F32) for ref in (up, gain, shift, bias)]
    rows = [fill(value) for value in [first] + rest] + [jnp.zeros((4, lanes), F32)]
    block[...] = jnp.concatenate(rows, axis=0).astype(block.dtype)


def spread_smalls(n_dp, smalls, vec_ref, bias_ref, upb_ref):
    width = vec_ref.shape[1]
    slim = width // n_dp
    per_qv = bias_ref.shape[1] // 3 // n_dp
    per_up = upb_ref.shape[1] // n_dp
    row = [
        [smalls[i, 16 * dp : 16 * dp + 16, :].astype(F32) for dp in range(n_dp)] for i in range(2)
    ]
    wide = jnp.concatenate([row[0][dp][2:12, 0:slim] for dp in range(n_dp)], axis=1)
    vec_ref[0:10, :] = wide
    vec_ref[10:16, :] = jnp.zeros((6, width), F32)
    for i in range(2):
        queries = [row[i][dp][0:1, 0:per_qv] for dp in range(n_dp)]
        values = [row[i][dp][0:1, per_qv : 2 * per_qv] for dp in range(n_dp)]
        zeros = [jnp.zeros((1, n_dp * per_qv), F32)]
        bias_ref[i : i + 1, :] = jnp.concatenate(queries + zeros + values, axis=1)
        upb_ref[i : i + 1, :] = jnp.concatenate(
            [row[i][dp][1:2, 0:per_up] for dp in range(n_dp)], axis=1
        )


def attend_pair_fwd(q_ref, k_ref, v_ref, count, o_ref, lse_ref, head0):
    length = q_ref.shape[0]
    lane = lax.broadcasted_iota(jnp.int32, (1, 128), 1)
    for start, stop in row_blocks(length):
        own, before = masks(start, stop, length, count)
        outs = []
        lses = []
        for head in range(2):
            q = jnp.where((lane >= 64) == (head == 1), q_ref[start:stop, :], jnp.zeros((), BF))
            s2 = jnp.where(own, dot_nt(q, k_ref[start:stop, :]), NEG)
            top = jnp.max(s2, axis=-1, keepdims=True)
            if start:
                s1 = dot_nt(q, k_ref[0:start, :])
                if before is not None:
                    s1 = jnp.where(before, s1, NEG)
                top = jnp.maximum(top, jnp.max(s1, axis=-1, keepdims=True))
            e2 = jnp.exp(ALPHA * (s2 - top))
            total = jnp.sum(e2, axis=-1, keepdims=True)
            acc = dot_nn(e2.astype(BF), v_ref[start:stop, :])
            if start:
                e1 = jnp.exp(ALPHA * (s1 - top))
                total = total + jnp.sum(e1, axis=-1, keepdims=True)
                acc = acc + dot_nn(e1.astype(BF), v_ref[0:start, :])
            outs.append(acc / total)
            lses.append(ALPHA * top + jnp.log(total))
        o_ref[start:stop, :] = jnp.where(lane < 64, outs[0], outs[1]).astype(BF)
        kept = jnp.where(lane == head0, lses[0], lse_ref[start:stop, :])
        lse_ref[start:stop, :] = jnp.where(lane == head0 + 1, lses[1], kept)


def forward_all(n_dp, n_mp, tokens, grads, seg_ids, smalls, qkv_weight, blocks):
    groups = n_dp // 2
    hops = groups - 1
    any_spec = pl.BlockSpec(memory_space=pl.ANY)
    vmem = pl.BlockSpec(memory_space=pltpu.VMEM)
    width = tokens.shape[2]
    half = 2 * tokens.shape[1]
    length = 2 * half
    cols3 = 3 * qkv_weight.shape[2]
    cols = cols3 // 3
    ff = n_dp * blocks[2].shape[0]
    shape = jax.ShapeDtypeStruct
    first = [(16, 128), (qkv_weight.shape[1], cols3)]
    full = [(2, n_dp * b[0], b[1]) for b in first + [b.shape for b in blocks]]
    out_shape = [
        shape((half, width), BF),
        shape((half, width), BF),
        shape((length, width), BF),
        shape((2, length, cols3), BF),
        shape((2, length, cols), BF),
        shape((length, 128), F32),
        shape((half, width), F32),
        shape((half, width), F32),
        shape((length, width), BF),
        shape((2, length, ff), BF),
        shape((2, length, ff), BF),
        shape((half, width), F32),
        shape((half, width), BF),
    ] + [shape(f, BF) for f in full[1:]] + [shape((8, 128), jnp.int32), shape((16, width), F32)]
    return pl.pallas_call(
        functools.partial(forward_kernel, n_dp, n_mp),
        in_specs=[any_spec] * 2 + [vmem] * 7 + [any_spec] * 3,
        out_specs=[any_spec] * 17 + [vmem] * 2,
        out_shape=out_shape,
        scratch_shapes=[pltpu.VMEM(f, BF) for f in full]
        + [
            pltpu.VMEM((half, width), BF),
            pltpu.VMEM(seg_ids.shape, jnp.int32),
            pltpu.VMEM((length, width), BF),
            pltpu.VMEM((2, length, cols3), BF),
            pltpu.VMEM((2, length, cols), BF),
            pltpu.VMEM((length, 128), F32),
            pltpu.VMEM((half, width), BF),
            pltpu.VMEM((half, width), BF),
            pltpu.VMEM((half, width), F32),
            pltpu.VMEM((half, width), F32),
            pltpu.VMEM((length, width), BF),
            pltpu.VMEM((2, length, ff), BF),
            pltpu.VMEM((2, length, ff), BF),
            pltpu.VMEM((half, width), BF),
            pltpu.VMEM((half, width), BF),
            pltpu.VMEM((half, width), F32),
            pltpu.VMEM((half, width), BF),
            pltpu.VMEM((2, cols3), F32),
            pltpu.VMEM((2, ff), F32),
            pltpu.SemaphoreType.DMA((9 + 5 * sends_of_column(n_mp, hops),)),
            pltpu.SemaphoreType.DMA((5, 2, 2)),
            pltpu.SemaphoreType.DMA((5, 2, groups)),
            pltpu.SemaphoreType.DMA((2, 2)),
            pltpu.SemaphoreType.DMA((5,)),
            pltpu.SemaphoreType.DMA((17,)),
        ]
        + [pltpu.VMEM(shape_of, BF) for shape_of in first],
        compiler_params=pltpu.CompilerParams(
            collective_id=0, has_side_effects=True, vmem_limit_bytes=60 << 20
        ),
    )(tokens, grads, seg_ids, *smalls, qkv_weight, *blocks)


def attend_pair_bwd(q_ref, k_ref, v_ref, do_ref, lse_ref, head0, count, dk_ref, dv_ref):
    length = q_ref.shape[0]
    lane = lax.broadcasted_iota(jnp.int32, (1, 128), 1)
    dk_ref[...] = jnp.zeros_like(dk_ref)
    dv_ref[...] = jnp.zeros_like(dv_ref)
    zero = jnp.zeros((), BF)
    for start, stop in row_blocks(length):
        own, before = masks(start, stop, length, count)
        dqs = []
        for head in range(2):
            mine = (lane >= 64) == (head == 1)
            q = jnp.where(mine, q_ref[start:stop, :], zero)
            do = jnp.where(mine, do_ref[start:stop, :], zero)
            lse = jnp.sum(
                jnp.where(lane == head0 + head, lse_ref[start:stop, :], 0.0), axis=-1, keepdims=True
            )
            p2 = jnp.where(own, jnp.exp(ALPHA * dot_nt(q, k_ref[start:stop, :]) - lse), 0.0)
            g2 = dot_nt(do, v_ref[start:stop, :])
            delta = jnp.sum(p2 * g2, axis=-1, keepdims=True)
            if start:
                p1 = jnp.exp(ALPHA * dot_nt(q, k_ref[0:start, :]) - lse)
                if before is not None:
                    p1 = jnp.where(before, p1, 0.0)
                g1 = dot_nt(do, v_ref[0:start, :])
                delta = delta + jnp.sum(p1 * g1, axis=-1, keepdims=True)
            ds2 = (ALPHA * p2 * (g2 - delta)).astype(BF)
            dq = dot_nn(ds2, k_ref[start:stop, :])
            dk_ref[start:stop, :] += dot_tn(ds2, q)
            dv_ref[start:stop, :] += dot_tn(p2.astype(BF), do)
            if start:
                ds1 = (ALPHA * p1 * (g1 - delta)).astype(BF)
                dq = dq + dot_nn(ds1, k_ref[0:start, :])
                dk_ref[0:start, :] += dot_tn(ds1, q)
                dv_ref[0:start, :] += dot_tn(p1.astype(BF), do)
            dqs.append(dq)
        q_ref[start:stop, :] = (jnp.where(lane < 64, dqs[0], dqs[1]) * SCALE).astype(BF)
    k_ref[...] = dk_ref[...].astype(BF)
    v_ref[...] = dv_ref[...].astype(BF)


FAR = (1, 3, 4)


class Reduce:
    def __init__(self, links, part, slots, column, merge, slot_sems, column_sems, merge_sems, load):
        self.load, self.near, self.copies = load, [], []
        self.links, self.part, self.slots = links, part, slots
        self.column, self.merge = column, merge
        self.slot_sems, self.column_sems, self.merge_sems = slot_sems, column_sems, merge_sems
        self.groups = links.n_dp // 2
        self.rows = part.shape[1] // links.n_dp
        self.steps = [plan_hops(self.groups, i)[::-1] for i in range(2)]
        self.place = jnp.where(links.core == 0, links.z, links.n_mp - 1 - links.z)
        self.terms = links.n_mp if merge is None else links.n_mp - 1

    def piece(self, i, rel):
        return self.part.at[i, rows_at(self.links.group ^ rel, 2 * self.rows), :]

    def slot(self, i, rel):
        return self.slots.at[i, pl.ds((rel - 1) * 2 * self.rows, 2 * self.rows), :]

    def give(self, i, rel, bit):
        k = self.links
        k.send(
            lambda: self.piece(i, rel),
            lambda: self.slot(i, rel),
            self.slot_sems.at[i, rel],
            k.dp ^ (2 * bit),
            k.z,
        )

    def start(self, i):
        bit, known = self.steps[i][0]
        for rel in known[::-1]:
            self.give(i, rel ^ bit, bit)

    def add(self, i, rel, source):
        tile = min(32, 2 * self.rows)
        base = (self.links.group ^ rel) * 2 * self.rows

        def body(t, _):
            rows = pl.ds(pl.multiple_of(base + t * tile, tile), tile)
            came = source[pl.ds(pl.multiple_of(t * tile, tile), tile), :]
            total = self.part[i, rows, :].astype(F32) + came.astype(F32)
            self.part[i, rows, :] = total.astype(self.part.dtype)
            return 0

        lax.fori_loop(0, 2 * self.rows // tile, body, 0)

    def level(self, i, number):
        k = self.links
        bit, known = self.steps[i][number]
        after = self.steps[i][number + 1][0] if number + 1 < len(self.steps[i]) else 0
        for rel in sorted(known, key=lambda r: not r & after):
            k.arrived(self.piece(i, rel), self.slot(i, rel ^ bit), self.slot_sems.at[i, rel ^ bit])
            self.add(i, rel, self.slot(i, rel ^ bit))
            if rel & after:
                self.give(i, rel, after)
        if not after:
            if self.merge is None:
                self.ship(i, None)
            else:
                k.send(
                    lambda: self.piece(i, 0),
                    self.merge.at[i],
                    self.merge_sems.at[i],
                    k.dp,
                    k.z - 1 + 2 * k.core,
                    when=lambda: self.place == 3,
                )
                self.ship(i, lambda: self.place < 2)

    def ship(self, i, when):
        k = self.links
        slot = k.z if self.merge is None else jnp.where(self.place == 3, 0, k.z - k.core)
        for c in range(2):
            k.send(
                lambda c=c: self.part.at[i, rows_at(2 * k.group + c, self.rows), :],
                lambda slot=slot: self.column.at[slot],
                self.column_sems.at[slot],
                lambda c=c: 2 * k.group + c,
                lambda: 2 * k.core + i,
                when=when,
                may_stay=True,
            )

    def levels(self, number):
        for i in range(2):
            self.level(i, number)

    def merged(self):
        for i in range(2):

            @pl.when(self.place == 2)
            def _(i=i):
                self.links.arrived(self.merge.at[i], self.merge.at[i], self.merge_sems.at[i])
                self.add(i, 0, self.merge.at[i])

            self.ship(i, lambda: self.place == 2)

    def collect(self):
        if self.near:
            return
        for zz in range(self.terms):
            term = self.column.at[zz]
            self.links.arrived(term, term, self.column_sems.at[zz])
            if self.load:
                near = self.slots.at[0, pl.ds(zz * self.rows, self.rows), :]
                self.copies.append(self.load(term, near))
                term = near
            self.near.append(term)

    def total(self, out):
        self.collect()
        for copy in self.copies:
            copy.wait()
        tile = min(32, self.rows)

        def body(t, _):
            rows = pl.ds(pl.multiple_of(t * tile, tile), tile)
            value = self.near[0][rows, :].astype(F32)
            for ref in self.near[1:]:
                value = value + ref[rows, :].astype(F32)
            out[rows, :] = value
            return 0

        lax.fori_loop(0, self.rows // tile, body, 0)


def return_tokens(links, parts, dst, sems):
    quarter = dst.shape[1]
    m = links.z // 2
    for s in range(2):
        links.send_or_keep(
            parts.at[pl.ds(s * quarter, quarter), :],
            dst.at[m],
            sems.at[m],
            2 * links.group + lax.rem(links.z, 2),
            2 * links.core + s,
        )


def return_tokens_wait(links, dst, sems):
    for m in range(2):
        links.arrived(dst.at[m], dst.at[m], sems.at[m])


def backward_kernel(n_dp, n_mp, *refs):
    (y_hbm, g_hbm, x_hbm, a_hbm, mid_hbm, f_hbm, h1_hbm, qkv_hbm, o_hbm, lse_hbm) = refs[0:10]
    (h2_hbm, act_hbm, slope_hbm, wq_hbm, wo_hbm, wu_hbm, wd_hbm, vec_ref, count_ref) = refs[10:19]
    (layer_out, back, q_out, o_out, u_out, d_out, v_out) = refs[19:26]
    fars = refs[26:29]
    refs = refs[:26] + refs[28:]
    parts = refs[27:32]
    slots = refs[32:37]
    columns = list(refs[37:42])
    merges = (None,) + tuple(refs[42:46])
    refs = refs[:42] + refs[46:]
    for a, far in zip(FAR, fars):
        columns[a] = far
    (pair, take, own, own2, g_buf) = refs[42:47]
    refs = refs[:47] + (None,) + refs[47:]
    (act, du, h, wd, wu, lse, dk, dv, vsum, vtake, vqkv, vup) = refs[48:60]
    (send_sems, slot_sems, column_sems, merge_sems, tok_sems, swap_sems, load_sems) = refs[60:67]
    links = Links(n_dp, n_mp, send_sems)
    half = g_buf.shape[0]
    length = 2 * half
    tile = half // 2
    width = g_buf.shape[1]
    other = links.dp + 1 - 2 * links.core
    mine0 = links.core * half
    other0 = (1 - links.core) * half
    cols3 = qkv_hbm.shape[2]
    cols = cols3 // 3
    loads = [0]
    parts = list(parts)
    give = h.at[pl.ds(0, half), :]
    parts[1] = du.at[:, pl.ds(0, width), pl.ds(cols, cols3)]
    if parts[2].dtype == BF:
        parts[2] = wu.at[:, pl.ds(half, cols), :]
    else:
        parts[2] = own2.at[:, pl.ds(0, cols), :]

    def load(src, dst):
        copy = pltpu.make_async_copy(src, dst, load_sems.at[loads[0]])
        loads[0] += 1
        copy.start()
        return copy

    def at(start, rows):
        return pl.ds(pl.multiple_of(start, 16), rows)

    def gain(k):
        return vec_ref[k : k + 1, :]

    f_load = load(f_hbm, own)
    g_load = load(g_hbm, g_buf)
    act_load = load(act_hbm, act)
    wd_load = load(wd_hbm, wd)
    slope_load = load(slope_hbm, du)
    h_load = load(h2_hbm, h)
    wu_load = load(wu_hbm, wu)
    lse_load = load(lse_hbm, lse)
    vsum[...] = jnp.zeros_like(vsum)
    vqkv[...] = jnp.zeros_like(vqkv)
    vup[...] = jnp.zeros_like(vup)
    links.barrier()
    ways = [
        Reduce(
            links,
            parts[a],
            slots[a],
            columns[a],
            merges[a],
            slot_sems.at[a],
            column_sems.at[a],
            merge_sems.at[a],
            load if a in FAR else None,
        )
        for a in range(5)
    ]
    v_way, q_way, o_way, u_way, d_way = ways
    return_tokens(links, y_hbm, layer_out, tok_sems.at[0])

    def norm_grad(value, k, grad):
        unit, inverse = stats(value)
        back, dgain, dshift = norm_back(unit, inverse, gain(k), grad)
        vsum[k : k + 1, :] += dgain[None]
        vsum[4 + k : 5 + k, :] += dshift[None]
        return back

    f_load.wait()
    g_load.wait()

    def last_norm(t, _):
        rows = at(t * tile, tile)
        back = norm_grad(own[rows, :], 3, g_buf[rows, :].astype(F32)).astype(BF)
        vsum[9:10, :] += jnp.sum(back.astype(F32), axis=0, keepdims=True)
        pair[at(mine0 + t * tile, tile), :] = back
        return 0

    lax.fori_loop(0, 2, last_norm, 0)
    ours = pair.at[at(mine0, half), :]
    theirs = pair.at[at(other0, half), :]
    df_send = links.send(ours, ours, swap_sems.at[0], other, links.z)
    act_load.wait()
    links.arrived(ours, theirs, swap_sems.at[0])

    def weight_grad(left, right, part, i):
        step = min(256, left.shape[1])

        def body(t, _):
            lanes = pl.ds(pl.multiple_of(t * step, 128), step)
            rows = pl.ds(pl.multiple_of(t * step, 16), step)
            part[i, rows, :] = dot_tn(left[:, lanes], right[...]).astype(part.dtype)
            return 0

        lax.fori_loop(0, left.shape[1] // step, body, 0)

    for i in range(2):
        weight_grad(act.at[i], pair, parts[4], i)
        d_way.start(i)
    qkv_load = load(qkv_hbm, act.at[:, :, 0:cols3])
    wd_load.wait()
    slope_load.wait()
    h_load.wait()
    for i in range(2):

        def slant(t, _, i=i):
            rows = at(t * tile, tile)
            value = (dot_nt(pair[rows, :], wd[i]) * du[i, rows, :].astype(F32)).astype(BF)
            du[i, rows, :] = value
            vup[i : i + 1, :] += jnp.sum(value.astype(F32), axis=0, keepdims=True)
            return 0

        lax.fori_loop(0, 4, slant, 0)
        weight_grad(h, du.at[i], parts[3], i)
    wq_load = load(wq_hbm, wd.at[:, :, 0:cols3])
    a_load = load(a_hbm.at[pl.ds(0, tile), :], own2.at[0])
    mid_load = load(mid_hbm.at[pl.ds(0, tile), :], own2.at[1])
    wu_load.wait()

    def up_tile(start):
        return dot_nt(du[0, at(start, tile), :], wu[0]) + dot_nt(du[1, at(start, tile), :], wu[1])

    def up_theirs(t, _):
        give[at(t * tile, tile), :] = up_tile(other0 + t * tile).astype(BF)
        return 0

    def up_ours(t, _):
        own[at(t * tile, tile), :] = up_tile(mine0 + t * tile)
        return 0

    lax.fori_loop(0, 2, up_theirs, 0)
    up_send = links.send(give, take, swap_sems.at[1], other, links.z)
    lax.fori_loop(0, 2, up_ours, 0)
    o_load = load(o_hbm, du.at[:, :, 0:cols])
    x_load = load(x_hbm, wu.at[0, pl.ds(0, half), :])
    wo_load = [load(wo_hbm.at[i], wu.at[1, pl.ds(i * cols, cols), :]) for i in range(2)]
    links.wait_sent(df_send)
    links.arrived(give, take, swap_sems.at[1])
    for t in range(2):
        a_load.wait()
        mid_load.wait()
        rows = pl.ds(t * tile, tile)
        grad = own[rows, :] + take[rows, :].astype(F32)
        grad = g_buf[rows, :].astype(F32) + norm_grad(own2[1], 2, grad)
        own[rows, :] = grad
        grad = norm_grad(own2[0], 1, grad).astype(BF)
        vsum[8:9, :] += jnp.sum(grad.astype(F32), axis=0, keepdims=True)
        pair[at(mine0 + t * tile, tile), :] = grad
        if t == 0:
            a_load = load(a_hbm.at[pl.ds(tile, tile), :], own2.at[0])
            mid_load = load(mid_hbm.at[pl.ds(tile, tile), :], own2.at[1])
    links.send(ours, ours, swap_sems.at[2], other, links.z)
    links.wait_sent(up_send)
    h_load = load(h1_hbm, h)
    d_way.levels(0)
    u_way.start(0)
    u_way.start(1)
    o_load.wait()
    qkv_load.wait()
    wo_load[0].wait()
    wo_load[1].wait()
    links.arrived(ours, theirs, swap_sems.at[2])

    def open_heads(t, _):
        rows = at(t * tile, tile)
        for i in range(2):
            value = dot_nt(pair[rows, :], wu[1, i * cols : (i + 1) * cols, :])
            act[i, rows, cols3 : cols3 + cols] = value.astype(BF)
        return 0

    lax.fori_loop(0, 4, open_heads, 0)
    for i in range(2):
        weight_grad(du.at[i, :, 0:cols], pair, parts[2], i)
        o_way.start(i)
    lse_load.wait()
    h_load.wait()
    wq_load.wait()
    count = count_ref[0:1, 0:1]
    pairs = cols // 128

    def attend(n, _):
        i = n // pairs
        lanes = lambda base: pl.ds(pl.multiple_of((base + lax.rem(n, pairs)) * 128, 128), 128)
        attend_pair_bwd(
            act.at[i, :, lanes(0)],
            act.at[i, :, lanes(pairs)],
            act.at[i, :, lanes(2 * pairs)],
            act.at[i, :, lanes(3 * pairs)],
            lse,
            2 * n,
            count,
            dk,
            dv,
        )

        @pl.when(n == 0)
        def _():
            d_way.levels(1)

        @pl.when(n == pairs - 1)
        def _():
            weight_grad(h, act.at[0, :, 0:cols3], parts[1], 0)
            d_way.merged()

        @pl.when(n == pairs)
        def _():
            u_way.levels(0)
            q_way.start(0)

        return 0

    lax.fori_loop(0, 2 * pairs, attend, 0)
    weight_grad(h, act.at[1, :, 0:cols3], parts[1], 1)
    q_way.start(1)

    def head_tile(start):
        rows = at(start, tile)
        total = None
        for i in range(2):
            value = act[i, rows, 0:cols3]
            vqkv[i : i + 1, :] += jnp.sum(value.astype(F32), axis=0, keepdims=True)
            term = dot_nt(value, wd[i, :, 0:cols3])
            total = term if total is None else total + term
        return total

    def head_theirs(t, _):
        give[at(t * tile, tile), :] = head_tile(other0 + t * tile).astype(BF)
        return 0

    lax.fori_loop(0, 2, head_theirs, 0)
    links.send(give, take, swap_sems.at[3], other, links.z)
    o_way.levels(0)
    u_way.levels(1)
    x_load.wait()
    links.arrived(give, take, swap_sems.at[3])

    def first_norm(t, _):
        rows = at(t * tile, tile)
        grad = head_tile(mine0 + t * tile) + take[rows, :].astype(F32)
        grad = own[rows, :] + norm_grad(wu[0, rows, :].astype(F32), 0, grad)
        g_buf[rows, :] = grad.astype(BF)
        return 0

    lax.fori_loop(0, 2, first_norm, 0)
    return_tokens(links, g_buf, back, tok_sems.at[1])
    links.send(vsum, vtake, swap_sems.at[4], other, links.z)
    q_way.level(0, 0)
    o_way.levels(1)
    links.arrived(vsum, vtake, swap_sems.at[4])
    gather_smalls(n_dp, vsum[...] + vtake[...], vqkv, vup, parts[0])
    v_way.start(0)
    v_way.start(1)
    u_way.merged()
    d_way.collect()
    q_way.level(1, 0)
    v_way.levels(0)
    o_way.merged()
    d_way.total(d_out)
    v_way.levels(1)
    q_way.levels(1)
    u_way.collect()
    o_way.total(o_out)
    u_way.total(u_out)
    q_way.merged()
    return_tokens_wait(links, back, tok_sems.at[1])
    v_way.total(v_out)
    q_way.total(q_out)
    return_tokens_wait(links, layer_out, tok_sems.at[0])
    links.finish()


def gather_smalls(n_dp, total, vqkv, vup, part):
    width = total.shape[1]
    slim = width // n_dp
    per_qv = vqkv.shape[1] // 3 // n_dp
    per_up = vup.shape[1] // n_dp
    lanes = part.shape[2]
    values = 2 * per_qv * n_dp

    def fill(value):
        short = lanes - value.shape[1]
        if not short:
            return value
        return jnp.concatenate([value, jnp.zeros((value.shape[0], short), F32)], axis=1)

    for i in range(2):
        qkv = vqkv[i : i + 1, :]
        up = vup[i : i + 1, :]
        for dp in range(n_dp):
            first = jnp.concatenate(
                [
                    qkv[:, dp * per_qv : (dp + 1) * per_qv],
                    qkv[:, values + dp * per_qv : values + (dp + 1) * per_qv],
                ],
                axis=1,
            )
            base = 16 * dp
            part[i, base : base + 1, :] = fill(first)
            part[i, base + 1 : base + 2, :] = fill(up[:, dp * per_up : (dp + 1) * per_up])
            part[i, base + 2 : base + 12, :] = fill(total[0:10, dp * slim : (dp + 1) * slim])
            part[i, base + 12 : base + 16, :] = jnp.zeros((4, lanes), F32)


def backward_all(n_dp, n_mp, saved, weights, vec, count):
    groups = n_dp // 2
    any_spec = pl.BlockSpec(memory_space=pl.ANY)
    vmem = pl.BlockSpec(memory_space=pltpu.VMEM)
    shape = jax.ShapeDtypeStruct
    half, width = saved[0].shape
    length = 2 * half
    cols3 = saved[7].shape[2]
    cols = cols3 // 3
    ff = saved[11].shape[2]
    full = [(2, n_dp * 16, 128)] + [w.shape for w in weights]
    each = [f[1] // n_dp for f in full]
    kinds = [F32] + [BF if r % 8 == 0 else F32 for r in each[1:]]
    out_shape = [shape((2, half // 2, width), BF)] * 2 + [
        shape((each[a], full[a][2]), F32) for a in (1, 2, 3, 4, 0)
    ]
    out_shape += [shape((n_mp, each[a], full[a][2]), kinds[a]) for a in FAR]
    sends = 4 + 5 + 5 * (2 * (groups - 1) + 10)
    return pl.pallas_call(
        functools.partial(backward_kernel, n_dp, n_mp),
        in_specs=[any_spec] * 17 + [vmem] * 2,
        out_specs=[any_spec] * 2 + [vmem] * 5 + [any_spec] * 3,
        out_shape=out_shape,
        scratch_shapes=[
            pltpu.VMEM((1, 16, 128) if a in (1, 2) else f, k)
            for a, (f, k) in enumerate(zip(full, kinds))
        ]
        + [
            pltpu.VMEM((2, (groups - 1) * 2 * r, f[2]), k) for f, r, k in zip(full, each, kinds)
        ]
        + [
            pltpu.VMEM((n_mp, 16 if a in FAR else r, f[2]), k)
            for a, (f, r, k) in enumerate(zip(full, each, kinds))
        ]
        + [
            pltpu.VMEM((2, 2 * r, f[2]), k) for f, r, k in zip(full[1:], each[1:], kinds[1:])
        ]
        + [
            pltpu.VMEM((length, width), BF),
            pltpu.VMEM((half, width), BF),
            pltpu.VMEM((half, width), F32),
            pltpu.VMEM((2, half // 2, width), F32),
            pltpu.VMEM((half, width), BF),
            pltpu.VMEM((2, length, ff), BF),
            pltpu.VMEM((2, length, ff), BF),
            pltpu.VMEM((length, width), BF),
            pltpu.VMEM((2, ff, width), BF),
            pltpu.VMEM((2, width, ff), BF),
            pltpu.VMEM((length, 128), F32),
            pltpu.VMEM((length, 128), F32),
            pltpu.VMEM((length, 128), F32),
            pltpu.VMEM((16, width), F32),
            pltpu.VMEM((16, width), F32),
            pltpu.VMEM((2, cols3), F32),
            pltpu.VMEM((2, ff), F32),
            pltpu.SemaphoreType.DMA((sends,)),
            pltpu.SemaphoreType.DMA((5, 2, groups)),
            pltpu.SemaphoreType.DMA((5, n_mp)),
            pltpu.SemaphoreType.DMA((5, 2)),
            pltpu.SemaphoreType.DMA((2, 2)),
            pltpu.SemaphoreType.DMA((5,)),
            pltpu.SemaphoreType.DMA((19 + len(FAR) * n_mp,)),
        ],
        compiler_params=pltpu.CompilerParams(
            collective_id=1, has_side_effects=True, vmem_limit_bytes=61 << 20
        ),
    )(*saved, *weights, vec, count)[:7]


def finish_kernel(*refs):
    far = refs[0:7]
    (layer_out, grad_out, q_out, qv_out, o_out, u_out, up_out, d_out) = refs[7:15]
    gain_out, shift_out, bias_out = refs[15:18]
    near, sems = refs[18:25], refs[25]
    copies = [
        pltpu.make_async_copy(a, b, sems.at[n]) for n, (a, b) in enumerate(zip(far, near))
    ]
    for copy in copies:
        copy.start()
    for copy in copies:
        copy.wait()
    layer, back, q, o, u, d, v = near
    layer_out[...] = layer[...]
    grad_out[...] = back[...].astype(F32)
    cols = q.shape[1] // 3
    for j in range(3):
        q_out[j] = q[:, j * cols : (j + 1) * cols]
    per = qv_out.shape[1]
    qv_out[0:1, :] = v[0:1, 0:per]
    qv_out[1:2, :] = v[0:1, per : 2 * per]
    o_out[...] = o[...]
    u_out[...] = u[...]
    up_out[...] = v[1:2, 0 : up_out.shape[1]]
    d_out[...] = d[...]
    slim = gain_out.shape[1]
    gain_out[...] = v[2:6, 0:slim]
    shift_out[...] = v[6:10, 0:slim]
    bias_out[...] = v[10:12, 0:slim]


def finish_all(arrays, per_qv, per_up, slim):
    layer, back, q, o, u, d, v = arrays
    far = pl.BlockSpec(memory_space=pl.ANY)
    vmem = pl.BlockSpec(memory_space=pltpu.VMEM)
    shape = jax.ShapeDtypeStruct
    return pl.pallas_call(
        finish_kernel,
        in_specs=[far] * 7,
        out_specs=[vmem] * 11,
        out_shape=[
            shape(layer.shape, BF),
            shape(back.shape, F32),
            shape((3, q.shape[0], q.shape[1] // 3), F32),
            shape((2, per_qv), F32),
            shape(o.shape, F32),
            shape(u.shape, F32),
            shape((1, per_up), F32),
            shape(d.shape, F32),
            shape((4, slim), F32),
            shape((4, slim), F32),
            shape((2, slim), F32),
        ],
        scratch_shapes=[pltpu.VMEM(a.shape, a.dtype) for a in arrays]
        + [pltpu.SemaphoreType.DMA((7,))],
        compiler_params=pltpu.CompilerParams(vmem_limit_bytes=60 << 20),
    )(*arrays)


def build(n_dp, n_mp):
    def on_device(
        tokens,
        seg_ids,
        qkv_weight,
        qv_bias,
        out_weight,
        up_weight,
        up_bias,
        down_weight,
        norm_gain,
        norm_bias,
        branch_bias,
        out_grad,
    ):
        (
            x,
            grad_y,
            h1,
            qkvs,
            attended,
            log_sums,
            branch,
            middle,
            h2,
            acts,
            slopes,
            ffn_out,
            out_rows,
            w_qkv,
            w_out,
            w_up,
            w_down,
            count,
            vec,
        ) = forward_all(
            n_dp,
            n_mp,
            tokens,
            out_grad,
            seg_ids,
            [qv_bias, up_bias.reshape(1, -1), norm_gain, norm_bias, branch_bias],
            qkv_weight,
            [out_weight, up_weight, down_weight],
        )
        saved = [
            out_rows,
            grad_y,
            x,
            branch,
            middle,
            ffn_out,
            h1,
            qkvs,
            attended,
            log_sums,
            h2,
            acts,
            slopes,
        ]
        sums = backward_all(n_dp, n_mp, saved, [w_qkv, w_out, w_up, w_down], vec, count)
        outs = list(finish_all(sums, qv_bias.shape[1], up_bias.shape[0], norm_gain.shape[1]))
        outs[6] = outs[6].reshape(-1)
        return tuple(outs)

    return on_device


def solution(mesh):
    n_dp, n_mp = mesh.shape["dp"], mesh.shape["mp"]
    in_specs = (
        P(None, ("dp", "mp"), None),
        P(None, "dp"),
        P(None, "dp", "mp"),
        P(None, ("mp", "dp")),
        P(("mp", "dp"), None),
        P("dp", "mp"),
        P(("mp", "dp")),
        P(("mp", "dp"), None),
        P(None, "dp"),
        P(None, "dp"),
        P(None, "dp"),
        P(None, ("dp", "mp"), None),
    )
    out_specs = (
        P(None, ("dp", "mp"), None),
        P(None, ("dp", "mp"), None),
        P(None, "dp", "mp"),
        P(None, ("mp", "dp")),
        P(("mp", "dp"), None),
        P("dp", "mp"),
        P(("mp", "dp")),
        P(("mp", "dp"), None),
        P(None, "dp"),
        P(None, "dp"),
        P(None, "dp"),
    )
    return jax.shard_map(
        build(n_dp, n_mp), mesh=mesh, in_specs=in_specs, out_specs=out_specs, check_vma=False
    )
```

```python
import functools
import math

import jax
import jax.numpy as jnp
from jax import lax
from jax.experimental import pallas as pl
from jax.experimental.pallas import tpu as pltpu
from jax.sharding import PartitionSpec as P

HEAD_DIM = 64
CAPTION = 64
ALPHA = 32.0
EPS = 1e-05
SCALE = 1.0 / (ALPHA * math.sqrt(HEAD_DIM))
NEG = -1e30
BF = jnp.bfloat16
F32 = jnp.float32


def stats(value):
    mean = jnp.mean(value, axis=-1, keepdims=True)
    centred = value - mean
    inverse = lax.rsqrt(jnp.mean(centred * centred, axis=-1, keepdims=True) + EPS)
    return centred * inverse, inverse


def norm_back(unit, inverse, gain, grad):
    scaled = grad * gain
    grad_in = inverse * (
        scaled
        - jnp.mean(scaled, axis=-1, keepdims=True)
        - unit * jnp.mean(scaled * unit, axis=-1, keepdims=True)
    )
    return grad_in, jnp.sum(grad * unit, axis=0), jnp.sum(grad, axis=0)


def gelu_both(value):
    cdf = 0.5 * (1.0 + lax.erf(value * (1.0 / math.sqrt(2.0))))
    pdf = jnp.exp(-0.5 * value * value) * (1.0 / math.sqrt(2.0 * math.pi))
    return (value * cdf).astype(BF), (cdf + value * pdf).astype(BF)


def dot_nt(a, b):
    return lax.dot_general(a, b, (((1,), (1,)), ((), ())), preferred_element_type=F32)


def dot_tn(a, b):
    return lax.dot_general(a, b, (((0,), (0,)), ((), ())), preferred_element_type=F32)


def dot_nn(a, b):
    return lax.dot_general(a, b, (((1,), (0,)), ((), ())), preferred_element_type=F32)


def row_blocks(length):
    body = length - CAPTION
    cuts = list(range(0, body, 256)) + [body, length]
    return list(zip(cuts[:-1], cuts[1:]))


def masks(start, stop, length, count):
    rows = stop - start
    query = lax.broadcasted_iota(jnp.int32, (rows, 1), 0)
    own = query >= lax.broadcasted_iota(jnp.int32, (1, rows), 1)
    if stop < length:
        return own, None
    real = query + start < count
    same = real == (lax.broadcasted_iota(jnp.int32, (1, rows), 1) + start < count)
    before = real == (lax.broadcasted_iota(jnp.int32, (1, start), 1) < count)
    return jnp.logical_and(own, same), before


MESH = pl.DeviceIdType.MESH


def plan_hops(groups, which):
    bits = [1 << b for b in range(groups.bit_length() - 1)]
    if len(bits) == 2 and which:
        bits = bits[::-1]
    known = [0]
    steps = []
    for bit in bits:
        steps.append((bit, list(known)))
        known = known + [rel ^ bit for rel in known]
    return steps


def now(value):
    return value() if callable(value) else value


class Links:
    def __init__(self, n_dp, n_mp, send_sems):
        self.n_dp, self.n_mp = n_dp, n_mp
        self.dp = lax.axis_index("dp")
        self.z = lax.axis_index("mp")
        self.core = lax.rem(self.dp, 2)
        self.group = self.dp // 2
        self.send_sems = send_sems
        self.used = 0
        self.open = []

    def barrier(self):
        sem = pltpu.get_barrier_semaphore()
        count = 0
        for cc in range(2):
            for zz in range(self.n_mp):

                @pl.when(jnp.logical_or(cc != self.core, zz != self.z))
                def _(cc=cc, zz=zz):
                    pl.semaphore_signal(
                        sem, inc=1, device_id=(2 * self.group + cc, zz), device_id_type=MESH
                    )

                count += 1
        bit = 1
        while bit < self.n_dp // 2:
            pl.semaphore_signal(
                sem, inc=1, device_id=(self.dp ^ (2 * bit), self.z), device_id_type=MESH
            )
            count += 1
            bit *= 2
        pl.semaphore_wait(sem, count - 1)

    def leaves(self, dp, z, when, may_stay):
        away = None if when is None else now(when)
        if may_stay:
            other = jnp.logical_or(now(dp) != self.dp, now(z) != self.z)
            away = other if away is None else jnp.logical_and(away, other)
        return away

    def copy(self, src, dst, recv_sem, dp, z, slot):
        return pltpu.make_async_remote_copy(
            src_ref=now(src),
            dst_ref=now(dst),
            send_sem=self.send_sems.at[slot],
            recv_sem=recv_sem,
            device_id=(now(dp), now(z)),
            device_id_type=MESH,
        )

    def send(self, src, dst, recv_sem, dp, z, when=None, may_stay=False):
        slot = self.used
        self.used += 1
        away = self.leaves(dp, z, when, may_stay)
        if may_stay:
            stays = jnp.logical_and(now(dp) == self.dp, now(z) == self.z)
            if when is not None:
                stays = jnp.logical_and(now(when), stays)

            @pl.when(stays)
            def _():
                pltpu.make_async_copy(now(src), now(dst), recv_sem).start()

        if away is None:
            self.copy(src, dst, recv_sem, dp, z, slot).start()
        else:

            @pl.when(away)
            def _():
                self.copy(src, dst, recv_sem, dp, z, slot).start()

        def wait():
            self.copy(src, src, self.send_sems.at[slot], self.dp ^ 1, self.z, slot).wait_send()

        entry = (may_stay, when, dp, z, wait)
        self.open.append(entry)
        return entry

    def send_or_keep(self, src, dst, recv_sem, dp, z):
        return self.send(src, dst, recv_sem, dp, z, may_stay=True)

    def send_if(self, condition, src, dst, recv_sem, dp, z):
        return self.send(src, dst, recv_sem, dp, z, when=condition)

    def wait_sent(self, entry):
        entry[4]()
        self.open = [other for other in self.open if other is not entry]

    def arrived(self, src, dst, recv_sem):
        self.copy(src, dst, recv_sem, self.dp ^ 1, self.z, 0).wait_recv()

    def finish(self):
        for may_stay, when, dp, z, wait in self.open:
            away = self.leaves(dp, z, when, may_stay)
            if away is None:
                wait()
            else:
                pl.when(away)(wait)
        self.open = []


def rows_at(index, rows):
    return pl.ds(pl.multiple_of(index * rows, rows), rows)


def exchange_tokens(links, src, dst, sems):
    quarter = src.shape[1]
    for m in range(2):
        links.send_or_keep(
            src.at[m],
            dst.at[rows_at(lax.rem(links.z, 2), quarter), :],
            sems.at[lax.rem(links.z, 2)],
            2 * links.group + links.z // 2,
            2 * m + links.core,
        )


def exchange_tokens_wait(links, src, dst, sems):
    quarter = src.shape[1]
    for s in range(2):
        links.arrived(src.at[0], dst.at[pl.ds(s * quarter, quarter), :], sems.at[s])


class Column:
    def __init__(self, links, src, dst, col_sems, hop_sems):
        self.links, self.src, self.dst = links, src, dst
        self.rows = src.shape[0]
        self.col_sems, self.hop_sems = col_sems, hop_sems
        self.groups = links.n_dp // 2
        self.waited = [set(), set()]

    def start(self):
        k = self.links
        i = lax.rem(k.z, 2)
        home = k.z // 2
        step = 1 - 2 * home
        dst = self.dst.at[i, rows_at(k.dp, self.rows), :]
        sem = self.col_sems.at[i, k.core]
        owner = 2 * k.group + home
        k.send(self.src, dst, sem, owner, k.z + step)
        k.send_if(jnp.logical_or(k.z == 1, k.z == 2), self.src, dst, sem, owner, k.z - step)
        k.send_or_keep(self.src, dst, sem, owner, k.z)

    def piece(self, i, group):
        return self.dst.at[i, rows_at(group, 2 * self.rows), :]

    def hop(self, i, rel, bit):
        k = self.links
        piece = self.piece(i, k.group ^ rel)
        k.send(piece, piece, self.hop_sems.at[i, rel ^ bit], k.dp ^ (2 * bit), k.z)

    def hop_wait(self, i, rel):
        if rel not in self.waited[i]:
            piece = self.piece(i, self.links.group ^ rel)
            self.links.arrived(piece, piece, self.hop_sems.at[i, rel])
            self.waited[i].add(rel)

    def first(self):
        k = self.links
        near = jnp.where(k.core == 0, jnp.minimum(k.z, 1), k.z // 3)
        for turn in range(2):
            i = near if turn == 0 else 1 - near
            for c in range(2):
                block = self.dst.at[i, rows_at(2 * k.group + c, self.rows), :]
                k.arrived(self.src, block, self.col_sems.at[i, c])
            up = jnp.logical_and(k.core == 0, jnp.logical_and(k.z > i, k.z < k.n_mp - 1))
            down = jnp.logical_and(k.core == 1, jnp.logical_and(k.z < 2 + i, k.z > 0))
            onward = jnp.logical_or(up, down)
            for c in range(2):
                block = self.dst.at[i, rows_at(2 * k.group + c, self.rows), :]
                k.send_if(
                    onward, block, block, self.col_sems.at[i, c], k.dp, k.z + 1 - 2 * k.core
                )
            for bit, _ in plan_hops(self.groups, turn):
                self.hop(i, 0, bit)

    def second(self):
        steps = [plan_hops(self.groups, i) for i in range(2)]
        for level in range(1, len(steps[0])):
            for i in range(2):
                bit, known = steps[i][level]
                for rel in known[1:]:
                    self.hop_wait(i, rel)
                    self.hop(i, rel, bit)

    def last(self):
        for i in range(2):
            for rel in range(1, self.groups):
                self.hop_wait(i, rel)


def sends_of_column(n_mp, hops):
    return 3 + 4 + 2 * hops


def forward_kernel(n_dp, n_mp, *refs):
    smallest = refs[3:8]
    qkv_ref = refs[8]
    v_block, q_block = refs[-2:]
    blocks = (v_block, q_block) + tuple(refs[9:12])
    refs = refs[0:3] + blocks + refs[12:]
    (tokens, grads, seg_ref) = refs[0:3]
    (x_out, g_out, h1_out, qkv_out, o_out, lse_out, a_out, mid_out, h2_out) = refs[8:17]
    (act_out, slope_out, f_out, y_out) = refs[17:21]
    w_outs = refs[21:25]
    count_out, vec_ref = refs[25:27]
    weights = refs[27:32]
    (xb, seg_other, h1, qkv, o, lse, a_send, a_recv, a_own, mid) = refs[32:42]
    (h2, act, slope, f_send, f_recv, f_own, y, bias_ref, upb_ref) = refs[42:51]
    (send_sems, col_sems, hop_sems, tok_sems, swap_sems, keep_sems) = refs[51:57]
    smalls, w_qkv, w_out, w_up, w_down = weights
    links = Links(n_dp, n_mp, send_sems)
    half = xb.shape[0]
    length = 2 * half
    tile = half // 2
    other = links.dp + 1 - 2 * links.core
    mine0 = links.core * half
    other0 = (1 - links.core) * half
    kept = []

    def keep(src, dst):
        copy = pltpu.make_async_copy(src, dst, keep_sems.at[len(kept)])
        copy.start()
        kept.append(copy)

    def at(start, rows):
        return pl.ds(pl.multiple_of(start, 16), rows)

    pack_smalls(smallest, v_block)
    for j in range(3):
        width = qkv_ref.shape[2]
        q_block[:, j * width : (j + 1) * width] = qkv_ref[j]
    links.barrier()
    ways = [Column(links, blocks[a], weights[a], col_sems.at[a], hop_sems.at[a]) for a in range(5)]
    v_way, q_way, o_way, u_way, d_way = ways
    v_way.start()
    o_way.start()
    q_way.start()
    links.send(seg_ref, seg_other, swap_sems.at[0], other, links.z)
    v_way.first()
    o_way.first()
    u_way.start()
    q_way.first()
    exchange_tokens(links, tokens, xb, tok_sems.at[0])
    v_way.second()
    o_way.second()
    q_way.second()
    d_way.start()
    u_way.first()
    links.arrived(seg_ref, seg_other, swap_sems.at[0])
    pick = lax.rem(links.core + links.z, 2) == 0
    seg_row = jnp.where(
        pick, seg_ref[pl.ds(links.z // 2, 1), :], seg_other[pl.ds(links.z // 2, 1), :]
    )
    count = jnp.sum((seg_row == 0).astype(jnp.int32), axis=1, keepdims=True)
    count_out[...] = jnp.broadcast_to(count, count_out.shape)
    v_way.last()
    spread_smalls(n_dp, smalls, vec_ref, bias_ref, upb_ref)
    exchange_tokens_wait(links, tokens, xb, tok_sems.at[0])
    keep(xb, x_out)

    def first_norm(t, _):
        rows = at(t * tile, tile)
        unit, _ = stats(xb[rows, :].astype(F32))
        h1[at(mine0 + t * tile, tile), :] = (unit * vec_ref[0:1, :] + vec_ref[4:5, :]).astype(BF)
        return 0

    lax.fori_loop(0, 2, first_norm, 0)
    links.send(h1.at[at(mine0, half), :], h1.at[at(mine0, half), :], swap_sems.at[1], other, links.z)
    q_way.last()
    cols = qkv.shape[2] // 3
    scale_row = jnp.where(
        lax.broadcasted_iota(jnp.int32, (1, 3 * cols), 1) < cols, SCALE, 1.0
    ).astype(F32)

    def project(start):
        def body(t, _):
            rows = at(start + t * tile, tile)
            for i in range(2):
                value = dot_nn(h1[rows, :], w_qkv[i]) + bias_ref[i : i + 1, :]
                qkv[i, rows, :] = (value * scale_row).astype(BF)
            return 0

        lax.fori_loop(0, 2, body, 0)

    keep(w_qkv, w_outs[0])
    project(mine0)
    links.arrived(
        h1.at[at(mine0, half), :], h1.at[at(other0, half), :], swap_sems.at[1]
    )
    project(other0)
    keep(h1, h1_out)
    keep(qkv, qkv_out)
    u_way.second()
    d_way.first()
    exchange_tokens(links, grads, g_out, tok_sems.at[1])
    pairs = cols // 128

    def attend(i):
        def body(j, _):
            attend_pair_fwd(
                qkv.at[i, :, pl.ds(pl.multiple_of(j * 128, 128), 128)],
                qkv.at[i, :, pl.ds(pl.multiple_of((pairs + j) * 128, 128), 128)],
                qkv.at[i, :, pl.ds(pl.multiple_of((2 * pairs + j) * 128, 128), 128)],
                count,
                o.at[i, :, pl.ds(pl.multiple_of(j * 128, 128), 128)],
                lse,
                2 * (i * pairs + j),
            )
            return 0

        lax.fori_loop(0, pairs, body, 0)

    lse[...] = jnp.zeros_like(lse)
    attend(0)
    attend(1)
    d_way.second()
    keep(o, o_out)
    keep(lse, lse_out)
    o_way.last()
    keep(w_out, w_outs[1])

    def out_tile(start):
        return dot_nn(o[0, at(start, tile), :], w_out[0]) + dot_nn(
            o[1, at(start, tile), :], w_out[1]
        )

    def out_theirs(t, _):
        a_send[at(t * tile, tile), :] = out_tile(other0 + t * tile).astype(BF)
        return 0

    def out_ours(t, _):
        a_own[at(t * tile, tile), :] = out_tile(mine0 + t * tile)
        return 0

    lax.fori_loop(0, 2, out_theirs, 0)
    links.send(a_send, a_recv, swap_sems.at[2], other, links.z)
    lax.fori_loop(0, 2, out_ours, 0)
    links.arrived(a_send, a_recv, swap_sems.at[2])

    def middle_norms(t, _):
        rows = at(t * tile, tile)
        branch = a_own[rows, :] + a_recv[rows, :].astype(F32) + vec_ref[8:9, :]
        a_own[rows, :] = branch
        unit, _ = stats(branch)
        middle = xb[rows, :].astype(F32) + unit * vec_ref[1:2, :] + vec_ref[5:6, :]
        mid[rows, :] = middle
        unit, _ = stats(middle)
        h2[at(mine0 + t * tile, tile), :] = (unit * vec_ref[2:3, :] + vec_ref[6:7, :]).astype(BF)
        return 0

    lax.fori_loop(0, 2, middle_norms, 0)
    links.send(h2.at[at(mine0, half), :], h2.at[at(mine0, half), :], swap_sems.at[3], other, links.z)
    keep(a_own, a_out)
    keep(mid, mid_out)
    u_way.last()
    keep(w_up, w_outs[2])

    def up(start):
        def body(t, _):
            rows = at(start + t * tile, tile)
            for i in range(2):
                value, slant = gelu_both(dot_nn(h2[rows, :], w_up[i]) + upb_ref[i : i + 1, :])
                act[i, rows, :] = value
                slope[i, rows, :] = slant
            return 0

        lax.fori_loop(0, 2, body, 0)

    up(mine0)
    links.arrived(h2.at[at(mine0, half), :], h2.at[at(other0, half), :], swap_sems.at[3])
    up(other0)
    keep(h2, h2_out)
    keep(act, act_out)
    keep(slope, slope_out)
    d_way.last()

    def down_tile(start):
        return dot_nn(act[0, at(start, tile), :], w_down[0]) + dot_nn(
            act[1, at(start, tile), :], w_down[1]
        )

    def down_theirs(t, _):
        f_send[at(t * tile, tile), :] = down_tile(other0 + t * tile).astype(BF)
        return 0

    def down_ours(t, _):
        f_own[at(t * tile, tile), :] = down_tile(mine0 + t * tile)
        return 0

    lax.fori_loop(0, 2, down_theirs, 0)
    links.send(f_send, f_recv, swap_sems.at[4], other, links.z)
    lax.fori_loop(0, 2, down_ours, 0)
    keep(w_down, w_outs[3])
    links.arrived(f_send, f_recv, swap_sems.at[4])

    def last_norm(t, _):
        rows = at(t * tile, tile)
        value = f_own[rows, :] + f_recv[rows, :].astype(F32) + vec_ref[9:10, :]
        f_own[rows, :] = value
        unit, _ = stats(value)
        y[rows, :] = (mid[rows, :] + unit * vec_ref[3:4, :] + vec_ref[7:8, :]).astype(BF)
        return 0

    lax.fori_loop(0, 2, last_norm, 0)
    keep(f_own, f_out)
    keep(y, y_out)
    exchange_tokens_wait(links, grads, g_out, tok_sems.at[1])
    for copy in kept:
        copy.wait()
    links.finish()


def pack_smalls(refs, block):
    qv, up, gain, shift, bias = refs
    lanes = block.shape[1]

    def fill(value):
        short = lanes - value.shape[1]
        if not short:
            return value
        return jnp.concatenate([value, jnp.zeros((value.shape[0], short), F32)], axis=1)

    first = qv[...].astype(F32)
    first = jnp.concatenate([first[0:1, :], first[1:2, :]], axis=1)
    rest = [ref[...].astype(F32) for ref in (up, gain, shift, bias)]
    rows = [fill(value) for value in [first] + rest] + [jnp.zeros((4, lanes), F32)]
    block[...] = jnp.concatenate(rows, axis=0).astype(block.dtype)


def spread_smalls(n_dp, smalls, vec_ref, bias_ref, upb_ref):
    width = vec_ref.shape[1]
    slim = width // n_dp
    per_qv = bias_ref.shape[1] // 3 // n_dp
    per_up = upb_ref.shape[1] // n_dp
    row = [
        [smalls[i, 16 * dp : 16 * dp + 16, :].astype(F32) for dp in range(n_dp)] for i in range(2)
    ]
    wide = jnp.concatenate([row[0][dp][2:12, 0:slim] for dp in range(n_dp)], axis=1)
    vec_ref[0:10, :] = wide
    vec_ref[10:16, :] = jnp.zeros((6, width), F32)
    for i in range(2):
        queries = [row[i][dp][0:1, 0:per_qv] for dp in range(n_dp)]
        values = [row[i][dp][0:1, per_qv : 2 * per_qv] for dp in range(n_dp)]
        zeros = [jnp.zeros((1, n_dp * per_qv), F32)]
        bias_ref[i : i + 1, :] = jnp.concatenate(queries + zeros + values, axis=1)
        upb_ref[i : i + 1, :] = jnp.concatenate(
            [row[i][dp][1:2, 0:per_up] for dp in range(n_dp)], axis=1
        )


def attend_pair_fwd(q_ref, k_ref, v_ref, count, o_ref, lse_ref, head0):
    length = q_ref.shape[0]
    lane = lax.broadcasted_iota(jnp.int32, (1, 128), 1)
    for start, stop in row_blocks(length):
        own, before = masks(start, stop, length, count)
        outs = []
        lses = []
        for head in range(2):
            q = jnp.where((lane >= 64) == (head == 1), q_ref[start:stop, :], jnp.zeros((), BF))
            s2 = jnp.where(own, dot_nt(q, k_ref[start:stop, :]), NEG)
            top = jnp.max(s2, axis=-1, keepdims=True)
            if start:
                s1 = dot_nt(q, k_ref[0:start, :])
                if before is not None:
                    s1 = jnp.where(before, s1, NEG)
                top = jnp.maximum(top, jnp.max(s1, axis=-1, keepdims=True))
            e2 = jnp.exp(ALPHA * (s2 - top))
            total = jnp.sum(e2, axis=-1, keepdims=True)
            acc = dot_nn(e2.astype(BF), v_ref[start:stop, :])
            if start:
                e1 = jnp.exp(ALPHA * (s1 - top))
                total = total + jnp.sum(e1, axis=-1, keepdims=True)
                acc = acc + dot_nn(e1.astype(BF), v_ref[0:start, :])
            outs.append(acc / total)
            lses.append(ALPHA * top + jnp.log(total))
        o_ref[start:stop, :] = jnp.where(lane < 64, outs[0], outs[1]).astype(BF)
        kept = jnp.where(lane == head0, lses[0], lse_ref[start:stop, :])
        lse_ref[start:stop, :] = jnp.where(lane == head0 + 1, lses[1], kept)


def forward_all(n_dp, n_mp, tokens, grads, seg_ids, smalls, qkv_weight, blocks):
    groups = n_dp // 2
    hops = groups - 1
    any_spec = pl.BlockSpec(memory_space=pl.ANY)
    vmem = pl.BlockSpec(memory_space=pltpu.VMEM)
    width = tokens.shape[2]
    half = 2 * tokens.shape[1]
    length = 2 * half
    cols3 = 3 * qkv_weight.shape[2]
    cols = cols3 // 3
    ff = n_dp * blocks[2].shape[0]
    shape = jax.ShapeDtypeStruct
    first = [(16, 128), (qkv_weight.shape[1], cols3)]
    full = [(2, n_dp * b[0], b[1]) for b in first + [b.shape for b in blocks]]
    out_shape = [
        shape((half, width), BF),
        shape((half, width), BF),
        shape((length, width), BF),
        shape((2, length, cols3), BF),
        shape((2, length, cols), BF),
        shape((length, 128), F32),
        shape((half, width), F32),
        shape((half, width), F32),
        shape((length, width), BF),
        shape((2, length, ff), BF),
        shape((2, length, ff), BF),
        shape((half, width), F32),
        shape((half, width), BF),
    ] + [shape(f, BF) for f in full[1:]] + [shape((8, 128), jnp.int32), shape((16, width), F32)]
    return pl.pallas_call(
        functools.partial(forward_kernel, n_dp, n_mp),
        in_specs=[any_spec] * 2 + [vmem] * 7 + [any_spec] * 3,
        out_specs=[any_spec] * 17 + [vmem] * 2,
        out_shape=out_shape,
        scratch_shapes=[pltpu.VMEM(f, BF) for f in full]
        + [
            pltpu.VMEM((half, width), BF),
            pltpu.VMEM(seg_ids.shape, jnp.int32),
            pltpu.VMEM((length, width), BF),
            pltpu.VMEM((2, length, cols3), BF),
            pltpu.VMEM((2, length, cols), BF),
            pltpu.VMEM((length, 128), F32),
            pltpu.VMEM((half, width), BF),
            pltpu.VMEM((half, width), BF),
            pltpu.VMEM((half, width), F32),
            pltpu.VMEM((half, width), F32),
            pltpu.VMEM((length, width), BF),
            pltpu.VMEM((2, length, ff), BF),
            pltpu.VMEM((2, length, ff), BF),
            pltpu.VMEM((half, width), BF),
            pltpu.VMEM((half, width), BF),
            pltpu.VMEM((half, width), F32),
            pltpu.VMEM((half, width), BF),
            pltpu.VMEM((2, cols3), F32),
            pltpu.VMEM((2, ff), F32),
            pltpu.SemaphoreType.DMA((9 + 5 * sends_of_column(n_mp, hops),)),
            pltpu.SemaphoreType.DMA((5, 2, 2)),
            pltpu.SemaphoreType.DMA((5, 2, groups)),
            pltpu.SemaphoreType.DMA((2, 2)),
            pltpu.SemaphoreType.DMA((5,)),
            pltpu.SemaphoreType.DMA((17,)),
        ]
        + [pltpu.VMEM(shape_of, BF) for shape_of in first],
        compiler_params=pltpu.CompilerParams(
            collective_id=0, has_side_effects=True, vmem_limit_bytes=60 << 20
        ),
    )(tokens, grads, seg_ids, *smalls, qkv_weight, *blocks)


def attend_pair_bwd(q_ref, k_ref, v_ref, do_ref, lse_ref, head0, count, dk_ref, dv_ref):
    length = q_ref.shape[0]
    lane = lax.broadcasted_iota(jnp.int32, (1, 128), 1)
    dk_ref[...] = jnp.zeros_like(dk_ref)
    dv_ref[...] = jnp.zeros_like(dv_ref)
    zero = jnp.zeros((), BF)
    for start, stop in row_blocks(length):
        own, before = masks(start, stop, length, count)
        dqs = []
        for head in range(2):
            mine = (lane >= 64) == (head == 1)
            q = jnp.where(mine, q_ref[start:stop, :], zero)
            do = jnp.where(mine, do_ref[start:stop, :], zero)
            lse = jnp.sum(
                jnp.where(lane == head0 + head, lse_ref[start:stop, :], 0.0), axis=-1, keepdims=True
            )
            p2 = jnp.where(own, jnp.exp(ALPHA * dot_nt(q, k_ref[start:stop, :]) - lse), 0.0)
            g2 = dot_nt(do, v_ref[start:stop, :])
            delta = jnp.sum(p2 * g2, axis=-1, keepdims=True)
            if start:
                p1 = jnp.exp(ALPHA * dot_nt(q, k_ref[0:start, :]) - lse)
                if before is not None:
                    p1 = jnp.where(before, p1, 0.0)
                g1 = dot_nt(do, v_ref[0:start, :])
                delta = delta + jnp.sum(p1 * g1, axis=-1, keepdims=True)
            ds2 = (ALPHA * p2 * (g2 - delta)).astype(BF)
            dq = dot_nn(ds2, k_ref[start:stop, :])
            dk_ref[start:stop, :] += dot_tn(ds2, q)
            dv_ref[start:stop, :] += dot_tn(p2.astype(BF), do)
            if start:
                ds1 = (ALPHA * p1 * (g1 - delta)).astype(BF)
                dq = dq + dot_nn(ds1, k_ref[0:start, :])
                dk_ref[0:start, :] += dot_tn(ds1, q)
                dv_ref[0:start, :] += dot_tn(p1.astype(BF), do)
            dqs.append(dq)
        q_ref[start:stop, :] = (jnp.where(lane < 64, dqs[0], dqs[1]) * SCALE).astype(BF)
    k_ref[...] = dk_ref[...].astype(BF)
    v_ref[...] = dv_ref[...].astype(BF)


FAR = (1, 3, 4)


class Reduce:
    def __init__(self, links, part, slots, column, merge, slot_sems, column_sems, merge_sems, load):
        self.load, self.near, self.copies = load, [], []
        self.links, self.part, self.slots = links, part, slots
        self.column, self.merge = column, merge
        self.slot_sems, self.column_sems, self.merge_sems = slot_sems, column_sems, merge_sems
        self.groups = links.n_dp // 2
        self.rows = part.shape[1] // links.n_dp
        self.steps = [plan_hops(self.groups, i)[::-1] for i in range(2)]
        self.place = jnp.where(links.core == 0, links.z, links.n_mp - 1 - links.z)
        self.terms = links.n_mp if merge is None else links.n_mp - 1

    def piece(self, i, rel):
        return self.part.at[i, rows_at(self.links.group ^ rel, 2 * self.rows), :]

    def slot(self, i, rel):
        return self.slots.at[i, pl.ds((rel - 1) * 2 * self.rows, 2 * self.rows), :]

    def give(self, i, rel, bit):
        k = self.links
        k.send(
            lambda: self.piece(i, rel),
            lambda: self.slot(i, rel),
            self.slot_sems.at[i, rel],
            k.dp ^ (2 * bit),
            k.z,
        )

    def start(self, i):
        bit, known = self.steps[i][0]
        for rel in known[::-1]:
            self.give(i, rel ^ bit, bit)

    def add(self, i, rel, source):
        tile = min(32, 2 * self.rows)
        base = (self.links.group ^ rel) * 2 * self.rows

        def body(t, _):
            rows = pl.ds(pl.multiple_of(base + t * tile, tile), tile)
            came = source[pl.ds(pl.multiple_of(t * tile, tile), tile), :]
            total = self.part[i, rows, :].astype(F32) + came.astype(F32)
            self.part[i, rows, :] = total.astype(self.part.dtype)
            return 0

        lax.fori_loop(0, 2 * self.rows // tile, body, 0)

    def level(self, i, number):
        k = self.links
        bit, known = self.steps[i][number]
        after = self.steps[i][number + 1][0] if number + 1 < len(self.steps[i]) else 0
        for rel in sorted(known, key=lambda r: not r & after):
            k.arrived(self.piece(i, rel), self.slot(i, rel ^ bit), self.slot_sems.at[i, rel ^ bit])
            self.add(i, rel, self.slot(i, rel ^ bit))
            if rel & after:
                self.give(i, rel, after)
        if not after:
            if self.merge is None:
                self.ship(i, None)
            else:
                k.send(
                    lambda: self.piece(i, 0),
                    self.merge.at[i],
                    self.merge_sems.at[i],
                    k.dp,
                    k.z - 1 + 2 * k.core,
                    when=lambda: self.place == 3,
                )
                self.ship(i, lambda: self.place < 2)

    def ship(self, i, when):
        k = self.links
        slot = k.z if self.merge is None else jnp.where(self.place == 3, 0, k.z - k.core)
        for c in range(2):
            k.send(
                lambda c=c: self.part.at[i, rows_at(2 * k.group + c, self.rows), :],
                lambda slot=slot: self.column.at[slot],
                self.column_sems.at[slot],
                lambda c=c: 2 * k.group + c,
                lambda: 2 * k.core + i,
                when=when,
                may_stay=True,
            )

    def levels(self, number):
        for i in range(2):
            self.level(i, number)

    def merged(self):
        for i in range(2):

            @pl.when(self.place == 2)
            def _(i=i):
                self.links.arrived(self.merge.at[i], self.merge.at[i], self.merge_sems.at[i])
                self.add(i, 0, self.merge.at[i])

            self.ship(i, lambda: self.place == 2)

    def collect(self):
        if self.near:
            return
        for zz in range(self.terms):
            term = self.column.at[zz]
            self.links.arrived(term, term, self.column_sems.at[zz])
            if self.load:
                near = self.slots.at[0, pl.ds(zz * self.rows, self.rows), :]
                self.copies.append(self.load(term, near))
                term = near
            self.near.append(term)

    def total(self, out):
        self.collect()
        for copy in self.copies:
            copy.wait()
        tile = min(32, self.rows)

        def body(t, _):
            rows = pl.ds(pl.multiple_of(t * tile, tile), tile)
            value = self.near[0][rows, :].astype(F32)
            for ref in self.near[1:]:
                value = value + ref[rows, :].astype(F32)
            out[rows, :] = value
            return 0

        lax.fori_loop(0, self.rows // tile, body, 0)


def return_tokens(links, parts, dst, sems):
    quarter = dst.shape[1]
    m = links.z // 2
    for s in range(2):
        links.send_or_keep(
            parts.at[pl.ds(s * quarter, quarter), :],
            dst.at[m],
            sems.at[m],
            2 * links.group + lax.rem(links.z, 2),
            2 * links.core + s,
        )


def return_tokens_wait(links, dst, sems):
    for m in range(2):
        links.arrived(dst.at[m], dst.at[m], sems.at[m])


def backward_kernel(n_dp, n_mp, *refs):
    (y_hbm, g_hbm, x_hbm, a_hbm, mid_hbm, f_hbm, h1_hbm, qkv_hbm, o_hbm, lse_hbm) = refs[0:10]
    (h2_hbm, act_hbm, slope_hbm, wq_hbm, wo_hbm, wu_hbm, wd_hbm, vec_ref, count_ref) = refs[10:19]
    (layer_out, back, q_out, o_out, u_out, d_out, v_out) = refs[19:26]
    fars = refs[26:29]
    refs = refs[:26] + refs[28:]
    parts = refs[27:32]
    slots = refs[32:37]
    columns = list(refs[37:42])
    merges = (None,) + tuple(refs[42:46])
    refs = refs[:42] + refs[46:]
    for a, far in zip(FAR, fars):
        columns[a] = far
    (pair, take, own, own2, g_buf) = refs[42:47]
    refs = refs[:47] + (None,) + refs[47:]
    (act, du, h, wd, wu, lse, dk, dv, vsum, vtake, vqkv, vup) = refs[48:60]
    (send_sems, slot_sems, column_sems, merge_sems, tok_sems, swap_sems, load_sems) = refs[60:67]
    links = Links(n_dp, n_mp, send_sems)
    half = g_buf.shape[0]
    length = 2 * half
    tile = half // 2
    width = g_buf.shape[1]
    other = links.dp + 1 - 2 * links.core
    mine0 = links.core * half
    other0 = (1 - links.core) * half
    cols3 = qkv_hbm.shape[2]
    cols = cols3 // 3
    loads = [0]
    parts = list(parts)
    give = h.at[pl.ds(0, half), :]
    parts[1] = du.at[:, pl.ds(0, width), pl.ds(cols, cols3)]
    if parts[2].dtype == BF:
        parts[2] = wu.at[:, pl.ds(half, cols), :]
    else:
        parts[2] = own2.at[:, pl.ds(0, cols), :]

    def load(src, dst):
        copy = pltpu.make_async_copy(src, dst, load_sems.at[loads[0]])
        loads[0] += 1
        copy.start()
        return copy

    def at(start, rows):
        return pl.ds(pl.multiple_of(start, 16), rows)

    def gain(k):
        return vec_ref[k : k + 1, :]

    f_load = load(f_hbm, own)
    g_load = load(g_hbm, g_buf)
    act_load = load(act_hbm, act)
    wd_load = load(wd_hbm, wd)
    slope_load = load(slope_hbm, du)
    h_load = load(h2_hbm, h)
    wu_load = load(wu_hbm, wu)
    lse_load = load(lse_hbm, lse)
    vsum[...] = jnp.zeros_like(vsum)
    vqkv[...] = jnp.zeros_like(vqkv)
    vup[...] = jnp.zeros_like(vup)
    links.barrier()
    ways = [
        Reduce(
            links,
            parts[a],
            slots[a],
            columns[a],
            merges[a],
            slot_sems.at[a],
            column_sems.at[a],
            merge_sems.at[a],
            load if a in FAR else None,
        )
        for a in range(5)
    ]
    v_way, q_way, o_way, u_way, d_way = ways
    return_tokens(links, y_hbm, layer_out, tok_sems.at[0])

    def norm_grad(value, k, grad):
        unit, inverse = stats(value)
        back, dgain, dshift = norm_back(unit, inverse, gain(k), grad)
        vsum[k : k + 1, :] += dgain[None]
        vsum[4 + k : 5 + k, :] += dshift[None]
        return back

    f_load.wait()
    g_load.wait()

    def last_norm(t, _):
        rows = at(t * tile, tile)
        back = norm_grad(own[rows, :], 3, g_buf[rows, :].astype(F32)).astype(BF)
        vsum[9:10, :] += jnp.sum(back.astype(F32), axis=0, keepdims=True)
        pair[at(mine0 + t * tile, tile), :] = back
        return 0

    lax.fori_loop(0, 2, last_norm, 0)
    ours = pair.at[at(mine0, half), :]
    theirs = pair.at[at(other0, half), :]
    df_send = links.send(ours, ours, swap_sems.at[0], other, links.z)
    act_load.wait()
    links.arrived(ours, theirs, swap_sems.at[0])

    def weight_grad(left, right, part, i):
        step = min(256, left.shape[1])

        def body(t, _):
            lanes = pl.ds(pl.multiple_of(t * step, 128), step)
            rows = pl.ds(pl.multiple_of(t * step, 16), step)
            part[i, rows, :] = dot_tn(left[:, lanes], right[...]).astype(part.dtype)
            return 0

        lax.fori_loop(0, left.shape[1] // step, body, 0)

    for i in range(2):
        weight_grad(act.at[i], pair, parts[4], i)
        d_way.start(i)
    qkv_load = load(qkv_hbm, act.at[:, :, 0:cols3])
    wd_load.wait()
    slope_load.wait()
    h_load.wait()
    for i in range(2):

        def slant(t, _, i=i):
            rows = at(t * tile, tile)
            value = (dot_nt(pair[rows, :], wd[i]) * du[i, rows, :].astype(F32)).astype(BF)
            du[i, rows, :] = value
            vup[i : i + 1, :] += jnp.sum(value.astype(F32), axis=0, keepdims=True)
            return 0

        lax.fori_loop(0, 4, slant, 0)
        weight_grad(h, du.at[i], parts[3], i)
    wq_load = load(wq_hbm, wd.at[:, :, 0:cols3])
    a_load = load(a_hbm.at[pl.ds(0, tile), :], own2.at[0])
    mid_load = load(mid_hbm.at[pl.ds(0, tile), :], own2.at[1])
    wu_load.wait()

    def up_tile(start):
        return dot_nt(du[0, at(start, tile), :], wu[0]) + dot_nt(du[1, at(start, tile), :], wu[1])

    def up_theirs(t, _):
        give[at(t * tile, tile), :] = up_tile(other0 + t * tile).astype(BF)
        return 0

    def up_ours(t, _):
        own[at(t * tile, tile), :] = up_tile(mine0 + t * tile)
        return 0

    lax.fori_loop(0, 2, up_theirs, 0)
    up_send = links.send(give, take, swap_sems.at[1], other, links.z)
    lax.fori_loop(0, 2, up_ours, 0)
    o_load = load(o_hbm, du.at[:, :, 0:cols])
    x_load = load(x_hbm, wu.at[0, pl.ds(0, half), :])
    wo_load = [load(wo_hbm.at[i], wu.at[1, pl.ds(i * cols, cols), :]) for i in range(2)]
    links.wait_sent(df_send)
    links.arrived(give, take, swap_sems.at[1])
    for t in range(2):
        a_load.wait()
        mid_load.wait()
        rows = pl.ds(t * tile, tile)
        grad = own[rows, :] + take[rows, :].astype(F32)
        grad = g_buf[rows, :].astype(F32) + norm_grad(own2[1], 2, grad)
        own[rows, :] = grad
        grad = norm_grad(own2[0], 1, grad).astype(BF)
        vsum[8:9, :] += jnp.sum(grad.astype(F32), axis=0, keepdims=True)
        pair[at(mine0 + t * tile, tile), :] = grad
        if t == 0:
            a_load = load(a_hbm.at[pl.ds(tile, tile), :], own2.at[0])
            mid_load = load(mid_hbm.at[pl.ds(tile, tile), :], own2.at[1])
    links.send(ours, ours, swap_sems.at[2], other, links.z)
    links.wait_sent(up_send)
    h_load = load(h1_hbm, h)
    d_way.levels(0)
    u_way.start(0)
    u_way.start(1)
    o_load.wait()
    qkv_load.wait()
    wo_load[0].wait()
    wo_load[1].wait()
    links.arrived(ours, theirs, swap_sems.at[2])

    def open_heads(t, _):
        rows = at(t * tile, tile)
        for i in range(2):
            value = dot_nt(pair[rows, :], wu[1, i * cols : (i + 1) * cols, :])
            act[i, rows, cols3 : cols3 + cols] = value.astype(BF)
        return 0

    lax.fori_loop(0, 4, open_heads, 0)
    for i in range(2):
        weight_grad(du.at[i, :, 0:cols], pair, parts[2], i)
    lse_load.wait()
    h_load.wait()
    wq_load.wait()
    count = count_ref[0:1, 0:1]
    pairs = cols // 128

    def attend(n, _):
        i = n // pairs
        lanes = lambda base: pl.ds(pl.multiple_of((base + lax.rem(n, pairs)) * 128, 128), 128)
        attend_pair_bwd(
            act.at[i, :, lanes(0)],
            act.at[i, :, lanes(pairs)],
            act.at[i, :, lanes(2 * pairs)],
            act.at[i, :, lanes(3 * pairs)],
            lse,
            2 * n,
            count,
            dk,
            dv,
        )

        @pl.when(n == 0)
        def _():
            d_way.levels(1)

        @pl.when(n == pairs - 1)
        def _():
            weight_grad(h, act.at[0, :, 0:cols3], parts[1], 0)
            d_way.merged()

        @pl.when(n == pairs)
        def _():
            u_way.levels(0)

        return 0

    lax.fori_loop(0, 2 * pairs, attend, 0)
    q_way.start(0)
    weight_grad(h, act.at[1, :, 0:cols3], parts[1], 1)
    q_way.start(1)
    o_way.start(0)
    o_way.start(1)

    def head_tile(start):
        rows = at(start, tile)
        total = None
        for i in range(2):
            value = act[i, rows, 0:cols3]
            vqkv[i : i + 1, :] += jnp.sum(value.astype(F32), axis=0, keepdims=True)
            term = dot_nt(value, wd[i, :, 0:cols3])
            total = term if total is None else total + term
        return total

    def head_theirs(t, _):
        give[at(t * tile, tile), :] = head_tile(other0 + t * tile).astype(BF)
        return 0

    lax.fori_loop(0, 2, head_theirs, 0)
    links.send(give, take, swap_sems.at[3], other, links.z)
    u_way.levels(1)
    x_load.wait()
    links.arrived(give, take, swap_sems.at[3])

    def first_norm(t, _):
        rows = at(t * tile, tile)
        grad = head_tile(mine0 + t * tile) + take[rows, :].astype(F32)
        grad = own[rows, :] + norm_grad(wu[0, rows, :].astype(F32), 0, grad)
        g_buf[rows, :] = grad.astype(BF)
        return 0

    lax.fori_loop(0, 2, first_norm, 0)
    return_tokens(links, g_buf, back, tok_sems.at[1])
    links.send(vsum, vtake, swap_sems.at[4], other, links.z)
    q_way.level(0, 0)
    links.arrived(vsum, vtake, swap_sems.at[4])
    gather_smalls(n_dp, vsum[...] + vtake[...], vqkv, vup, parts[0])
    v_way.start(0)
    v_way.start(1)
    u_way.merged()
    d_way.collect()
    q_way.level(1, 0)
    o_way.levels(0)
    v_way.levels(0)
    d_way.total(d_out)
    v_way.levels(1)
    q_way.levels(1)
    o_way.levels(1)
    u_way.collect()
    u_way.total(u_out)
    q_way.merged()
    o_way.merged()
    o_way.total(o_out)
    return_tokens_wait(links, back, tok_sems.at[1])
    v_way.total(v_out)
    q_way.total(q_out)
    return_tokens_wait(links, layer_out, tok_sems.at[0])
    links.finish()


def gather_smalls(n_dp, total, vqkv, vup, part):
    width = total.shape[1]
    slim = width // n_dp
    per_qv = vqkv.shape[1] // 3 // n_dp
    per_up = vup.shape[1] // n_dp
    lanes = part.shape[2]
    values = 2 * per_qv * n_dp

    def fill(value):
        short = lanes - value.shape[1]
        if not short:
            return value
        return jnp.concatenate([value, jnp.zeros((value.shape[0], short), F32)], axis=1)

    for i in range(2):
        qkv = vqkv[i : i + 1, :]
        up = vup[i : i + 1, :]
        for dp in range(n_dp):
            first = jnp.concatenate(
                [
                    qkv[:, dp * per_qv : (dp + 1) * per_qv],
                    qkv[:, values + dp * per_qv : values + (dp + 1) * per_qv],
                ],
                axis=1,
            )
            base = 16 * dp
            part[i, base : base + 1, :] = fill(first)
            part[i, base + 1 : base + 2, :] = fill(up[:, dp * per_up : (dp + 1) * per_up])
            part[i, base + 2 : base + 12, :] = fill(total[0:10, dp * slim : (dp + 1) * slim])
            part[i, base + 12 : base + 16, :] = jnp.zeros((4, lanes), F32)


def backward_all(n_dp, n_mp, saved, weights, vec, count):
    groups = n_dp // 2
    any_spec = pl.BlockSpec(memory_space=pl.ANY)
    vmem = pl.BlockSpec(memory_space=pltpu.VMEM)
    shape = jax.ShapeDtypeStruct
    half, width = saved[0].shape
    length = 2 * half
    cols3 = saved[7].shape[2]
    cols = cols3 // 3
    ff = saved[11].shape[2]
    full = [(2, n_dp * 16, 128)] + [w.shape for w in weights]
    each = [f[1] // n_dp for f in full]
    kinds = [F32] + [BF if r % 8 == 0 else F32 for r in each[1:]]
    out_shape = [shape((2, half // 2, width), BF)] * 2 + [
        shape((each[a], full[a][2]), F32) for a in (1, 2, 3, 4, 0)
    ]
    out_shape += [shape((n_mp, each[a], full[a][2]), kinds[a]) for a in FAR]
    sends = 4 + 5 + 5 * (2 * (groups - 1) + 10)
    return pl.pallas_call(
        functools.partial(backward_kernel, n_dp, n_mp),
        in_specs=[any_spec] * 17 + [vmem] * 2,
        out_specs=[any_spec] * 2 + [vmem] * 5 + [any_spec] * 3,
        out_shape=out_shape,
        scratch_shapes=[
            pltpu.VMEM((1, 16, 128) if a in (1, 2) else f, k)
            for a, (f, k) in enumerate(zip(full, kinds))
        ]
        + [
            pltpu.VMEM((2, (groups - 1) * 2 * r, f[2]), k) for f, r, k in zip(full, each, kinds)
        ]
        + [
            pltpu.VMEM((n_mp, 16 if a in FAR else r, f[2]), k)
            for a, (f, r, k) in enumerate(zip(full, each, kinds))
        ]
        + [
            pltpu.VMEM((2, 2 * r, f[2]), k) for f, r, k in zip(full[1:], each[1:], kinds[1:])
        ]
        + [
            pltpu.VMEM((length, width), BF),
            pltpu.VMEM((half, width), BF),
            pltpu.VMEM((half, width), F32),
            pltpu.VMEM((2, half // 2, width), F32),
            pltpu.VMEM((half, width), BF),
            pltpu.VMEM((2, length, ff), BF),
            pltpu.VMEM((2, length, ff), BF),
            pltpu.VMEM((length, width), BF),
            pltpu.VMEM((2, ff, width), BF),
            pltpu.VMEM((2, width, ff), BF),
            pltpu.VMEM((length, 128), F32),
            pltpu.VMEM((length, 128), F32),
            pltpu.VMEM((length, 128), F32),
            pltpu.VMEM((16, width), F32),
            pltpu.VMEM((16, width), F32),
            pltpu.VMEM((2, cols3), F32),
            pltpu.VMEM((2, ff), F32),
            pltpu.SemaphoreType.DMA((sends,)),
            pltpu.SemaphoreType.DMA((5, 2, groups)),
            pltpu.SemaphoreType.DMA((5, n_mp)),
            pltpu.SemaphoreType.DMA((5, 2)),
            pltpu.SemaphoreType.DMA((2, 2)),
            pltpu.SemaphoreType.DMA((5,)),
            pltpu.SemaphoreType.DMA((19 + len(FAR) * n_mp,)),
        ],
        compiler_params=pltpu.CompilerParams(
            collective_id=1, has_side_effects=True, vmem_limit_bytes=61 << 20
        ),
    )(*saved, *weights, vec, count)[:7]


def finish_kernel(*refs):
    far = refs[0:7]
    (layer_out, grad_out, q_out, qv_out, o_out, u_out, up_out, d_out) = refs[7:15]
    gain_out, shift_out, bias_out = refs[15:18]
    near, sems = refs[18:25], refs[25]
    copies = [
        pltpu.make_async_copy(a, b, sems.at[n]) for n, (a, b) in enumerate(zip(far, near))
    ]
    for copy in copies:
        copy.start()
    for copy in copies:
        copy.wait()
    layer, back, q, o, u, d, v = near
    layer_out[...] = layer[...]
    grad_out[...] = back[...].astype(F32)
    cols = q.shape[1] // 3
    for j in range(3):
        q_out[j] = q[:, j * cols : (j + 1) * cols]
    per = qv_out.shape[1]
    qv_out[0:1, :] = v[0:1, 0:per]
    qv_out[1:2, :] = v[0:1, per : 2 * per]
    o_out[...] = o[...]
    u_out[...] = u[...]
    up_out[...] = v[1:2, 0 : up_out.shape[1]]
    d_out[...] = d[...]
    slim = gain_out.shape[1]
    gain_out[...] = v[2:6, 0:slim]
    shift_out[...] = v[6:10, 0:slim]
    bias_out[...] = v[10:12, 0:slim]


def finish_all(arrays, per_qv, per_up, slim):
    layer, back, q, o, u, d, v = arrays
    far = pl.BlockSpec(memory_space=pl.ANY)
    vmem = pl.BlockSpec(memory_space=pltpu.VMEM)
    shape = jax.ShapeDtypeStruct
    return pl.pallas_call(
        finish_kernel,
        in_specs=[far] * 7,
        out_specs=[vmem] * 11,
        out_shape=[
            shape(layer.shape, BF),
            shape(back.shape, F32),
            shape((3, q.shape[0], q.shape[1] // 3), F32),
            shape((2, per_qv), F32),
            shape(o.shape, F32),
            shape(u.shape, F32),
            shape((1, per_up), F32),
            shape(d.shape, F32),
            shape((4, slim), F32),
            shape((4, slim), F32),
            shape((2, slim), F32),
        ],
        scratch_shapes=[pltpu.VMEM(a.shape, a.dtype) for a in arrays]
        + [pltpu.SemaphoreType.DMA((7,))],
        compiler_params=pltpu.CompilerParams(vmem_limit_bytes=60 << 20),
    )(*arrays)


def build(n_dp, n_mp):
    def on_device(
        tokens,
        seg_ids,
        qkv_weight,
        qv_bias,
        out_weight,
        up_weight,
        up_bias,
        down_weight,
        norm_gain,
        norm_bias,
        branch_bias,
        out_grad,
    ):
        (
            x,
            grad_y,
            h1,
            qkvs,
            attended,
            log_sums,
            branch,
            middle,
            h2,
            acts,
            slopes,
            ffn_out,
            out_rows,
            w_qkv,
            w_out,
            w_up,
            w_down,
            count,
            vec,
        ) = forward_all(
            n_dp,
            n_mp,
            tokens,
            out_grad,
            seg_ids,
            [qv_bias, up_bias.reshape(1, -1), norm_gain, norm_bias, branch_bias],
            qkv_weight,
            [out_weight, up_weight, down_weight],
        )
        saved = [
            out_rows,
            grad_y,
            x,
            branch,
            middle,
            ffn_out,
            h1,
            qkvs,
            attended,
            log_sums,
            h2,
            acts,
            slopes,
        ]
        sums = backward_all(n_dp, n_mp, saved, [w_qkv, w_out, w_up, w_down], vec, count)
        outs = list(finish_all(sums, qv_bias.shape[1], up_bias.shape[0], norm_gain.shape[1]))
        outs[6] = outs[6].reshape(-1)
        return tuple(outs)

    return on_device


def solution(mesh):
    n_dp, n_mp = mesh.shape["dp"], mesh.shape["mp"]
    in_specs = (
        P(None, ("dp", "mp"), None),
        P(None, "dp"),
        P(None, "dp", "mp"),
        P(None, ("mp", "dp")),
        P(("mp", "dp"), None),
        P("dp", "mp"),
        P(("mp", "dp")),
        P(("mp", "dp"), None),
        P(None, "dp"),
        P(None, "dp"),
        P(None, "dp"),
        P(None, ("dp", "mp"), None),
    )
    out_specs = (
        P(None, ("dp", "mp"), None),
        P(None, ("dp", "mp"), None),
        P(None, "dp", "mp"),
        P(None, ("mp", "dp")),
        P(("mp", "dp"), None),
        P("dp", "mp"),
        P(("mp", "dp")),
        P(("mp", "dp"), None),
        P(None, "dp"),
        P(None, "dp"),
        P(None, "dp"),
    )
    return jax.shard_map(
        build(n_dp, n_mp), mesh=mesh, in_specs=in_specs, out_specs=out_specs, check_vma=False
    )
```

```python
import functools
import math

import jax
import jax.numpy as jnp
from jax import lax
from jax.experimental import pallas as pl
from jax.experimental.pallas import tpu as pltpu
from jax.sharding import PartitionSpec as P

HEAD_DIM = 64
CAPTION = 64
ALPHA = 32.0
EPS = 1e-05
SCALE = 1.0 / (ALPHA * math.sqrt(HEAD_DIM))
NEG = -1e30
BF = jnp.bfloat16
F32 = jnp.float32


def stats(value):
    mean = jnp.mean(value, axis=-1, keepdims=True)
    centred = value - mean
    inverse = lax.rsqrt(jnp.mean(centred * centred, axis=-1, keepdims=True) + EPS)
    return centred * inverse, inverse


def norm_back(unit, inverse, gain, grad):
    scaled = grad * gain
    grad_in = inverse * (
        scaled
        - jnp.mean(scaled, axis=-1, keepdims=True)
        - unit * jnp.mean(scaled * unit, axis=-1, keepdims=True)
    )
    return grad_in, jnp.sum(grad * unit, axis=0), jnp.sum(grad, axis=0)


def gelu_both(value):
    cdf = 0.5 * (1.0 + lax.erf(value * (1.0 / math.sqrt(2.0))))
    pdf = jnp.exp(-0.5 * value * value) * (1.0 / math.sqrt(2.0 * math.pi))
    return (value * cdf).astype(BF), (cdf + value * pdf).astype(BF)


def dot_nt(a, b):
    return lax.dot_general(a, b, (((1,), (1,)), ((), ())), preferred_element_type=F32)


def dot_tn(a, b):
    return lax.dot_general(a, b, (((0,), (0,)), ((), ())), preferred_element_type=F32)


def dot_nn(a, b):
    return lax.dot_general(a, b, (((1,), (0,)), ((), ())), preferred_element_type=F32)


def row_blocks(length):
    body = length - CAPTION
    cuts = list(range(0, body, 256)) + [body, length]
    return list(zip(cuts[:-1], cuts[1:]))


def masks(start, stop, length, count):
    rows = stop - start
    query = lax.broadcasted_iota(jnp.int32, (rows, 1), 0)
    own = query >= lax.broadcasted_iota(jnp.int32, (1, rows), 1)
    if stop < length:
        return own, None
    real = query + start < count
    same = real == (lax.broadcasted_iota(jnp.int32, (1, rows), 1) + start < count)
    before = real == (lax.broadcasted_iota(jnp.int32, (1, start), 1) < count)
    return jnp.logical_and(own, same), before


MESH = pl.DeviceIdType.MESH


def plan_hops(groups, which):
    bits = [1 << b for b in range(groups.bit_length() - 1)]
    if len(bits) == 2 and which:
        bits = bits[::-1]
    known = [0]
    steps = []
    for bit in bits:
        steps.append((bit, list(known)))
        known = known + [rel ^ bit for rel in known]
    return steps


def now(value):
    return value() if callable(value) else value


class Links:
    def __init__(self, n_dp, n_mp, send_sems):
        self.n_dp, self.n_mp = n_dp, n_mp
        self.dp = lax.axis_index("dp")
        self.z = lax.axis_index("mp")
        self.core = lax.rem(self.dp, 2)
        self.group = self.dp // 2
        self.send_sems = send_sems
        self.used = 0
        self.open = []

    def barrier(self):
        sem = pltpu.get_barrier_semaphore()
        count = 0
        for cc in range(2):
            for zz in range(self.n_mp):

                @pl.when(jnp.logical_or(cc != self.core, zz != self.z))
                def _(cc=cc, zz=zz):
                    pl.semaphore_signal(
                        sem, inc=1, device_id=(2 * self.group + cc, zz), device_id_type=MESH
                    )

                count += 1
        bit = 1
        while bit < self.n_dp // 2:
            pl.semaphore_signal(
                sem, inc=1, device_id=(self.dp ^ (2 * bit), self.z), device_id_type=MESH
            )
            count += 1
            bit *= 2
        pl.semaphore_wait(sem, count - 1)

    def leaves(self, dp, z, when, may_stay):
        away = None if when is None else now(when)
        if may_stay:
            other = jnp.logical_or(now(dp) != self.dp, now(z) != self.z)
            away = other if away is None else jnp.logical_and(away, other)
        return away

    def copy(self, src, dst, recv_sem, dp, z, slot):
        return pltpu.make_async_remote_copy(
            src_ref=now(src),
            dst_ref=now(dst),
            send_sem=self.send_sems.at[slot],
            recv_sem=recv_sem,
            device_id=(now(dp), now(z)),
            device_id_type=MESH,
        )

    def send(self, src, dst, recv_sem, dp, z, when=None, may_stay=False):
        slot = self.used
        self.used += 1
        away = self.leaves(dp, z, when, may_stay)
        if may_stay:
            stays = jnp.logical_and(now(dp) == self.dp, now(z) == self.z)
            if when is not None:
                stays = jnp.logical_and(now(when), stays)

            @pl.when(stays)
            def _():
                pltpu.make_async_copy(now(src), now(dst), recv_sem).start()

        if away is None:
            self.copy(src, dst, recv_sem, dp, z, slot).start()
        else:

            @pl.when(away)
            def _():
                self.copy(src, dst, recv_sem, dp, z, slot).start()

        def wait():
            self.copy(src, src, self.send_sems.at[slot], self.dp ^ 1, self.z, slot).wait_send()

        entry = (may_stay, when, dp, z, wait)
        self.open.append(entry)
        return entry

    def send_or_keep(self, src, dst, recv_sem, dp, z):
        return self.send(src, dst, recv_sem, dp, z, may_stay=True)

    def send_if(self, condition, src, dst, recv_sem, dp, z):
        return self.send(src, dst, recv_sem, dp, z, when=condition)

    def wait_sent(self, entry):
        entry[4]()
        self.open = [other for other in self.open if other is not entry]

    def arrived(self, src, dst, recv_sem):
        self.copy(src, dst, recv_sem, self.dp ^ 1, self.z, 0).wait_recv()

    def finish(self):
        for may_stay, when, dp, z, wait in self.open:
            away = self.leaves(dp, z, when, may_stay)
            if away is None:
                wait()
            else:
                pl.when(away)(wait)
        self.open = []


def rows_at(index, rows):
    return pl.ds(pl.multiple_of(index * rows, rows), rows)


def exchange_tokens(links, src, dst, sems):
    quarter = src.shape[1]
    for m in range(2):
        links.send_or_keep(
            src.at[m],
            dst.at[rows_at(lax.rem(links.z, 2), quarter), :],
            sems.at[lax.rem(links.z, 2)],
            2 * links.group + links.z // 2,
            2 * m + links.core,
        )


def exchange_tokens_wait(links, src, dst, sems):
    quarter = src.shape[1]
    for s in range(2):
        links.arrived(src.at[0], dst.at[pl.ds(s * quarter, quarter), :], sems.at[s])


class Column:
    def __init__(self, links, src, dst, col_sems, hop_sems):
        self.links, self.src, self.dst = links, src, dst
        self.rows = src.shape[0]
        self.col_sems, self.hop_sems = col_sems, hop_sems
        self.groups = links.n_dp // 2
        self.waited = [set(), set()]

    def start(self):
        k = self.links
        i = lax.rem(k.z, 2)
        home = k.z // 2
        step = 1 - 2 * home
        dst = self.dst.at[i, rows_at(k.dp, self.rows), :]
        sem = self.col_sems.at[i, k.core]
        owner = 2 * k.group + home
        k.send(self.src, dst, sem, owner, k.z + step)
        k.send_if(jnp.logical_or(k.z == 1, k.z == 2), self.src, dst, sem, owner, k.z - step)
        k.send_or_keep(self.src, dst, sem, owner, k.z)

    def piece(self, i, group):
        return self.dst.at[i, rows_at(group, 2 * self.rows), :]

    def hop(self, i, rel, bit):
        k = self.links
        piece = self.piece(i, k.group ^ rel)
        k.send(piece, piece, self.hop_sems.at[i, rel ^ bit], k.dp ^ (2 * bit), k.z)

    def hop_wait(self, i, rel):
        if rel not in self.waited[i]:
            piece = self.piece(i, self.links.group ^ rel)
            self.links.arrived(piece, piece, self.hop_sems.at[i, rel])
            self.waited[i].add(rel)

    def first(self):
        k = self.links
        near = jnp.where(k.core == 0, jnp.minimum(k.z, 1), k.z // 3)
        for turn in range(2):
            i = near if turn == 0 else 1 - near
            for c in range(2):
                block = self.dst.at[i, rows_at(2 * k.group + c, self.rows), :]
                k.arrived(self.src, block, self.col_sems.at[i, c])
            up = jnp.logical_and(k.core == 0, jnp.logical_and(k.z > i, k.z < k.n_mp - 1))
            down = jnp.logical_and(k.core == 1, jnp.logical_and(k.z < 2 + i, k.z > 0))
            onward = jnp.logical_or(up, down)
            for c in range(2):
                block = self.dst.at[i, rows_at(2 * k.group + c, self.rows), :]
                k.send_if(
                    onward, block, block, self.col_sems.at[i, c], k.dp, k.z + 1 - 2 * k.core
                )
            for bit, _ in plan_hops(self.groups, turn):
                self.hop(i, 0, bit)

    def second(self):
        steps = [plan_hops(self.groups, i) for i in range(2)]
        for level in range(1, len(steps[0])):
            for i in range(2):
                bit, known = steps[i][level]
                for rel in known[1:]:
                    self.hop_wait(i, rel)
                    self.hop(i, rel, bit)

    def last(self):
        for i in range(2):
            for rel in range(1, self.groups):
                self.hop_wait(i, rel)


def sends_of_column(n_mp, hops):
    return 3 + 4 + 2 * hops


def forward_kernel(n_dp, n_mp, *refs):
    smallest = refs[3:8]
    qkv_ref = refs[8]
    v_block, q_block = refs[-2:]
    blocks = (v_block, q_block) + tuple(refs[9:12])
    refs = refs[0:3] + blocks + refs[12:]
    (tokens, grads, seg_ref) = refs[0:3]
    (x_out, g_out, h1_out, qkv_out, o_out, lse_out, a_out, mid_out, h2_out) = refs[8:17]
    (act_out, slope_out, f_out, y_out) = refs[17:21]
    w_outs = refs[21:25]
    count_out, vec_ref = refs[25:27]
    weights = refs[27:32]
    (xb, seg_other, h1, qkv, o, lse, a_send, a_recv, a_own, mid) = refs[32:42]
    (h2, act, slope, f_send, f_recv, f_own, y, bias_ref, upb_ref) = refs[42:51]
    (send_sems, col_sems, hop_sems, tok_sems, swap_sems, keep_sems) = refs[51:57]
    smalls, w_qkv, w_out, w_up, w_down = weights
    links = Links(n_dp, n_mp, send_sems)
    half = xb.shape[0]
    length = 2 * half
    tile = half // 2
    other = links.dp + 1 - 2 * links.core
    mine0 = links.core * half
    other0 = (1 - links.core) * half
    kept = []

    def keep(src, dst):
        copy = pltpu.make_async_copy(src, dst, keep_sems.at[len(kept)])
        copy.start()
        kept.append(copy)

    def at(start, rows):
        return pl.ds(pl.multiple_of(start, 16), rows)

    pack_smalls(smallest, v_block)
    for j in range(3):
        width = qkv_ref.shape[2]
        q_block[:, j * width : (j + 1) * width] = qkv_ref[j]
    links.barrier()
    ways = [Column(links, blocks[a], weights[a], col_sems.at[a], hop_sems.at[a]) for a in range(5)]
    v_way, q_way, o_way, u_way, d_way = ways
    v_way.start()
    o_way.start()
    q_way.start()
    links.send(seg_ref, seg_other, swap_sems.at[0], other, links.z)
    v_way.first()
    o_way.first()
    u_way.start()
    q_way.first()
    exchange_tokens(links, tokens, xb, tok_sems.at[0])
    v_way.second()
    o_way.second()
    q_way.second()
    d_way.start()
    u_way.first()
    links.arrived(seg_ref, seg_other, swap_sems.at[0])
    pick = lax.rem(links.core + links.z, 2) == 0
    seg_row = jnp.where(
        pick, seg_ref[pl.ds(links.z // 2, 1), :], seg_other[pl.ds(links.z // 2, 1), :]
    )
    count = jnp.sum((seg_row == 0).astype(jnp.int32), axis=1, keepdims=True)
    count_out[...] = jnp.broadcast_to(count, count_out.shape)
    v_way.last()
    spread_smalls(n_dp, smalls, vec_ref, bias_ref, upb_ref)
    exchange_tokens_wait(links, tokens, xb, tok_sems.at[0])
    keep(xb, x_out)

    def first_norm(t, _):
        rows = at(t * tile, tile)
        unit, _ = stats(xb[rows, :].astype(F32))
        h1[at(mine0 + t * tile, tile), :] = (unit * vec_ref[0:1, :] + vec_ref[4:5, :]).astype(BF)
        return 0

    lax.fori_loop(0, 2, first_norm, 0)
    links.send(h1.at[at(mine0, half), :], h1.at[at(mine0, half), :], swap_sems.at[1], other, links.z)
    q_way.last()
    cols = qkv.shape[2] // 3
    scale_row = jnp.where(
        lax.broadcasted_iota(jnp.int32, (1, 3 * cols), 1) < cols, SCALE, 1.0
    ).astype(F32)

    def project(start):
        def body(t, _):
            rows = at(start + t * tile, tile)
            for i in range(2):
                value = dot_nn(h1[rows, :], w_qkv[i]) + bias_ref[i : i + 1, :]
                qkv[i, rows, :] = (value * scale_row).astype(BF)
            return 0

        lax.fori_loop(0, 2, body, 0)

    keep(w_qkv, w_outs[0])
    project(mine0)
    links.arrived(
        h1.at[at(mine0, half), :], h1.at[at(other0, half), :], swap_sems.at[1]
    )
    project(other0)
    keep(h1, h1_out)
    keep(qkv, qkv_out)
    u_way.second()
    d_way.first()
    exchange_tokens(links, grads, g_out, tok_sems.at[1])
    pairs = cols // 128

    def attend(i):
        def body(j, _):
            attend_pair_fwd(
                qkv.at[i, :, pl.ds(pl.multiple_of(j * 128, 128), 128)],
                qkv.at[i, :, pl.ds(pl.multiple_of((pairs + j) * 128, 128), 128)],
                qkv.at[i, :, pl.ds(pl.multiple_of((2 * pairs + j) * 128, 128), 128)],
                count,
                o.at[i, :, pl.ds(pl.multiple_of(j * 128, 128), 128)],
                lse,
                2 * (i * pairs + j),
            )
            return 0

        lax.fori_loop(0, pairs, body, 0)

    lse[...] = jnp.zeros_like(lse)
    attend(0)
    attend(1)
    d_way.second()
    keep(o, o_out)
    keep(lse, lse_out)
    o_way.last()
    keep(w_out, w_outs[1])

    def out_tile(start):
        return dot_nn(o[0, at(start, tile), :], w_out[0]) + dot_nn(
            o[1, at(start, tile), :], w_out[1]
        )

    def out_theirs(t, _):
        a_send[at(t * tile, tile), :] = out_tile(other0 + t * tile).astype(BF)
        return 0

    def out_ours(t, _):
        a_own[at(t * tile, tile), :] = out_tile(mine0 + t * tile)
        return 0

    lax.fori_loop(0, 2, out_theirs, 0)
    links.send(a_send, a_recv, swap_sems.at[2], other, links.z)
    lax.fori_loop(0, 2, out_ours, 0)
    links.arrived(a_send, a_recv, swap_sems.at[2])

    def middle_norms(t, _):
        rows = at(t * tile, tile)
        branch = a_own[rows, :] + a_recv[rows, :].astype(F32) + vec_ref[8:9, :]
        a_own[rows, :] = branch
        unit, _ = stats(branch)
        middle = xb[rows, :].astype(F32) + unit * vec_ref[1:2, :] + vec_ref[5:6, :]
        mid[rows, :] = middle
        unit, _ = stats(middle)
        h2[at(mine0 + t * tile, tile), :] = (unit * vec_ref[2:3, :] + vec_ref[6:7, :]).astype(BF)
        return 0

    lax.fori_loop(0, 2, middle_norms, 0)
    links.send(h2.at[at(mine0, half), :], h2.at[at(mine0, half), :], swap_sems.at[3], other, links.z)
    keep(a_own, a_out)
    keep(mid, mid_out)
    u_way.last()
    keep(w_up, w_outs[2])

    def up(start):
        def body(t, _):
            rows = at(start + t * tile, tile)
            for i in range(2):
                value, slant = gelu_both(dot_nn(h2[rows, :], w_up[i]) + upb_ref[i : i + 1, :])
                act[i, rows, :] = value
                slope[i, rows, :] = slant
            return 0

        lax.fori_loop(0, 2, body, 0)

    up(mine0)
    links.arrived(h2.at[at(mine0, half), :], h2.at[at(other0, half), :], swap_sems.at[3])
    up(other0)
    keep(h2, h2_out)
    keep(act, act_out)
    keep(slope, slope_out)
    d_way.last()

    def down_tile(start):
        return dot_nn(act[0, at(start, tile), :], w_down[0]) + dot_nn(
            act[1, at(start, tile), :], w_down[1]
        )

    def down_theirs(t, _):
        f_send[at(t * tile, tile), :] = down_tile(other0 + t * tile).astype(BF)
        return 0

    def down_ours(t, _):
        f_own[at(t * tile, tile), :] = down_tile(mine0 + t * tile)
        return 0

    lax.fori_loop(0, 2, down_theirs, 0)
    links.send(f_send, f_recv, swap_sems.at[4], other, links.z)
    lax.fori_loop(0, 2, down_ours, 0)
    keep(w_down, w_outs[3])
    links.arrived(f_send, f_recv, swap_sems.at[4])

    def last_norm(t, _):
        rows = at(t * tile, tile)
        value = f_own[rows, :] + f_recv[rows, :].astype(F32) + vec_ref[9:10, :]
        f_own[rows, :] = value
        unit, _ = stats(value)
        y[rows, :] = (mid[rows, :] + unit * vec_ref[3:4, :] + vec_ref[7:8, :]).astype(BF)
        return 0

    lax.fori_loop(0, 2, last_norm, 0)
    keep(f_own, f_out)
    keep(y, y_out)
    exchange_tokens_wait(links, grads, g_out, tok_sems.at[1])
    for copy in kept:
        copy.wait()
    links.finish()


def pack_smalls(refs, block):
    qv, up, gain, shift, bias = refs
    lanes = block.shape[1]

    def fill(value):
        short = lanes - value.shape[1]
        if not short:
            return value
        return jnp.concatenate([value, jnp.zeros((value.shape[0], short), F32)], axis=1)

    first = qv[...].astype(F32)
    first = jnp.concatenate([first[0:1, :], first[1:2, :]], axis=1)
    rest = [ref[...].astype(F32) for ref in (up, gain, shift, bias)]
    rows = [fill(value) for value in [first] + rest] + [jnp.zeros((4, lanes), F32)]
    block[...] = jnp.concatenate(rows, axis=0).astype(block.dtype)


def spread_smalls(n_dp, smalls, vec_ref, bias_ref, upb_ref):
    width = vec_ref.shape[1]
    slim = width // n_dp
    per_qv = bias_ref.shape[1] // 3 // n_dp
    per_up = upb_ref.shape[1] // n_dp
    row = [
        [smalls[i, 16 * dp : 16 * dp + 16, :].astype(F32) for dp in range(n_dp)] for i in range(2)
    ]
    wide = jnp.concatenate([row[0][dp][2:12, 0:slim] for dp in range(n_dp)], axis=1)
    vec_ref[0:10, :] = wide
    vec_ref[10:16, :] = jnp.zeros((6, width), F32)
    for i in range(2):
        queries = [row[i][dp][0:1, 0:per_qv] for dp in range(n_dp)]
        values = [row[i][dp][0:1, per_qv : 2 * per_qv] for dp in range(n_dp)]
        zeros = [jnp.zeros((1, n_dp * per_qv), F32)]
        bias_ref[i : i + 1, :] = jnp.concatenate(queries + zeros + values, axis=1)
        upb_ref[i : i + 1, :] = jnp.concatenate(
            [row[i][dp][1:2, 0:per_up] for dp in range(n_dp)], axis=1
        )


def attend_pair_fwd(q_ref, k_ref, v_ref, count, o_ref, lse_ref, head0):
    length = q_ref.shape[0]
    lane = lax.broadcasted_iota(jnp.int32, (1, 128), 1)
    for start, stop in row_blocks(length):
        own, before = masks(start, stop, length, count)
        outs = []
        lses = []
        for head in range(2):
            q = jnp.where((lane >= 64) == (head == 1), q_ref[start:stop, :], jnp.zeros((), BF))
            s2 = jnp.where(own, dot_nt(q, k_ref[start:stop, :]), NEG)
            top = jnp.max(s2, axis=-1, keepdims=True)
            if start:
                s1 = dot_nt(q, k_ref[0:start, :])
                if before is not None:
                    s1 = jnp.where(before, s1, NEG)
                top = jnp.maximum(top, jnp.max(s1, axis=-1, keepdims=True))
            e2 = jnp.exp(ALPHA * (s2 - top))
            total = jnp.sum(e2, axis=-1, keepdims=True)
            acc = dot_nn(e2.astype(BF), v_ref[start:stop, :])
            if start:
                e1 = jnp.exp(ALPHA * (s1 - top))
                total = total + jnp.sum(e1, axis=-1, keepdims=True)
                acc = acc + dot_nn(e1.astype(BF), v_ref[0:start, :])
            outs.append(acc / total)
            lses.append(ALPHA * top + jnp.log(total))
        o_ref[start:stop, :] = jnp.where(lane < 64, outs[0], outs[1]).astype(BF)
        kept = jnp.where(lane == head0, lses[0], lse_ref[start:stop, :])
        lse_ref[start:stop, :] = jnp.where(lane == head0 + 1, lses[1], kept)


def forward_all(n_dp, n_mp, tokens, grads, seg_ids, smalls, qkv_weight, blocks):
    groups = n_dp // 2
    hops = groups - 1
    any_spec = pl.BlockSpec(memory_space=pl.ANY)
    vmem = pl.BlockSpec(memory_space=pltpu.VMEM)
    width = tokens.shape[2]
    half = 2 * tokens.shape[1]
    length = 2 * half
    cols3 = 3 * qkv_weight.shape[2]
    cols = cols3 // 3
    ff = n_dp * blocks[2].shape[0]
    shape = jax.ShapeDtypeStruct
    first = [(16, 128), (qkv_weight.shape[1], cols3)]
    full = [(2, n_dp * b[0], b[1]) for b in first + [b.shape for b in blocks]]
    out_shape = [
        shape((half, width), BF),
        shape((half, width), BF),
        shape((length, width), BF),
        shape((2, length, cols3), BF),
        shape((2, length, cols), BF),
        shape((length, 128), F32),
        shape((half, width), F32),
        shape((half, width), F32),
        shape((length, width), BF),
        shape((2, length, ff), BF),
        shape((2, length, ff), BF),
        shape((half, width), F32),
        shape((half, width), BF),
    ] + [shape(f, BF) for f in full[1:]] + [shape((8, 128), jnp.int32), shape((16, width), F32)]
    return pl.pallas_call(
        functools.partial(forward_kernel, n_dp, n_mp),
        in_specs=[any_spec] * 2 + [vmem] * 7 + [any_spec] * 3,
        out_specs=[any_spec] * 17 + [vmem] * 2,
        out_shape=out_shape,
        scratch_shapes=[pltpu.VMEM(f, BF) for f in full]
        + [
            pltpu.VMEM((half, width), BF),
            pltpu.VMEM(seg_ids.shape, jnp.int32),
            pltpu.VMEM((length, width), BF),
            pltpu.VMEM((2, length, cols3), BF),
            pltpu.VMEM((2, length, cols), BF),
            pltpu.VMEM((length, 128), F32),
            pltpu.VMEM((half, width), BF),
            pltpu.VMEM((half, width), BF),
            pltpu.VMEM((half, width), F32),
            pltpu.VMEM((half, width), F32),
            pltpu.VMEM((length, width), BF),
            pltpu.VMEM((2, length, ff), BF),
            pltpu.VMEM((2, length, ff), BF),
            pltpu.VMEM((half, width), BF),
            pltpu.VMEM((half, width), BF),
            pltpu.VMEM((half, width), F32),
            pltpu.VMEM((half, width), BF),
            pltpu.VMEM((2, cols3), F32),
            pltpu.VMEM((2, ff), F32),
            pltpu.SemaphoreType.DMA((9 + 5 * sends_of_column(n_mp, hops),)),
            pltpu.SemaphoreType.DMA((5, 2, 2)),
            pltpu.SemaphoreType.DMA((5, 2, groups)),
            pltpu.SemaphoreType.DMA((2, 2)),
            pltpu.SemaphoreType.DMA((5,)),
            pltpu.SemaphoreType.DMA((17,)),
        ]
        + [pltpu.VMEM(shape_of, BF) for shape_of in first],
        compiler_params=pltpu.CompilerParams(
            collective_id=0, has_side_effects=True, vmem_limit_bytes=60 << 20
        ),
    )(tokens, grads, seg_ids, *smalls, qkv_weight, *blocks)


def attend_pair_bwd(q_ref, k_ref, v_ref, do_ref, lse_ref, head0, count, dk_ref, dv_ref):
    length = q_ref.shape[0]
    lane = lax.broadcasted_iota(jnp.int32, (1, 128), 1)
    dk_ref[...] = jnp.zeros_like(dk_ref)
    dv_ref[...] = jnp.zeros_like(dv_ref)
    zero = jnp.zeros((), BF)
    for start, stop in row_blocks(length):
        own, before = masks(start, stop, length, count)
        dqs = []
        for head in range(2):
            mine = (lane >= 64) == (head == 1)
            q = jnp.where(mine, q_ref[start:stop, :], zero)
            do = jnp.where(mine, do_ref[start:stop, :], zero)
            lse = jnp.sum(
                jnp.where(lane == head0 + head, lse_ref[start:stop, :], 0.0), axis=-1, keepdims=True
            )
            p2 = jnp.where(own, jnp.exp(ALPHA * dot_nt(q, k_ref[start:stop, :]) - lse), 0.0)
            g2 = dot_nt(do, v_ref[start:stop, :])
            delta = jnp.sum(p2 * g2, axis=-1, keepdims=True)
            if start:
                p1 = jnp.exp(ALPHA * dot_nt(q, k_ref[0:start, :]) - lse)
                if before is not None:
                    p1 = jnp.where(before, p1, 0.0)
                g1 = dot_nt(do, v_ref[0:start, :])
                delta = delta + jnp.sum(p1 * g1, axis=-1, keepdims=True)
            ds2 = (ALPHA * p2 * (g2 - delta)).astype(BF)
            dq = dot_nn(ds2, k_ref[start:stop, :])
            dk_ref[start:stop, :] += dot_tn(ds2, q)
            dv_ref[start:stop, :] += dot_tn(p2.astype(BF), do)
            if start:
                ds1 = (ALPHA * p1 * (g1 - delta)).astype(BF)
                dq = dq + dot_nn(ds1, k_ref[0:start, :])
                dk_ref[0:start, :] += dot_tn(ds1, q)
                dv_ref[0:start, :] += dot_tn(p1.astype(BF), do)
            dqs.append(dq)
        q_ref[start:stop, :] = (jnp.where(lane < 64, dqs[0], dqs[1]) * SCALE).astype(BF)
    k_ref[...] = dk_ref[...].astype(BF)
    v_ref[...] = dv_ref[...].astype(BF)


FAR = (3, 4)


class Reduce:
    def __init__(self, links, part, slots, column, merge, slot_sems, column_sems, merge_sems, load):
        self.load, self.near, self.copies = load, [], []
        self.links, self.part, self.slots = links, part, slots
        self.column, self.merge = column, merge
        self.slot_sems, self.column_sems, self.merge_sems = slot_sems, column_sems, merge_sems
        self.groups = links.n_dp // 2
        self.rows = part.shape[1] // links.n_dp
        self.steps = [plan_hops(self.groups, i)[::-1] for i in range(2)]
        self.place = jnp.where(links.core == 0, links.z, links.n_mp - 1 - links.z)
        self.terms = links.n_mp if merge is None else links.n_mp - 1

    def piece(self, i, rel):
        return self.part.at[i, rows_at(self.links.group ^ rel, 2 * self.rows), :]

    def slot(self, i, rel):
        return self.slots.at[i, pl.ds((rel - 1) * 2 * self.rows, 2 * self.rows), :]

    def give(self, i, rel, bit):
        k = self.links
        k.send(
            lambda: self.piece(i, rel),
            lambda: self.slot(i, rel),
            self.slot_sems.at[i, rel],
            k.dp ^ (2 * bit),
            k.z,
        )

    def start(self, i):
        bit, known = self.steps[i][0]
        for rel in known[::-1]:
            self.give(i, rel ^ bit, bit)

    def add(self, i, rel, source):
        tile = min(32, 2 * self.rows)
        base = (self.links.group ^ rel) * 2 * self.rows

        def body(t, _):
            rows = pl.ds(pl.multiple_of(base + t * tile, tile), tile)
            came = source[pl.ds(pl.multiple_of(t * tile, tile), tile), :]
            total = self.part[i, rows, :].astype(F32) + came.astype(F32)
            self.part[i, rows, :] = total.astype(self.part.dtype)
            return 0

        lax.fori_loop(0, 2 * self.rows // tile, body, 0)

    def level(self, i, number):
        k = self.links
        bit, known = self.steps[i][number]
        after = self.steps[i][number + 1][0] if number + 1 < len(self.steps[i]) else 0
        for rel in sorted(known, key=lambda r: not r & after):
            k.arrived(self.piece(i, rel), self.slot(i, rel ^ bit), self.slot_sems.at[i, rel ^ bit])
            self.add(i, rel, self.slot(i, rel ^ bit))
            if rel & after:
                self.give(i, rel, after)
        if not after:
            if self.merge is None:
                self.ship(i, None)
            else:
                k.send(
                    lambda: self.piece(i, 0),
                    self.merge.at[i],
                    self.merge_sems.at[i],
                    k.dp,
                    k.z - 1 + 2 * k.core,
                    when=lambda: self.place == 3,
                )
                self.ship(i, lambda: self.place < 2)

    def ship(self, i, when):
        k = self.links
        slot = k.z if self.merge is None else jnp.where(self.place == 3, 0, k.z - k.core)
        for c in range(2):
            k.send(
                lambda c=c: self.part.at[i, rows_at(2 * k.group + c, self.rows), :],
                lambda slot=slot: self.column.at[slot],
                self.column_sems.at[slot],
                lambda c=c: 2 * k.group + c,
                lambda: 2 * k.core + i,
                when=when,
                may_stay=True,
            )

    def levels(self, number):
        for i in range(2):
            self.level(i, number)

    def merged(self):
        for i in range(2):

            @pl.when(self.place == 2)
            def _(i=i):
                self.links.arrived(self.merge.at[i], self.merge.at[i], self.merge_sems.at[i])
                self.add(i, 0, self.merge.at[i])

            self.ship(i, lambda: self.place == 2)

    def collect(self):
        if self.near:
            return
        for zz in range(self.terms):
            term = self.column.at[zz]
            self.links.arrived(term, term, self.column_sems.at[zz])
            if self.load:
                near = self.slots.at[0, pl.ds(zz * self.rows, self.rows), :]
                self.copies.append(self.load(term, near))
                term = near
            self.near.append(term)

    def total(self, out):
        self.collect()
        for copy in self.copies:
            copy.wait()
        tile = min(32, self.rows)

        def body(t, _):
            rows = pl.ds(pl.multiple_of(t * tile, tile), tile)
            value = self.near[0][rows, :].astype(F32)
            for ref in self.near[1:]:
                value = value + ref[rows, :].astype(F32)
            out[rows, :] = value
            return 0

        lax.fori_loop(0, self.rows // tile, body, 0)


def return_tokens(links, parts, dst, sems, quarters=(0, 1)):
    quarter = dst.shape[1]
    m = links.z // 2
    for s in quarters:
        links.send_or_keep(
            parts.at[pl.ds(s * quarter, quarter), :],
            dst.at[m],
            sems.at[m],
            2 * links.group + lax.rem(links.z, 2),
            2 * links.core + s,
        )


def return_tokens_wait(links, dst, sems):
    for m in range(2):
        links.arrived(dst.at[m], dst.at[m], sems.at[m])


def backward_kernel(n_dp, n_mp, *refs):
    (y_hbm, g_hbm, x_hbm, a_hbm, mid_hbm, f_hbm, h1_hbm, qkv_hbm, o_hbm, lse_hbm) = refs[0:10]
    (h2_hbm, act_hbm, slope_hbm, wq_hbm, wo_hbm, wu_hbm, wd_hbm, vec_ref, count_ref) = refs[10:19]
    (layer_out, back, q_out, o_out, u_out, d_out, v_out) = refs[19:26]
    fars = refs[26:28]
    refs = refs[:26] + refs[27:]
    parts = refs[27:32]
    slots = refs[32:37]
    columns = list(refs[37:42])
    merges = (None,) + tuple(refs[42:46])
    refs = refs[:42] + refs[46:]
    for a, far in zip(FAR, fars):
        columns[a] = far
    (pair, take, own, own2, g_buf) = refs[42:47]
    refs = refs[:47] + (None,) + refs[47:]
    (act, du, h, wd, wu, lse, dk, dv, vsum, vtake, vqkv, vup) = refs[48:60]
    (send_sems, slot_sems, column_sems, merge_sems, tok_sems, swap_sems, load_sems) = refs[60:67]
    links = Links(n_dp, n_mp, send_sems)
    half = g_buf.shape[0]
    length = 2 * half
    tile = half // 2
    width = g_buf.shape[1]
    other = links.dp + 1 - 2 * links.core
    mine0 = links.core * half
    other0 = (1 - links.core) * half
    cols3 = qkv_hbm.shape[2]
    cols = cols3 // 3
    loads = [0]
    parts = list(parts)
    give = h.at[pl.ds(0, half), :]
    parts[1] = du.at[:, pl.ds(0, width), pl.ds(cols, cols3)]
    if parts[2].dtype == BF:
        parts[2] = wu.at[:, pl.ds(half, cols), :]
    else:
        parts[2] = own2.at[:, pl.ds(0, cols), :]

    def load(src, dst):
        copy = pltpu.make_async_copy(src, dst, load_sems.at[loads[0]])
        loads[0] += 1
        copy.start()
        return copy

    def at(start, rows):
        return pl.ds(pl.multiple_of(start, 16), rows)

    def gain(k):
        return vec_ref[k : k + 1, :]

    f_load = load(f_hbm, own)
    g_load = load(g_hbm, g_buf)
    act_load = load(act_hbm, act)
    wd_load = load(wd_hbm, wd)
    slope_load = load(slope_hbm, du)
    h_load = load(h2_hbm, h)
    wu_load = load(wu_hbm, wu)
    lse_load = load(lse_hbm, lse)
    vsum[...] = jnp.zeros_like(vsum)
    vqkv[...] = jnp.zeros_like(vqkv)
    vup[...] = jnp.zeros_like(vup)
    links.barrier()
    ways = [
        Reduce(
            links,
            parts[a],
            slots[a],
            columns[a],
            merges[a],
            slot_sems.at[a],
            column_sems.at[a],
            merge_sems.at[a],
            load if a in FAR else None,
        )
        for a in range(5)
    ]
    v_way, q_way, o_way, u_way, d_way = ways
    return_tokens(links, y_hbm, layer_out, tok_sems.at[0])

    def norm_grad(value, k, grad):
        unit, inverse = stats(value)
        back, dgain, dshift = norm_back(unit, inverse, gain(k), grad)
        vsum[k : k + 1, :] += dgain[None]
        vsum[4 + k : 5 + k, :] += dshift[None]
        return back

    f_load.wait()
    g_load.wait()

    def last_norm(t, _):
        rows = at(t * tile, tile)
        back = norm_grad(own[rows, :], 3, g_buf[rows, :].astype(F32)).astype(BF)
        vsum[9:10, :] += jnp.sum(back.astype(F32), axis=0, keepdims=True)
        pair[at(mine0 + t * tile, tile), :] = back
        return 0

    lax.fori_loop(0, 2, last_norm, 0)
    ours = pair.at[at(mine0, half), :]
    theirs = pair.at[at(other0, half), :]
    df_send = links.send(ours, ours, swap_sems.at[0], other, links.z)
    act_load.wait()
    links.arrived(ours, theirs, swap_sems.at[0])

    def weight_grad(left, right, part, i):
        step = min(256, left.shape[1])

        def body(t, _):
            lanes = pl.ds(pl.multiple_of(t * step, 128), step)
            rows = pl.ds(pl.multiple_of(t * step, 16), step)
            part[i, rows, :] = dot_tn(left[:, lanes], right[...]).astype(part.dtype)
            return 0

        lax.fori_loop(0, left.shape[1] // step, body, 0)

    for i in range(2):
        weight_grad(act.at[i], pair, parts[4], i)
        d_way.start(i)
    qkv_load = load(qkv_hbm, act.at[:, :, 0:cols3])
    wd_load.wait()
    slope_load.wait()
    h_load.wait()
    for i in range(2):

        def slant(t, _, i=i):
            rows = at(t * tile, tile)
            value = (dot_nt(pair[rows, :], wd[i]) * du[i, rows, :].astype(F32)).astype(BF)
            du[i, rows, :] = value
            vup[i : i + 1, :] += jnp.sum(value.astype(F32), axis=0, keepdims=True)
            return 0

        lax.fori_loop(0, 4, slant, 0)
        weight_grad(h, du.at[i], parts[3], i)
    wq_load = load(wq_hbm, wd.at[:, :, 0:cols3])
    a_load = load(a_hbm.at[pl.ds(0, tile), :], own2.at[0])
    mid_load = load(mid_hbm.at[pl.ds(0, tile), :], own2.at[1])
    wu_load.wait()

    def up_tile(start):
        return dot_nt(du[0, at(start, tile), :], wu[0]) + dot_nt(du[1, at(start, tile), :], wu[1])

    def up_theirs(t, _):
        give[at(t * tile, tile), :] = up_tile(other0 + t * tile).astype(BF)
        return 0

    def up_ours(t, _):
        own[at(t * tile, tile), :] = up_tile(mine0 + t * tile)
        return 0

    lax.fori_loop(0, 2, up_theirs, 0)
    up_send = links.send(give, take, swap_sems.at[1], other, links.z)
    lax.fori_loop(0, 2, up_ours, 0)
    o_load = load(o_hbm, du.at[:, :, 0:cols])
    x_load = load(x_hbm, wu.at[0, pl.ds(0, half), :])
    wo_load = [load(wo_hbm.at[i], wu.at[1, pl.ds(i * cols, cols), :]) for i in range(2)]
    links.wait_sent(df_send)
    links.arrived(give, take, swap_sems.at[1])
    for t in range(2):
        a_load.wait()
        mid_load.wait()
        rows = pl.ds(t * tile, tile)
        grad = own[rows, :] + take[rows, :].astype(F32)
        grad = g_buf[rows, :].astype(F32) + norm_grad(own2[1], 2, grad)
        own[rows, :] = grad
        grad = norm_grad(own2[0], 1, grad).astype(BF)
        vsum[8:9, :] += jnp.sum(grad.astype(F32), axis=0, keepdims=True)
        pair[at(mine0 + t * tile, tile), :] = grad
        if t == 0:
            a_load = load(a_hbm.at[pl.ds(tile, tile), :], own2.at[0])
            mid_load = load(mid_hbm.at[pl.ds(tile, tile), :], own2.at[1])
    links.send(ours, ours, swap_sems.at[2], other, links.z)
    links.wait_sent(up_send)
    h_load = load(h1_hbm, h)
    d_way.levels(0)
    u_way.start(0)
    u_way.start(1)
    o_load.wait()
    qkv_load.wait()
    wo_load[0].wait()
    wo_load[1].wait()
    links.arrived(ours, theirs, swap_sems.at[2])

    def open_heads(t, _):
        rows = at(t * tile, tile)
        for i in range(2):
            value = dot_nt(pair[rows, :], wu[1, i * cols : (i + 1) * cols, :])
            act[i, rows, cols3 : cols3 + cols] = value.astype(BF)
        return 0

    lax.fori_loop(0, 4, open_heads, 0)
    for i in range(2):
        weight_grad(du.at[i, :, 0:cols], pair, parts[2], i)
    lse_load.wait()
    h_load.wait()
    wq_load.wait()
    count = count_ref[0:1, 0:1]
    pairs = cols // 128

    def attend(n, _):
        i = n // pairs
        lanes = lambda base: pl.ds(pl.multiple_of((base + lax.rem(n, pairs)) * 128, 128), 128)
        attend_pair_bwd(
            act.at[i, :, lanes(0)],
            act.at[i, :, lanes(pairs)],
            act.at[i, :, lanes(2 * pairs)],
            act.at[i, :, lanes(3 * pairs)],
            lse,
            2 * n,
            count,
            dk,
            dv,
        )

        @pl.when(n == 0)
        def _():
            d_way.levels(1)

        @pl.when(n == pairs - 1)
        def _():
            weight_grad(h, act.at[0, :, 0:cols3], parts[1], 0)
            d_way.merged()

        @pl.when(n == pairs)
        def _():
            u_way.levels(0)

        return 0

    lax.fori_loop(0, 2 * pairs, attend, 0)
    q_way.start(0)
    weight_grad(h, act.at[1, :, 0:cols3], parts[1], 1)
    q_way.start(1)
    o_way.start(0)
    o_way.start(1)

    def head_tile(start):
        rows = at(start, tile)
        total = None
        for i in range(2):
            value = act[i, rows, 0:cols3]
            vqkv[i : i + 1, :] += jnp.sum(value.astype(F32), axis=0, keepdims=True)
            term = dot_nt(value, wd[i, :, 0:cols3])
            total = term if total is None else total + term
        return total

    def head_theirs(t, _):
        give[at(t * tile, tile), :] = head_tile(other0 + t * tile).astype(BF)
        return 0

    lax.fori_loop(0, 2, head_theirs, 0)
    links.send(give, take, swap_sems.at[3], other, links.z)
    u_way.levels(1)
    x_load.wait()
    links.arrived(give, take, swap_sems.at[3])

    def first_norm(t, _):
        rows = at(t * tile, tile)
        grad = head_tile(mine0 + t * tile) + take[rows, :].astype(F32)
        grad = own[rows, :] + norm_grad(wu[0, rows, :].astype(F32), 0, grad)
        g_buf[rows, :] = grad.astype(BF)
        return 0

    for t in range(2):
        first_norm(t, 0)
        return_tokens(links, g_buf, back, tok_sems.at[1], (t,))
    links.send(vsum, vtake, swap_sems.at[4], other, links.z)
    q_way.level(0, 0)
    links.arrived(vsum, vtake, swap_sems.at[4])
    gather_smalls(n_dp, vsum[...] + vtake[...], vqkv, vup, parts[0])
    v_way.start(0)
    v_way.start(1)
    u_way.merged()
    d_way.collect()
    q_way.level(1, 0)
    o_way.levels(0)
    v_way.levels(0)
    d_way.total(d_out)
    v_way.levels(1)
    q_way.levels(1)
    o_way.levels(1)
    u_way.collect()
    u_way.total(u_out)
    q_way.merged()
    o_way.merged()
    o_way.total(o_out)
    return_tokens_wait(links, back, tok_sems.at[1])
    v_way.total(v_out)
    q_way.total(q_out)
    return_tokens_wait(links, layer_out, tok_sems.at[0])
    links.finish()


def gather_smalls(n_dp, total, vqkv, vup, part):
    width = total.shape[1]
    slim = width // n_dp
    per_qv = vqkv.shape[1] // 3 // n_dp
    per_up = vup.shape[1] // n_dp
    lanes = part.shape[2]
    values = 2 * per_qv * n_dp

    def fill(value):
        short = lanes - value.shape[1]
        if not short:
            return value
        return jnp.concatenate([value, jnp.zeros((value.shape[0], short), F32)], axis=1)

    for i in range(2):
        qkv = vqkv[i : i + 1, :]
        up = vup[i : i + 1, :]
        for dp in range(n_dp):
            first = jnp.concatenate(
                [
                    qkv[:, dp * per_qv : (dp + 1) * per_qv],
                    qkv[:, values + dp * per_qv : values + (dp + 1) * per_qv],
                ],
                axis=1,
            )
            base = 16 * dp
            part[i, base : base + 1, :] = fill(first)
            part[i, base + 1 : base + 2, :] = fill(up[:, dp * per_up : (dp + 1) * per_up])
            part[i, base + 2 : base + 12, :] = fill(total[0:10, dp * slim : (dp + 1) * slim])
            part[i, base + 12 : base + 16, :] = jnp.zeros((4, lanes), F32)


def backward_all(n_dp, n_mp, saved, weights, vec, count):
    groups = n_dp // 2
    any_spec = pl.BlockSpec(memory_space=pl.ANY)
    vmem = pl.BlockSpec(memory_space=pltpu.VMEM)
    shape = jax.ShapeDtypeStruct
    half, width = saved[0].shape
    length = 2 * half
    cols3 = saved[7].shape[2]
    cols = cols3 // 3
    ff = saved[11].shape[2]
    full = [(2, n_dp * 16, 128)] + [w.shape for w in weights]
    each = [f[1] // n_dp for f in full]
    kinds = [F32] + [BF if r % 8 == 0 else F32 for r in each[1:]]
    out_shape = [shape((2, half // 2, width), BF)] * 2 + [
        shape((each[a], full[a][2]), F32) for a in (1, 2, 3, 4, 0)
    ]
    out_shape += [shape((n_mp, each[a], full[a][2]), kinds[a]) for a in FAR]
    sends = 4 + 5 + 5 * (2 * (groups - 1) + 10)
    return pl.pallas_call(
        functools.partial(backward_kernel, n_dp, n_mp),
        in_specs=[any_spec] * 17 + [vmem] * 2,
        out_specs=[any_spec] * 2 + [vmem] * 5 + [any_spec] * len(FAR),
        out_shape=out_shape,
        scratch_shapes=[
            pltpu.VMEM((1, 16, 128) if a in (1, 2) else f, k)
            for a, (f, k) in enumerate(zip(full, kinds))
        ]
        + [
            pltpu.VMEM((2, (groups - 1) * 2 * r, f[2]), k) for f, r, k in zip(full, each, kinds)
        ]
        + [
            pltpu.VMEM((n_mp, 16 if a in FAR else r, f[2]), k)
            for a, (f, r, k) in enumerate(zip(full, each, kinds))
        ]
        + [
            pltpu.VMEM((2, 2 * r, f[2]), k) for f, r, k in zip(full[1:], each[1:], kinds[1:])
        ]
        + [
            pltpu.VMEM((length, width), BF),
            pltpu.VMEM((half, width), BF),
            pltpu.VMEM((half, width), F32),
            pltpu.VMEM((2, half // 2, width), F32),
            pltpu.VMEM((half, width), BF),
            pltpu.VMEM((2, length, ff), BF),
            pltpu.VMEM((2, length, ff), BF),
            pltpu.VMEM((length, width), BF),
            pltpu.VMEM((2, ff, width), BF),
            pltpu.VMEM((2, width, ff), BF),
            pltpu.VMEM((length, 128), F32),
            pltpu.VMEM((length, 128), F32),
            pltpu.VMEM((length, 128), F32),
            pltpu.VMEM((16, width), F32),
            pltpu.VMEM((16, width), F32),
            pltpu.VMEM((2, cols3), F32),
            pltpu.VMEM((2, ff), F32),
            pltpu.SemaphoreType.DMA((sends,)),
            pltpu.SemaphoreType.DMA((5, 2, groups)),
            pltpu.SemaphoreType.DMA((5, n_mp)),
            pltpu.SemaphoreType.DMA((5, 2)),
            pltpu.SemaphoreType.DMA((2, 2)),
            pltpu.SemaphoreType.DMA((5,)),
            pltpu.SemaphoreType.DMA((19 + len(FAR) * n_mp,)),
        ],
        compiler_params=pltpu.CompilerParams(
            collective_id=1, has_side_effects=True, vmem_limit_bytes=61 << 20
        ),
    )(*saved, *weights, vec, count)[:7]


def finish_kernel(*refs):
    far = refs[0:7]
    (layer_out, grad_out, q_out, qv_out, o_out, u_out, up_out, d_out) = refs[7:15]
    gain_out, shift_out, bias_out = refs[15:18]
    near, sems = refs[18:25], refs[25]
    copies = [
        pltpu.make_async_copy(a, b, sems.at[n]) for n, (a, b) in enumerate(zip(far, near))
    ]
    for copy in copies:
        copy.start()
    for copy in copies:
        copy.wait()
    layer, back, q, o, u, d, v = near
    layer_out[...] = layer[...]
    grad_out[...] = back[...].astype(F32)
    cols = q.shape[1] // 3
    for j in range(3):
        q_out[j] = q[:, j * cols : (j + 1) * cols]
    per = qv_out.shape[1]
    qv_out[0:1, :] = v[0:1, 0:per]
    qv_out[1:2, :] = v[0:1, per : 2 * per]
    o_out[...] = o[...]
    u_out[...] = u[...]
    up_out[...] = v[1:2, 0 : up_out.shape[1]]
    d_out[...] = d[...]
    slim = gain_out.shape[1]
    gain_out[...] = v[2:6, 0:slim]
    shift_out[...] = v[6:10, 0:slim]
    bias_out[...] = v[10:12, 0:slim]


def finish_all(arrays, per_qv, per_up, slim):
    layer, back, q, o, u, d, v = arrays
    far = pl.BlockSpec(memory_space=pl.ANY)
    vmem = pl.BlockSpec(memory_space=pltpu.VMEM)
    shape = jax.ShapeDtypeStruct
    return pl.pallas_call(
        finish_kernel,
        in_specs=[far] * 7,
        out_specs=[vmem] * 11,
        out_shape=[
            shape(layer.shape, BF),
            shape(back.shape, F32),
            shape((3, q.shape[0], q.shape[1] // 3), F32),
            shape((2, per_qv), F32),
            shape(o.shape, F32),
            shape(u.shape, F32),
            shape((1, per_up), F32),
            shape(d.shape, F32),
            shape((4, slim), F32),
            shape((4, slim), F32),
            shape((2, slim), F32),
        ],
        scratch_shapes=[pltpu.VMEM(a.shape, a.dtype) for a in arrays]
        + [pltpu.SemaphoreType.DMA((7,))],
        compiler_params=pltpu.CompilerParams(vmem_limit_bytes=60 << 20),
    )(*arrays)


def build(n_dp, n_mp):
    def on_device(
        tokens,
        seg_ids,
        qkv_weight,
        qv_bias,
        out_weight,
        up_weight,
        up_bias,
        down_weight,
        norm_gain,
        norm_bias,
        branch_bias,
        out_grad,
    ):
        (
            x,
            grad_y,
            h1,
            qkvs,
            attended,
            log_sums,
            branch,
            middle,
            h2,
            acts,
            slopes,
            ffn_out,
            out_rows,
            w_qkv,
            w_out,
            w_up,
            w_down,
            count,
            vec,
        ) = forward_all(
            n_dp,
            n_mp,
            tokens,
            out_grad,
            seg_ids,
            [qv_bias, up_bias.reshape(1, -1), norm_gain, norm_bias, branch_bias],
            qkv_weight,
            [out_weight, up_weight, down_weight],
        )
        saved = [
            out_rows,
            grad_y,
            x,
            branch,
            middle,
            ffn_out,
            h1,
            qkvs,
            attended,
            log_sums,
            h2,
            acts,
            slopes,
        ]
        sums = backward_all(n_dp, n_mp, saved, [w_qkv, w_out, w_up, w_down], vec, count)
        outs = list(finish_all(sums, qv_bias.shape[1], up_bias.shape[0], norm_gain.shape[1]))
        outs[6] = outs[6].reshape(-1)
        return tuple(outs)

    return on_device


def solution(mesh):
    n_dp, n_mp = mesh.shape["dp"], mesh.shape["mp"]
    in_specs = (
        P(None, ("dp", "mp"), None),
        P(None, "dp"),
        P(None, "dp", "mp"),
        P(None, ("mp", "dp")),
        P(("mp", "dp"), None),
        P("dp", "mp"),
        P(("mp", "dp")),
        P(("mp", "dp"), None),
        P(None, "dp"),
        P(None, "dp"),
        P(None, "dp"),
        P(None, ("dp", "mp"), None),
    )
    out_specs = (
        P(None, ("dp", "mp"), None),
        P(None, ("dp", "mp"), None),
        P(None, "dp", "mp"),
        P(None, ("mp", "dp")),
        P(("mp", "dp"), None),
        P("dp", "mp"),
        P(("mp", "dp")),
        P(("mp", "dp"), None),
        P(None, "dp"),
        P(None, "dp"),
        P(None, "dp"),
    )
    return jax.shard_map(
        build(n_dp, n_mp), mesh=mesh, in_specs=in_specs, out_specs=out_specs, check_vma=False
    )
```
